256 devices in a mesh: pairs: 128 (over y, x, z), side: 2 (over core).
Axes of the slice: x: 4, y: 4, z: 8, core: 2. Of those that a mesh axis runs over, the one named last changes fastest.
Arguments:
- features: bfloat16 [128, 196, 768], P('pairs', None, 'side'), may hold values from -6 to 6
- image_slot: int32 [128], replicated, may hold values from 0 to 127, as said below
- slot_images: int32 [384, 2], P('pairs'), may hold values from 0 to 127, as said below
- slot_count: int32 [128], P('pairs'), may hold values from 1 to 3, as said below
- gain_self: float32 [2, 768], P('side'), may hold values from 0.5 to 1.5
- gain_query: float32 [2, 768], P('side'), may hold values from 0.5 to 1.5
- gain_memory: float32 [2, 768], P('side'), may hold values from 0.5 to 1.5
- gain_mlp: float32 [2, 768], P('side'), may hold values from 0.5 to 1.5
- gain_head: float32 [2, 768], P('side'), may hold values from 0.5 to 1.5
- w_qkv: bfloat16 [2, 768, 2304], P('side'), may hold values from -0.21875 to 0.21875
- w_self_out: bfloat16 [2, 768, 768], P('side'), may hold values from -0.21875 to 0.21875
- w_query: bfloat16 [2, 768, 768], P('side'), may hold values from -0.21875 to 0.21875
- w_memory: bfloat16 [2, 768, 1536], P('side'), may hold values from -0.21875 to 0.21875
- w_cross_out: bfloat16 [2, 768, 768], P('side'), may hold values from -0.21875 to 0.21875
- w_fc1: bfloat16 [2, 3072, 768], P('side', 'pairs'), may hold values from -0.21875 to 0.21875
- w_fc2: bfloat16 [2, 3072, 768], P('side', 'pairs'), may hold values from -0.109375 to 0.109375
- w_head: bfloat16 [2, 768, 1024], P('side'), may hold values from -0.21875 to 0.21875
Outputs:
- merged_points: bfloat16 [128, 196, 768], P('pairs', None, 'side')
The draws below stay inside these ranges and needn't reach their ends.
Inputs may be any that keep to these rules, and one draw needn't show every extreme that they name: A permutation: image i is storage row image_slot[i] of features, held by device image_slot[i] // 1 of pairs. `slot_images`: slot j belongs to device j // 3 of pairs; its two images are distinct, and each is held by device (j // 3 + k) mod the size of pairs for some 0 <= k < 4; k = 3 occurs. `slot_count`: the counts sum to 256; 3 is reached on a quarter of the devices.
All inputs are finite; a program needn't handle non-finite values.
Results may differ from the reference program's by a relative error of at most 0.015.
Values may be sent and summed in bfloat16 or wider, within the bound.
No kernel may reach another device: no remote copies, remote signals or barrier semaphores. Data moves between devices by JAX's collectives and lax.ppermute only.
A program may use at most 128 MiB of HBM per device.

```python
import jax
import jax.numpy as jnp
from jax import lax

D = 768
HEADS = 12
FF = 3072
HEAD_DIM = 64
TOKI = 196
PIXELS = 256
WINDOW = 4
IMG_DEV = 1
PAIR_DEV = 2
PAIR_MAX = 3
IMAGES = 128
SLOTS = 384


def routing_tables(key):
    n_dev = IMAGES // IMG_DEV
    keys = jax.random.split(jax.random.fold_in(key, 31), 4)
    image_slot = jax.random.permutation(keys[0], IMAGES).astype(jnp.int32)
    row_image = jnp.zeros((IMAGES,), jnp.int32).at[image_slot].set(jnp.arange(IMAGES, dtype=jnp.int32))
    order = jax.random.permutation(keys[1], n_dev).astype(jnp.int32)
    ranking = jnp.zeros((n_dev,), jnp.int32).at[order].set(jnp.arange(n_dev, dtype=jnp.int32))
    quarter = n_dev // 4
    halfway = PAIR_DEV // 2
    counts = PAIR_DEV + jnp.where(ranking < quarter, halfway, 0) - jnp.where((ranking >= quarter) & (ranking < 2 * quarter), halfway, 0)
    offsets = jax.random.randint(keys[2], (SLOTS, 2), 0, WINDOW).astype(jnp.int32)
    offsets = offsets.at[0, 0].set(WINDOW - 1)
    within = jax.random.randint(keys[3], (SLOTS, 2), 0, IMG_DEV).astype(jnp.int32)
    clash = (offsets[:, 0] == offsets[:, 1]) & (within[:, 0] == within[:, 1])
    second = jnp.where(clash, (offsets[:, 1] + 1) % WINDOW, offsets[:, 1])
    offsets = jnp.stack([offsets[:, 0], second], axis=1)
    device = (jnp.arange(SLOTS, dtype=jnp.int32) // PAIR_MAX)[:, None]
    holder = (device + offsets) % n_dev
    slot_images = row_image[holder * IMG_DEV + within]
    return (image_slot, slot_images.astype(jnp.int32), counts.astype(jnp.int32))


def draw_image_slot(key, part):
    return routing_tables(key)[0]


def draw_slot_images(key, part):
    return routing_tables(key)[1]


def draw_slot_count(key, part):
    return routing_tables(key)[2]


def shard_levels(stream_key, dims, pieces, least, top_value):
    loudness = 1.0
    for dim, blocks in pieces:
        draws = jax.random.uniform(jax.random.fold_in(jax.random.fold_in(stream_key, 6), dim), (blocks,), jnp.float32, least / len(pieces), top_value / len(pieces))
        loudness = loudness * jnp.repeat(jnp.exp(draws), dims[dim] // blocks).reshape((-1,) + (1,) * (len(dims) - 1 - dim))
    return loudness


def bell_draw(rng, extent, width, limit, cuts=(), kind=jnp.bfloat16):
    entries = width * jax.random.normal(rng, extent, jnp.float32)
    if cuts:
        entries = entries * shard_levels(rng, extent, cuts, -0.22, 0.18)
    return jnp.clip(entries, -limit, limit).astype(kind)


def setup_inputs(seed: int = 0) -> dict:
    key_list = jax.random.split(jax.random.key(seed), 18)
    features = bell_draw(key_list[0], (IMAGES, TOKI, D), 1.0, 6.0, ((0, 128), (2, 2)))
    image_slot = draw_image_slot(jax.random.fold_in(key_list[17], 71), 0)
    slot_images = draw_slot_images(jax.random.fold_in(key_list[17], 71), 0)
    slot_count = draw_slot_count(jax.random.fold_in(key_list[17], 71), 0)
    gain_self = jnp.clip(1.0 + 0.1 * jax.random.normal(key_list[4], (2, D), jnp.float32), 0.5, 1.5)
    gain_query = jnp.clip(1.0 + 0.1 * jax.random.normal(key_list[5], (2, D), jnp.float32), 0.5, 1.5)
    gain_memory = jnp.clip(1.0 + 0.1 * jax.random.normal(key_list[6], (2, D), jnp.float32), 0.5, 1.5)
    gain_mlp = jnp.clip(1.0 + 0.1 * jax.random.normal(key_list[7], (2, D), jnp.float32), 0.5, 1.5)
    gain_head = jnp.clip(1.0 + 0.1 * jax.random.normal(key_list[8], (2, D), jnp.float32), 0.5, 1.5)
    w_qkv = bell_draw(key_list[9], (2, D, 3 * D), D ** -0.5, 0.21875, ((0, 2),))
    w_self_out = bell_draw(key_list[10], (2, D, D), D ** -0.5, 0.21875, ((0, 2),))
    w_query = bell_draw(key_list[11], (2, D, D), D ** -0.5, 0.21875, ((0, 2),))
    w_memory = bell_draw(key_list[12], (2, D, 2 * D), D ** -0.5, 0.21875, ((0, 2),))
    w_cross_out = bell_draw(key_list[13], (2, D, D), D ** -0.5, 0.21875, ((0, 2),))
    w_fc1 = bell_draw(key_list[14], (2, FF, D), D ** -0.5, 0.21875, ((0, 2), (1, 128)))
    w_fc2 = bell_draw(key_list[15], (2, FF, D), FF ** -0.5, 0.109375, ((0, 2), (1, 128)))
    w_head = bell_draw(key_list[16], (2, D, 4 * PIXELS), D ** -0.5, 0.21875, ((0, 2),))
    return dict(features=features, image_slot=image_slot, slot_images=slot_images, slot_count=slot_count, gain_self=gain_self, gain_query=gain_query, gain_memory=gain_memory, gain_mlp=gain_mlp, gain_head=gain_head, w_qkv=w_qkv, w_self_out=w_self_out, w_query=w_query, w_memory=w_memory, w_cross_out=w_cross_out, w_fc1=w_fc1, w_fc2=w_fc2, w_head=w_head)


def layer_norm(values, gain):
    center = values - lax.optimization_barrier(jnp.mean(values, axis=-1, keepdims=True))
    spread = lax.optimization_barrier(jnp.mean(center * center, axis=-1, keepdims=True))
    return center * lax.rsqrt(spread + 1e-06) * gain

def attend(queries, key_rows, value_rows):
    length = queries.shape[0]
    key_len = key_rows.shape[0]
    q_heads = queries.astype(jnp.float32).reshape(length, HEADS, HEAD_DIM)
    k_heads = key_rows.astype(jnp.float32).reshape(key_len, HEADS, HEAD_DIM)
    v_heads = value_rows.astype(jnp.float32).reshape(key_len, HEADS, HEAD_DIM)
    scores = jnp.einsum('qhd,khd->hqk', q_heads, k_heads) * HEAD_DIM ** (-0.5)
    expon = jnp.exp(scores)
    weights = (expon / lax.optimization_barrier(jnp.sum(expon, axis=-1, keepdims=True))).astype(jnp.bfloat16)
    mixed = jnp.einsum('hqk,khd->qhd', weights.astype(jnp.float32), v_heads)
    return mixed.astype(jnp.bfloat16).reshape(length, D)

def decode(tokens, memory, gains, mats):
    g_self, g_query, g_memory, g_mlp, g_head = gains
    m_qkv, m_self_out, m_query, m_memory, m_cross_out, m_fc_in, m_fc_out, m_head = mats
    hidden = layer_norm(tokens.astype(jnp.float32), g_self).astype(jnp.bfloat16)
    triple = jnp.dot(hidden, m_qkv, preferred_element_type=jnp.float32).astype(jnp.bfloat16)
    attended = attend(triple[:, :D], triple[:, D:2 * D], triple[:, 2 * D:])
    first = tokens.astype(jnp.float32) + jnp.dot(attended, m_self_out, preferred_element_type=jnp.float32)
    query_in = layer_norm(first, g_query).astype(jnp.bfloat16)
    memory_in = layer_norm(memory.astype(jnp.float32), g_memory).astype(jnp.bfloat16)
    queries = jnp.dot(query_in, m_query, preferred_element_type=jnp.float32).astype(jnp.bfloat16)
    key_value = jnp.dot(memory_in, m_memory, preferred_element_type=jnp.float32).astype(jnp.bfloat16)
    crossed = attend(queries, key_value[:, :D], key_value[:, D:])
    second = first + jnp.dot(crossed, m_cross_out, preferred_element_type=jnp.float32)
    mlp_in = layer_norm(second, g_mlp).astype(jnp.bfloat16)
    pre_act = jnp.dot(mlp_in, m_fc_in.T, preferred_element_type=jnp.float32)
    activated = jax.nn.gelu(pre_act, approximate=False).astype(jnp.bfloat16)
    third = second + jnp.dot(activated, m_fc_out, preferred_element_type=jnp.float32)
    final = layer_norm(third, g_head).astype(jnp.bfloat16)
    return jnp.dot(final, m_head, preferred_element_type=jnp.float32)

def map_terms(raw):
    lead = raw.shape[:-1]
    parts = raw.reshape(lead + (2, 4, PIXELS // 2))
    conf = 1.0 + jnp.exp(parts[..., 3, :])
    joined = jnp.concatenate([conf[..., None, :] * parts[..., :3, :], conf[..., None, :]], axis=-2)
    return joined.reshape(lead + (4 * PIXELS,))

def reference(features, image_slot, slot_images, slot_count, gain_self, gain_query, gain_memory, gain_mlp, gain_head, w_qkv, w_self_out, w_query, w_memory, w_cross_out, w_fc1, w_fc2, w_head):
    gain_list = [gain_self, gain_query, gain_memory, gain_mlp, gain_head]
    mat_list = [w_qkv, w_self_out, w_query, w_memory, w_cross_out, w_fc1, w_fc2, w_head]

    def one_slot(sums, index):
        live = (index % PAIR_MAX < slot_count[index // PAIR_MAX]).astype(jnp.float32)
        stored = image_slot[slot_images[index]].astype(jnp.int32)
        views = [lax.dynamic_index_in_dim(features, stored[which], 0, keepdims=False) for which in range(2)]
        for which in range(2):
            result = decode(views[which], views[1 - which], [g[which] for g in gain_list], [m[which] for m in mat_list])
            sums = sums.at[stored[which]].add(live * map_terms(result))
        return (sums, None)
    start = jnp.zeros((IMAGES, TOKI, 4 * PIXELS), jnp.float32)
    sums, _ = lax.scan(one_slot, start, jnp.arange(SLOTS, dtype=jnp.int32))
    parts = sums.reshape(IMAGES, TOKI, 2, 4, PIXELS // 2)
    merged = parts[:, :, :, :3] / jnp.maximum(parts[:, :, :, 3:], 1.0)
    return merged.reshape(IMAGES, TOKI, 3 * PIXELS).astype(jnp.bfloat16)
```

```python
import jax
import jax.numpy as jnp
from jax import lax
from jax.experimental import pallas as pl
from jax.experimental.pallas import tpu as pltpu
from jax.sharding import PartitionSpec as P

D = 768
HEAD_DIM = 64
TOKI = 196
ROWS = 208
HALF = 384
WINDOW = 4
SLOTS = 3
ALL = SLOTS * ROWS
FF = 3072
CHUNK = 512
F32 = jnp.float32
BF16 = jnp.bfloat16


def shifted(array, by):
    count = lax.axis_size("pairs")
    return lax.ppermute(array, "pairs", [(i, (i + by) % count) for i in range(count)])


def other_core(array):
    return lax.ppermute(array, "side", [(0, 1), (1, 0)])


def layer_norm(values, gain):
    center = values - jnp.mean(values, axis=-1, keepdims=True)
    spread = jnp.mean(center * center, axis=-1, keepdims=True)
    return center * lax.rsqrt(spread + 1e-06) * gain


def window_place(image_slot, slot_images, place, slot, which):
    stored = image_slot[slot_images[2 * slot + which]]
    return lax.rem(stored - place[0] + 128, 128)


def load_tokens(image_slot, slot_images, place, mine, theirs, swap, slot):
    which = place[1] if not swap else 1 - place[1]
    index = window_place(image_slot, slot_images, place, slot, which)
    first = place[1] == 0
    low = mine[index].astype(F32)
    high = theirs[index].astype(F32)
    return jnp.where(first, low, high), jnp.where(first, high, low)


def padded_rows(image_slot, slot_images, place, mine, theirs, swap, target):
    for slot in range(SLOTS):
        low, high = load_tokens(image_slot, slot_images, place, mine, theirs, swap, slot)
        base = slot * ROWS
        target[base + 192 : base + ROWS, :] = jnp.zeros((ROWS - 192, D), F32)
        target[base : base + TOKI, :HALF] = low
        target[base : base + TOKI, HALF:] = high


def norm_into(source, gain, target):
    for slot in range(SLOTS):
        rows = slice(slot * ROWS, (slot + 1) * ROWS)
        target[rows, :] = layer_norm(source[rows, :], gain[...]).astype(BF16)


def attention(q_ref, q_base, k_ref, k_base, v_ref, v_base, out_ref):
    lane = lax.broadcasted_iota(jnp.int32, (ROWS, 128), 1)
    low_lanes = lane < HEAD_DIM
    key_ok = lax.broadcasted_iota(jnp.int32, (ROWS, ROWS), 1) < TOKI

    def step(t, carry):
        slot = t // 3
        group = t - 3 * slot
        rows = pl.ds(pl.multiple_of(slot * ROWS, ROWS), ROWS)
        for pair in range(2):
            col = group * 256 + pair * 128
            q = q_ref[rows, pl.ds(pl.multiple_of(q_base + col, 128), 128)]
            k = k_ref[rows, pl.ds(pl.multiple_of(k_base + col, 128), 128)]
            v = v_ref[rows, pl.ds(pl.multiple_of(v_base + col, 128), 128)]
            outs = []
            for head in range(2):
                own = low_lanes if head == 0 else jnp.logical_not(low_lanes)
                scores = lax.dot_general(
                    jnp.where(own, q, jnp.zeros_like(q)),
                    k,
                    (((1,), (1,)), ((), ())),
                    preferred_element_type=F32,
                )
                expon = jnp.where(key_ok, jnp.exp(scores), 0.0)
                total = jnp.sum(expon, axis=-1, keepdims=True)
                weights = (expon * (1.0 / total)).astype(BF16)
                outs.append(jnp.dot(weights, v, preferred_element_type=F32))
            out_ref[rows, pl.ds(pl.multiple_of(col, 128), 128)] = jnp.where(
                low_lanes, outs[0], outs[1]
            ).astype(BF16)
        return carry

    lax.fori_loop(0, 3 * SLOTS, step, 0)


def project(source, weight, width, write):
    def step(n, carry):
        cols = pl.ds(pl.multiple_of(n * 256, 256), 256)
        write(n, cols, jnp.dot(source[...], weight[:, cols], preferred_element_type=F32))
        return carry

    lax.fori_loop(0, width // 256, step, 0)


def self_kernel(
    image_slot, slot_images, place, mine, theirs, g_self, g_query, w_qkv, w_out, w_query,
    first_ref, query_ref, hidden, triple, mixed,
):
    padded_rows(image_slot, slot_images, place, mine, theirs, False, first_ref)
    norm_into(first_ref, g_self, hidden)

    def write_triple(n, cols, value):
        triple[:, cols] = (value * jnp.where(n < 3, 0.125, 1.0)).astype(BF16)

    project(hidden, w_qkv, 3 * D, write_triple)
    attention(triple, 0, triple, D, triple, 2 * D, mixed)

    def add_first(n, cols, value):
        first_ref[:, cols] = first_ref[:, cols] + value

    project(mixed, w_out, D, add_first)
    norm_into(first_ref, g_query, hidden)

    def write_query(n, cols, value):
        query_ref[:, cols] = (value * 0.125).astype(BF16)

    project(hidden, w_query, D, write_query)


def cross_kernel(
    image_slot, slot_images, place, mine, theirs, first, query, g_memory, g_mlp, w_memory, w_out,
    second_ref, mlp_ref, rows_ref, hidden, key_value, mixed,
):
    padded_rows(image_slot, slot_images, place, mine, theirs, True, rows_ref)
    norm_into(rows_ref, g_memory, hidden)

    def write_kv(n, cols, value):
        key_value[:, cols] = value.astype(BF16)

    project(hidden, w_memory, 2 * D, write_kv)
    attention(query, 0, key_value, 0, key_value, D, mixed)

    def add_second(n, cols, value):
        second_ref[:, cols] = first[:, cols] + value

    project(mixed, w_out, D, add_second)
    norm_into(second_ref, g_mlp, mlp_ref)


def gelu(value):
    return value * (1.0 + lax.erf(value * 0.7071067811865476)) * 0.5


def mlp_kernel(
    place, second, mlp_in, fc, g_head, w_head, keep_ref, send_ref, pre, total, hidden,
):
    steps = FF // CHUNK

    def before(c):
        rows = pl.ds(pl.multiple_of(c * CHUNK, CHUNK), CHUNK)
        return lax.dot_general(
            mlp_in[...], fc[0, rows, :], (((1,), (1,)), ((), ())), preferred_element_type=F32
        )

    pre[0] = before(0)
    total[...] = second[...]

    def step(c, carry):
        now = lax.rem(c, 2)
        active = gelu(pre[now]).astype(BF16)
        pre[1 - now] = before(jnp.minimum(c + 1, steps - 1))
        rows = pl.ds(pl.multiple_of(c * CHUNK, CHUNK), CHUNK)
        total[...] = total[...] + jnp.dot(active, fc[1, rows, :], preferred_element_type=F32)
        return carry

    lax.fori_loop(0, steps, step, 0)
    norm_into(total, g_head, hidden)
    first = place[1] == 0
    for slot in range(SLOTS):
        rows = slice(slot * ROWS, (slot + 1) * ROWS)
        terms = []
        for half in range(2):
            raw = jnp.dot(
                hidden[rows, :], w_head[:, half * 512 : (half + 1) * 512],
                preferred_element_type=F32,
            )
            conf = 1.0 + jnp.exp(raw[:, 384:])
            terms.append([conf * raw[:, c * 128 : (c + 1) * 128] for c in range(3)] + [conf])
        for c in range(4):
            cols = slice(c * 128, (c + 1) * 128)
            low, high = terms[0][c][:TOKI], terms[1][c][:TOKI]
            keep_ref[slot, :, cols] = jnp.where(first, low, high)
            send_ref[slot, :, cols] = jnp.where(first, high, low).astype(BF16)


def window_kernel(
    image_slot, slot_images, slot_count, place, keep, got, out0, out1, out2, out3
):
    outs = [out0, out1, out2, out3]
    chosen = []
    for slot in range(SLOTS):
        live = slot < slot_count[0]
        for which in range(2):
            index = window_place(image_slot, slot_images, place, slot, which)
            chosen.append((slot, which, jnp.where(live, index, -1)))
    for w in range(WINDOW):
        for c in range(4):
            cols = slice(c * 128, (c + 1) * 128)
            acc = jnp.zeros((TOKI, 128), F32)
            for slot in range(SLOTS):
                own = jnp.where(place[1] == 0, chosen[2 * slot][2], chosen[2 * slot + 1][2])
                far = jnp.where(place[1] == 0, chosen[2 * slot + 1][2], chosen[2 * slot][2])
                acc = acc + jnp.where(own == w, keep[slot, :, cols], 0.0)
                acc = acc + jnp.where(far == w, got[slot, :, cols].astype(F32), 0.0)
            outs[w][:, cols] = acc.astype(outs[w].dtype)


def merge_kernel(base, passed, out):
    weight = jnp.maximum(base[:, 384:] + passed[:, 384:].astype(F32), 1.0)
    for c in range(3):
        cols = slice(c * 128, (c + 1) * 128)
        out[0, :, cols] = ((base[:, cols] + passed[:, cols].astype(F32)) / weight).astype(BF16)


SMEM = pl.BlockSpec(memory_space=pltpu.SMEM)
VMEM = pl.BlockSpec(memory_space=pltpu.VMEM)


def call(kernel, scalars, arrays, outs, scratch, flops, name):
    return pl.pallas_call(
        kernel,
        in_specs=[SMEM] * len(scalars) + [VMEM] * len(arrays),
        out_specs=[VMEM] * len(outs),
        out_shape=[jax.ShapeDtypeStruct(s, d) for s, d in outs],
        scratch_shapes=[pltpu.VMEM(s, d) for s, d in scratch],
        compiler_params=pltpu.CompilerParams(vmem_limit_bytes=48 << 20),
        cost_estimate=pl.CostEstimate(flops=flops, transcendentals=0, bytes_accessed=8 << 20),
        name=name,
    )(*scalars, *arrays)


def self_call(scalars, mine, theirs, g_self, g_query, w_qkv, w_out, w_query):
    return call(
        self_kernel, scalars, [mine, theirs, g_self, g_query, w_qkv, w_out, w_query],
        [((ALL, D), F32), ((ALL, D), BF16)],
        [((ALL, D), BF16), ((ALL, 3 * D), BF16), ((ALL, D), BF16)],
        6 * 10**9, "self_part",
    )


def cross_call(scalars, mine, theirs, first, query, g_memory, g_mlp, w_memory, w_out):
    return call(
        cross_kernel, scalars, [mine, theirs, first, query, g_memory, g_mlp, w_memory, w_out],
        [((ALL, D), F32), ((ALL, D), BF16)],
        [((ALL, D), F32), ((ALL, D), BF16), ((ALL, 2 * D), BF16), ((ALL, D), BF16)],
        5 * 10**9, "cross_part",
    )


def mlp_call(place, second, mlp_in, fc, g_head, w_head):
    return call(
        mlp_kernel, [place], [second, mlp_in, fc, g_head, w_head],
        [((SLOTS, TOKI, 512), F32), ((SLOTS, TOKI, 512), BF16)],
        [((2, ALL, CHUNK), F32), ((ALL, D), F32), ((ALL, D), BF16)],
        7 * 10**9, "mlp_part",
    )


def window_call(scalars, keep, got):
    return call(
        window_kernel, scalars, [keep, got],
        [((TOKI, 512), F32)] + [((TOKI, 512), BF16)] * 3, [], 10**8, "window_part",
    )


def merge_call(base, passed):
    return call(merge_kernel, [], [base, passed], [((1, TOKI, HALF), BF16)], [], 10**8, "merge_part")[0]


def gather_hidden(shard):
    return lax.all_gather(shard, "pairs", axis=1, tiled=True)


def on_device(
    features,
    image_slot,
    slot_images,
    slot_count,
    gain_self,
    gain_query,
    gain_memory,
    gain_mlp,
    gain_head,
    w_qkv,
    w_self_out,
    w_query,
    w_memory,
    w_cross_out,
    w_fc1,
    w_fc2,
    w_head,
):
    place = jnp.stack([lax.axis_index("pairs"), lax.axis_index("side")]).astype(jnp.int32)
    fc = gather_hidden(jnp.concatenate([w_fc1, w_fc2], axis=0))
    blocks = [features]
    for _ in range(1, WINDOW):
        blocks.append(shifted(blocks[-1], -1))
    mine = jnp.concatenate(blocks, axis=0)
    theirs = other_core(mine)
    scalars = [image_slot, slot_images.reshape(-1), place]
    first, query = self_call(
        scalars, mine, theirs, gain_self, gain_query, w_qkv[0], w_self_out[0], w_query[0]
    )
    second, mlp_in = cross_call(
        scalars, mine, theirs, first, query, gain_memory, gain_mlp, w_memory[0], w_cross_out[0]
    )
    keep, send = mlp_call(place, second, mlp_in, fc, gain_head, w_head[0])
    got = other_core(send)
    pieces = window_call([image_slot, slot_images.reshape(-1), slot_count, place], keep, got)
    passed = shifted(pieces[3], 1)
    for w in (2, 1):
        passed = shifted((pieces[w].astype(F32) + passed.astype(F32)).astype(BF16), 1)
    return merge_call(pieces[0], passed)


def solution(mesh):
    placed = (
        P("pairs", None, "side"),
        P(),
        P("pairs", None),
        P("pairs"),
        P("side", None),
        P("side", None),
        P("side", None),
        P("side", None),
        P("side", None),
        P("side", None, None),
        P("side", None, None),
        P("side", None, None),
        P("side", None, None),
        P("side", None, None),
        P("side", "pairs", None),
        P("side", "pairs", None),
        P("side", None, None),
    )
    return jax.shard_map(
        on_device, mesh=mesh, in_specs=placed, out_specs=P("pairs", None, "side"), check_vma=False
    )
```

```python
import jax
import jax.numpy as jnp
from jax import lax
from jax.experimental import pallas as pl
from jax.experimental.pallas import tpu as pltpu
from jax.sharding import PartitionSpec as P

D = 768
HEAD_DIM = 64
TOKI = 196
ROWS = 208
HALF = 384
WINDOW = 4
SLOTS = 3
ALL = SLOTS * ROWS
CHUNK = 256
F32 = jnp.float32
BF16 = jnp.bfloat16


def shifted(array, by):
    count = lax.axis_size("pairs")
    return lax.ppermute(array, "pairs", [(i, (i + by) % count) for i in range(count)])


def other_core(array):
    return lax.ppermute(array, "side", [(0, 1), (1, 0)])


def layer_norm(values, gain):
    center = values - jnp.mean(values, axis=-1, keepdims=True)
    spread = jnp.mean(center * center, axis=-1, keepdims=True)
    return center * lax.rsqrt(spread + 1e-06) * gain


def window_place(image_slot, slot_images, place, slot, which):
    stored = image_slot[slot_images[2 * slot + which]]
    return lax.rem(stored - place[0] + 128, 128)


def load_tokens(image_slot, slot_images, place, mine, theirs, swap, slot):
    which = place[1] if not swap else 1 - place[1]
    index = window_place(image_slot, slot_images, place, slot, which)
    first = place[1] == 0
    low = mine[index].astype(F32)
    high = theirs[index].astype(F32)
    return jnp.where(first, low, high), jnp.where(first, high, low)


def padded_rows(image_slot, slot_images, place, mine, theirs, swap, target):
    for slot in range(SLOTS):
        low, high = load_tokens(image_slot, slot_images, place, mine, theirs, swap, slot)
        base = slot * ROWS
        target[base + 192 : base + ROWS, :] = jnp.zeros((ROWS - 192, D), F32)
        target[base : base + TOKI, :HALF] = low
        target[base : base + TOKI, HALF:] = high


def norm_into(source, gain, target):
    for slot in range(SLOTS):
        rows = slice(slot * ROWS, (slot + 1) * ROWS)
        target[rows, :] = layer_norm(source[rows, :], gain[...]).astype(BF16)


def attention(q_ref, q_base, k_ref, k_base, v_ref, v_base, out_ref):
    lane = lax.broadcasted_iota(jnp.int32, (ROWS, 128), 1)
    low_lanes = lane < HEAD_DIM
    key_ok = lax.broadcasted_iota(jnp.int32, (ROWS, ROWS), 1) < TOKI

    def step(t, carry):
        slot = t // 3
        group = t - 3 * slot
        rows = pl.ds(pl.multiple_of(slot * ROWS, ROWS), ROWS)
        for pair in range(2):
            col = group * 256 + pair * 128
            q = q_ref[rows, pl.ds(pl.multiple_of(q_base + col, 128), 128)]
            k = k_ref[rows, pl.ds(pl.multiple_of(k_base + col, 128), 128)]
            v = v_ref[rows, pl.ds(pl.multiple_of(v_base + col, 128), 128)]
            outs = []
            for head in range(2):
                own = low_lanes if head == 0 else jnp.logical_not(low_lanes)
                scores = lax.dot_general(
                    jnp.where(own, q, jnp.zeros_like(q)),
                    k,
                    (((1,), (1,)), ((), ())),
                    preferred_element_type=F32,
                )
                expon = jnp.where(key_ok, jnp.exp(scores), 0.0)
                total = jnp.sum(expon, axis=-1, keepdims=True)
                weights = (expon * (1.0 / total)).astype(BF16)
                outs.append(jnp.dot(weights, v, preferred_element_type=F32))
            out_ref[rows, pl.ds(pl.multiple_of(col, 128), 128)] = jnp.where(
                low_lanes, outs[0], outs[1]
            ).astype(BF16)
        return carry

    lax.fori_loop(0, 3 * SLOTS, step, 0)


def project(source, weight, width, write):
    def step(n, carry):
        cols = pl.ds(pl.multiple_of(n * 256, 256), 256)
        write(n, cols, jnp.dot(source[...], weight[:, cols], preferred_element_type=F32))
        return carry

    lax.fori_loop(0, width // 256, step, 0)


def triple_kernel(
    image_slot, slot_images, place, mine, theirs, g_self, w_qkv, rows_ref, triple_ref, hidden
):
    padded_rows(image_slot, slot_images, place, mine, theirs, False, rows_ref)
    norm_into(rows_ref, g_self, hidden)

    def write_triple(n, cols, value):
        triple_ref[:, cols] = (value * jnp.where(n < 3, 0.125, 1.0)).astype(BF16)

    project(hidden, w_qkv, 3 * D, write_triple)


def memory_kernel(
    image_slot, slot_images, place, mine, theirs, g_memory, w_memory, kv_ref, rows, hidden
):
    padded_rows(image_slot, slot_images, place, mine, theirs, True, rows)
    norm_into(rows, g_memory, hidden)

    def write_kv(n, cols, value):
        kv_ref[:, cols] = value.astype(BF16)

    project(hidden, w_memory, 2 * D, write_kv)


def self_kernel(rows, triple, g_query, w_out, w_query, first_ref, query_ref, hidden, mixed):
    attention(triple, 0, triple, D, triple, 2 * D, mixed)

    def add_first(n, cols, value):
        first_ref[:, cols] = rows[:, cols] + value

    project(mixed, w_out, D, add_first)
    norm_into(first_ref, g_query, hidden)

    def write_query(n, cols, value):
        query_ref[:, cols] = (value * 0.125).astype(BF16)

    project(hidden, w_query, D, write_query)


def cross_kernel(first, query, key_value, g_mlp, w_out, second_ref, mlp_ref, mixed):
    attention(query, 0, key_value, 0, key_value, D, mixed)

    def add_second(n, cols, value):
        second_ref[:, cols] = first[:, cols] + value

    project(mixed, w_out, D, add_second)
    norm_into(second_ref, g_mlp, mlp_ref)


def gelu(value):
    return value * (1.0 + lax.erf(value * 0.7071067811865476)) * 0.5


def hidden_units(mlp_in, fc, pre, total):
    steps = fc.shape[1] // CHUNK

    def before(c):
        rows = pl.ds(pl.multiple_of(c * CHUNK, CHUNK), CHUNK)
        return lax.dot_general(
            mlp_in[...], fc[0, rows, :], (((1,), (1,)), ((), ())), preferred_element_type=F32
        )

    def after(c, active):
        rows = pl.ds(pl.multiple_of(c * CHUNK, CHUNK), CHUNK)
        total[...] = total[...] + jnp.dot(active, fc[1, rows, :], preferred_element_type=F32)

    pre[0] = before(0)

    def step(c, carry):
        now = lax.rem(c, 2)
        active = gelu(pre[now]).astype(BF16)
        pre[1 - now] = before(c + 1)
        after(c, active)
        return carry

    lax.fori_loop(0, steps - 1, step, 0)
    after(steps - 1, gelu(pre[(steps - 1) % 2]).astype(BF16))


def early_kernel(second, mlp_in, fc, total, pre):
    total[...] = second[...]
    hidden_units(mlp_in, fc, pre, total)


def late_kernel(place, early, mlp_in, fc, g_head, w_head, keep_ref, send_ref, pre, total, hidden):
    total[...] = early[...]
    hidden_units(mlp_in, fc, pre, total)
    norm_into(total, g_head, hidden)
    first = place[1] == 0
    for slot in range(SLOTS):
        rows = slice(slot * ROWS, (slot + 1) * ROWS)
        terms = []
        for half in range(2):
            raw = jnp.dot(
                hidden[rows, :], w_head[:, half * 512 : (half + 1) * 512],
                preferred_element_type=F32,
            )
            conf = 1.0 + jnp.exp(raw[:, 384:])
            terms.append([conf * raw[:, c * 128 : (c + 1) * 128] for c in range(3)] + [conf])
        for c in range(4):
            cols = slice(c * 128, (c + 1) * 128)
            low, high = terms[0][c][:TOKI], terms[1][c][:TOKI]
            keep_ref[slot, :, cols] = jnp.where(first, low, high)
            send_ref[slot, :, cols] = jnp.where(first, high, low).astype(BF16)


def window_kernel(
    image_slot, slot_images, slot_count, place, keep, got, out0, out1, out2, out3
):
    outs = [out0, out1, out2, out3]
    chosen = []
    for slot in range(SLOTS):
        live = slot < slot_count[0]
        for which in range(2):
            index = window_place(image_slot, slot_images, place, slot, which)
            chosen.append((slot, which, jnp.where(live, index, -1)))
    for w in range(WINDOW):
        for c in range(4):
            cols = slice(c * 128, (c + 1) * 128)
            acc = jnp.zeros((TOKI, 128), F32)
            for slot in range(SLOTS):
                own = jnp.where(place[1] == 0, chosen[2 * slot][2], chosen[2 * slot + 1][2])
                far = jnp.where(place[1] == 0, chosen[2 * slot + 1][2], chosen[2 * slot][2])
                acc = acc + jnp.where(own == w, keep[slot, :, cols], 0.0)
                acc = acc + jnp.where(far == w, got[slot, :, cols].astype(F32), 0.0)
            outs[w][:, cols] = acc.astype(outs[w].dtype)


def merge_kernel(base, passed, out):
    weight = jnp.maximum(base[:, 384:] + passed[:, 384:].astype(F32), 1.0)
    for c in range(3):
        cols = slice(c * 128, (c + 1) * 128)
        out[0, :, cols] = ((base[:, cols] + passed[:, cols].astype(F32)) / weight).astype(BF16)


SMEM = pl.BlockSpec(memory_space=pltpu.SMEM)
VMEM = pl.BlockSpec(memory_space=pltpu.VMEM)


def call(kernel, scalars, arrays, outs, scratch, flops, name):
    return pl.pallas_call(
        kernel,
        in_specs=[SMEM] * len(scalars) + [VMEM] * len(arrays),
        out_specs=[VMEM] * len(outs),
        out_shape=[jax.ShapeDtypeStruct(s, d) for s, d in outs],
        scratch_shapes=[pltpu.VMEM(s, d) for s, d in scratch],
        compiler_params=pltpu.CompilerParams(vmem_limit_bytes=48 << 20),
        cost_estimate=pl.CostEstimate(flops=flops, transcendentals=0, bytes_accessed=8 << 20),
        name=name,
    )(*scalars, *arrays)


def triple_call(scalars, mine, theirs, g_self, w_qkv):
    return call(
        triple_kernel, scalars, [mine, theirs, g_self, w_qkv],
        [((ALL, D), F32), ((ALL, 3 * D), BF16)], [((ALL, D), BF16)],
        4 * 10**9, "triple_part",
    )


def memory_call(scalars, mine, theirs, g_memory, w_memory):
    return call(
        memory_kernel, scalars, [mine, theirs, g_memory, w_memory],
        [((ALL, 2 * D), BF16)], [((ALL, D), F32), ((ALL, D), BF16)],
        3 * 10**9, "memory_part",
    )[0]


def self_call(rows, triple, g_query, w_out, w_query):
    return call(
        self_kernel, [], [rows, triple, g_query, w_out, w_query],
        [((ALL, D), F32), ((ALL, D), BF16)], [((ALL, D), BF16), ((ALL, D), BF16)],
        12 * 10**9, "self_part",
    )


def cross_call(first, query, key_value, g_mlp, w_out):
    return call(
        cross_kernel, [], [first, query, key_value, g_mlp, w_out],
        [((ALL, D), F32), ((ALL, D), BF16)], [((ALL, D), BF16)],
        12 * 10**9, "cross_part",
    )


def early_call(second, mlp_in, fc):
    return call(
        early_kernel, [], [second, mlp_in, fc],
        [((ALL, D), F32)], [((2, ALL, CHUNK), F32)], 10 * 10**9, "early_part",
    )[0]


def late_call(place, early, mlp_in, fc, g_head, w_head):
    return call(
        late_kernel, [place], [early, mlp_in, fc, g_head, w_head],
        [((SLOTS, TOKI, 512), F32), ((SLOTS, TOKI, 512), BF16)],
        [((2, ALL, CHUNK), F32), ((ALL, D), F32), ((ALL, D), BF16)],
        5 * 10**9, "late_part",
    )


def window_call(scalars, keep, got):
    return call(
        window_kernel, scalars, [keep, got],
        [((TOKI, 512), F32)] + [((TOKI, 512), BF16)] * 3, [], 10**8, "window_part",
    )


def merge_call(base, passed):
    return call(merge_kernel, [], [base, passed], [((1, TOKI, HALF), BF16)], [], 10**8, "merge_part")[0]


def along(array, axis, by):
    count = lax.axis_size("pairs")
    stride, size = {"y": (32, 4), "x": (8, 4), "z": (1, 8)}[axis]

    def target(p):
        here = p // stride % size
        return p + ((here + by) % size - here) * stride

    return lax.ppermute(array, "pairs", [(p, target(p)) for p in range(count)])


def tied(*arrays):
    return lax.optimization_barrier(arrays)


def gather_line(shard):
    up, down = along(shard, "z", 1), along(shard, "z", -1)
    near = jnp.concatenate([up, shard, down], axis=1)
    far = along(near, "z", 3)
    other = along(near[:, : 2 * shard.shape[1]], "z", -3)
    return jnp.concatenate([near, far, other], axis=1)


def first_hop(block, axis):
    return along(block, axis, 1), along(block, axis, -1)


def second_hop(left, right, axis):
    half = left.shape[1] // 2
    return along(left[:, :half], axis, 1), along(right[:, half:], axis, -1)


def on_device(
    features,
    image_slot,
    slot_images,
    slot_count,
    gain_self,
    gain_query,
    gain_memory,
    gain_mlp,
    gain_head,
    w_qkv,
    w_self_out,
    w_query,
    w_memory,
    w_cross_out,
    w_fc1,
    w_fc2,
    w_head,
):
    place = jnp.stack([lax.axis_index("pairs"), lax.axis_index("side")]).astype(jnp.int32)
    shard = jnp.concatenate([w_fc1, w_fc2], axis=0)
    blocks = [features]
    for _ in range(1, WINDOW):
        blocks.append(shifted(blocks[-1], -1))
    mine = jnp.concatenate(blocks, axis=0)
    theirs = other_core(mine)
    line = gather_line(shard)
    half = line.shape[1] // 2
    part_x, part_y = line[:, :half], line[:, half:]
    scalars = [image_slot, slot_images.reshape(-1), place]
    near_x, near_y = first_hop(part_x, "x"), first_hop(part_y, "y")
    rows, triple = triple_call(scalars, mine, theirs, gain_self, w_qkv[0])
    near_x, near_y, rows, triple, mine, theirs = tied(near_x, near_y, rows, triple, mine, theirs)
    far_x, far_y = second_hop(*near_x, "x"), second_hop(*near_y, "y")
    key_value = memory_call(scalars, mine, theirs, gain_memory, w_memory[0])
    far_x, far_y, key_value, rows, triple = tied(far_x, far_y, key_value, rows, triple)
    plane_x = jnp.concatenate([part_x, *near_x, *far_x], axis=1)
    plane_y = jnp.concatenate([part_y, *near_y, *far_y], axis=1)
    near_x, near_y = first_hop(plane_x, "y"), first_hop(plane_y, "x")
    first, query = self_call(rows, triple, gain_query, w_self_out[0], w_query[0])
    second, mlp_in = cross_call(first, query, key_value, gain_mlp, w_cross_out[0])
    near_x, near_y, second, mlp_in = tied(near_x, near_y, second, mlp_in)
    far_x, far_y = second_hop(*near_x, "y"), second_hop(*near_y, "x")
    fc_early = jnp.concatenate([plane_x, *near_x, plane_y, *near_y], axis=1)
    early = early_call(second, mlp_in, fc_early)
    fc_late = jnp.concatenate([*far_x, *far_y], axis=1)
    keep, send = late_call(place, early, mlp_in, fc_late, gain_head, w_head[0])
    got = other_core(send)
    pieces = window_call([image_slot, slot_images.reshape(-1), slot_count, place], keep, got)
    passed = shifted(pieces[3], 1)
    for w in (2, 1):
        passed = shifted((pieces[w].astype(F32) + passed.astype(F32)).astype(BF16), 1)
    return merge_call(pieces[0], passed)


def solution(mesh):
    placed = (
        P("pairs", None, "side"),
        P(),
        P("pairs", None),
        P("pairs"),
        P("side", None),
        P("side", None),
        P("side", None),
        P("side", None),
        P("side", None),
        P("side", None, None),
        P("side", None, None),
        P("side", None, None),
        P("side", None, None),
        P("side", None, None),
        P("side", "pairs", None),
        P("side", "pairs", None),
        P("side", None, None),
    )
    return jax.shard_map(
        on_device, mesh=mesh, in_specs=placed, out_specs=P("pairs", None, "side"), check_vma=False
    )
```

```python
import jax
import jax.numpy as jnp
from jax import lax
from jax.experimental import pallas as pl
from jax.experimental.pallas import tpu as pltpu
from jax.sharding import PartitionSpec as P

D = 768
HEAD_DIM = 64
TOKI = 196
ROWS = 208
HALF = 384
WINDOW = 4
SLOTS = 3
ALL = SLOTS * ROWS
CHUNK = 256
F32 = jnp.float32
BF16 = jnp.bfloat16


def shifted(array, by):
    count = lax.axis_size("pairs")
    return lax.ppermute(array, "pairs", [(i, (i + by) % count) for i in range(count)])


def other_core(array):
    return lax.ppermute(array, "side", [(0, 1), (1, 0)])


def layer_norm(values, gain):
    center = values - jnp.mean(values, axis=-1, keepdims=True)
    spread = jnp.mean(center * center, axis=-1, keepdims=True)
    return center * lax.rsqrt(spread + 1e-06) * gain


def window_place(image_slot, slot_images, place, slot, which):
    stored = image_slot[slot_images[2 * slot + which]]
    return lax.rem(stored - place[0] + 128, 128)


def load_tokens(image_slot, slot_images, place, mine, theirs, swap, slot):
    which = place[1] if not swap else 1 - place[1]
    index = window_place(image_slot, slot_images, place, slot, which)
    first = place[1] == 0
    low = mine[index].astype(F32)
    high = theirs[index].astype(F32)
    return jnp.where(first, low, high), jnp.where(first, high, low)


def padded_rows(image_slot, slot_images, place, mine, theirs, swap, target):
    for slot in range(SLOTS):
        low, high = load_tokens(image_slot, slot_images, place, mine, theirs, swap, slot)
        base = slot * ROWS
        target[base + 192 : base + ROWS, :] = jnp.zeros((ROWS - 192, D), F32)
        target[base : base + TOKI, :HALF] = low
        target[base : base + TOKI, HALF:] = high


def norm_into(source, gain, target):
    for slot in range(SLOTS):
        rows = slice(slot * ROWS, (slot + 1) * ROWS)
        target[rows, :] = layer_norm(source[rows, :], gain[...]).astype(BF16)


def attention(q_ref, q_base, k_ref, k_base, v_ref, v_base, out_ref):
    lane = lax.broadcasted_iota(jnp.int32, (ROWS, 128), 1)
    low_lanes = lane < HEAD_DIM
    key_ok = lax.broadcasted_iota(jnp.int32, (ROWS, ROWS), 1) < TOKI

    def step(t, carry):
        slot = t // 3
        group = t - 3 * slot
        rows = pl.ds(pl.multiple_of(slot * ROWS, ROWS), ROWS)
        for pair in range(2):
            col = group * 256 + pair * 128
            q = q_ref[rows, pl.ds(pl.multiple_of(q_base + col, 128), 128)]
            k = k_ref[rows, pl.ds(pl.multiple_of(k_base + col, 128), 128)]
            v = v_ref[rows, pl.ds(pl.multiple_of(v_base + col, 128), 128)]
            outs = []
            for head in range(2):
                own = low_lanes if head == 0 else jnp.logical_not(low_lanes)
                scores = lax.dot_general(
                    jnp.where(own, q, jnp.zeros_like(q)),
                    k,
                    (((1,), (1,)), ((), ())),
                    preferred_element_type=F32,
                )
                expon = jnp.where(key_ok, jnp.exp(scores), 0.0)
                total = jnp.sum(expon, axis=-1, keepdims=True)
                weights = (expon * (1.0 / total)).astype(BF16)
                outs.append(jnp.dot(weights, v, preferred_element_type=F32))
            out_ref[rows, pl.ds(pl.multiple_of(col, 128), 128)] = jnp.where(
                low_lanes, outs[0], outs[1]
            ).astype(BF16)
        return carry

    lax.fori_loop(0, 3 * SLOTS, step, 0)


def project(source, weight, width, write):
    def step(n, carry):
        cols = pl.ds(pl.multiple_of(n * 256, 256), 256)
        write(n, cols, jnp.dot(source[...], weight[:, cols], preferred_element_type=F32))
        return carry

    lax.fori_loop(0, width // 256, step, 0)


def triple_kernel(
    image_slot, slot_images, place, mine, theirs, g_self, w_qkv, rows_ref, triple_ref, hidden
):
    padded_rows(image_slot, slot_images, place, mine, theirs, False, rows_ref)
    norm_into(rows_ref, g_self, hidden)

    def write_triple(n, cols, value):
        triple_ref[:, cols] = (value * jnp.where(n < 3, 0.125, 1.0)).astype(BF16)

    project(hidden, w_qkv, 3 * D, write_triple)


def memory_kernel(
    image_slot, slot_images, place, mine, theirs, g_memory, w_memory, kv_ref, rows, hidden
):
    padded_rows(image_slot, slot_images, place, mine, theirs, True, rows)
    norm_into(rows, g_memory, hidden)

    def write_kv(n, cols, value):
        kv_ref[:, cols] = value.astype(BF16)

    project(hidden, w_memory, 2 * D, write_kv)


def self_kernel(rows, triple, g_query, w_out, w_query, first_ref, query_ref, hidden, mixed):
    attention(triple, 0, triple, D, triple, 2 * D, mixed)

    def add_first(n, cols, value):
        first_ref[:, cols] = rows[:, cols] + value

    project(mixed, w_out, D, add_first)
    norm_into(first_ref, g_query, hidden)

    def write_query(n, cols, value):
        query_ref[:, cols] = (value * 0.125).astype(BF16)

    project(hidden, w_query, D, write_query)


def cross_kernel(first, query, key_value, g_mlp, w_out, second_ref, mlp_ref, mixed):
    attention(query, 0, key_value, 0, key_value, D, mixed)

    def add_second(n, cols, value):
        second_ref[:, cols] = first[:, cols] + value

    project(mixed, w_out, D, add_second)
    norm_into(second_ref, g_mlp, mlp_ref)


def gelu(value):
    return value * (1.0 + lax.erf(value * 0.7071067811865476)) * 0.5


def hidden_units(mlp_in, fc, pre, total):
    steps = fc.shape[1] // CHUNK

    def before(c):
        rows = pl.ds(pl.multiple_of(c * CHUNK, CHUNK), CHUNK)
        return lax.dot_general(
            mlp_in[...], fc[0, rows, :], (((1,), (1,)), ((), ())), preferred_element_type=F32
        )

    def after(c, active):
        rows = pl.ds(pl.multiple_of(c * CHUNK, CHUNK), CHUNK)
        total[...] = total[...] + jnp.dot(active, fc[1, rows, :], preferred_element_type=F32)

    pre[0] = before(0)

    def step(c, carry):
        now = lax.rem(c, 2)
        active = gelu(pre[now]).astype(BF16)
        pre[1 - now] = before(c + 1)
        after(c, active)
        return carry

    lax.fori_loop(0, steps - 1, step, 0)
    after(steps - 1, gelu(pre[(steps - 1) % 2]).astype(BF16))


def early_kernel(second, mlp_in, fc, total, pre):
    total[...] = second[...]
    hidden_units(mlp_in, fc, pre, total)


def late_kernel(place, early, mlp_in, fc, g_head, w_head, keep_ref, send_ref, pre, total, hidden):
    total[...] = early[...]
    hidden_units(mlp_in, fc, pre, total)
    norm_into(total, g_head, hidden)
    first = place[1] == 0
    for slot in range(SLOTS):
        rows = slice(slot * ROWS, (slot + 1) * ROWS)
        terms = []
        for half in range(2):
            raw = jnp.dot(
                hidden[rows, :], w_head[:, half * 512 : (half + 1) * 512],
                preferred_element_type=F32,
            )
            conf = 1.0 + jnp.exp(raw[:, 384:])
            terms.append([conf * raw[:, c * 128 : (c + 1) * 128] for c in range(3)] + [conf])
        for c in range(4):
            cols = slice(c * 128, (c + 1) * 128)
            low, high = terms[0][c][:TOKI], terms[1][c][:TOKI]
            keep_ref[slot, :, cols] = jnp.where(first, low, high)
            send_ref[slot, :, cols] = jnp.where(first, high, low).astype(BF16)


def window_kernel(
    image_slot, slot_images, slot_count, place, keep, got, out0, out1, out2, out3
):
    outs = [out0, out1, out2, out3]
    chosen = []
    for slot in range(SLOTS):
        live = slot < slot_count[0]
        for which in range(2):
            index = window_place(image_slot, slot_images, place, slot, which)
            chosen.append((slot, which, jnp.where(live, index, -1)))
    for w in range(WINDOW):
        for c in range(4):
            cols = slice(c * 128, (c + 1) * 128)
            acc = jnp.zeros((TOKI, 128), F32)
            for slot in range(SLOTS):
                own = jnp.where(place[1] == 0, chosen[2 * slot][2], chosen[2 * slot + 1][2])
                far = jnp.where(place[1] == 0, chosen[2 * slot + 1][2], chosen[2 * slot][2])
                acc = acc + jnp.where(own == w, keep[slot, :, cols], 0.0)
                acc = acc + jnp.where(far == w, got[slot, :, cols].astype(F32), 0.0)
            outs[w][:, cols] = acc.astype(outs[w].dtype)


def merge_kernel(base, nearest, further, out):
    def total(cols):
        return base[:, cols] + nearest[:, cols].astype(F32) + further[:, cols].astype(F32)

    weight = jnp.maximum(total(slice(384, 512)), 1.0)
    for c in range(3):
        cols = slice(c * 128, (c + 1) * 128)
        out[0, :, cols] = (total(cols) / weight).astype(BF16)


SMEM = pl.BlockSpec(memory_space=pltpu.SMEM)
VMEM = pl.BlockSpec(memory_space=pltpu.VMEM)


def call(kernel, scalars, arrays, outs, scratch, flops, name):
    return pl.pallas_call(
        kernel,
        in_specs=[SMEM] * len(scalars) + [VMEM] * len(arrays),
        out_specs=[VMEM] * len(outs),
        out_shape=[jax.ShapeDtypeStruct(s, d) for s, d in outs],
        scratch_shapes=[pltpu.VMEM(s, d) for s, d in scratch],
        compiler_params=pltpu.CompilerParams(vmem_limit_bytes=20 << 20),
        cost_estimate=pl.CostEstimate(flops=flops, transcendentals=0, bytes_accessed=8 << 20),
        name=name,
    )(*scalars, *arrays)


def triple_call(scalars, mine, theirs, g_self, w_qkv):
    return call(
        triple_kernel, scalars, [mine, theirs, g_self, w_qkv],
        [((ALL, D), F32), ((ALL, 3 * D), BF16)], [((ALL, D), BF16)],
        4 * 10**9, "triple_part",
    )


def memory_call(scalars, mine, theirs, g_memory, w_memory):
    return call(
        memory_kernel, scalars, [mine, theirs, g_memory, w_memory],
        [((ALL, 2 * D), BF16)], [((ALL, D), F32), ((ALL, D), BF16)],
        3 * 10**9, "memory_part",
    )[0]


def self_call(rows, triple, g_query, w_out, w_query):
    return call(
        self_kernel, [], [rows, triple, g_query, w_out, w_query],
        [((ALL, D), F32), ((ALL, D), BF16)], [((ALL, D), BF16), ((ALL, D), BF16)],
        12 * 10**9, "self_part",
    )


def cross_call(first, query, key_value, g_mlp, w_out):
    return call(
        cross_kernel, [], [first, query, key_value, g_mlp, w_out],
        [((ALL, D), F32), ((ALL, D), BF16)], [((ALL, D), BF16)],
        12 * 10**9, "cross_part",
    )


def early_call(second, mlp_in, fc):
    return call(
        early_kernel, [], [second, mlp_in, fc],
        [((ALL, D), F32)], [((2, ALL, CHUNK), F32)], 10 * 10**9, "early_part",
    )[0]


def late_call(place, early, mlp_in, fc, g_head, w_head):
    return call(
        late_kernel, [place], [early, mlp_in, fc, g_head, w_head],
        [((SLOTS, TOKI, 512), F32), ((SLOTS, TOKI, 512), BF16)],
        [((2, ALL, CHUNK), F32), ((ALL, D), F32), ((ALL, D), BF16)],
        5 * 10**9, "late_part",
    )


def window_call(scalars, keep, got):
    return call(
        window_kernel, scalars, [keep, got],
        [((TOKI, 512), F32)] + [((TOKI, 512), BF16)] * 3, [], 10**8, "window_part",
    )


def merge_call(*arrays):
    return call(merge_kernel, [], arrays, [((1, TOKI, HALF), BF16)], [], 10**8, "merge_part")[0]


def along(array, axis, by):
    count = lax.axis_size("pairs")
    stride, size = {"y": (32, 4), "x": (8, 4), "z": (1, 8)}[axis]

    def target(p):
        here = p // stride % size
        return p + ((here + by) % size - here) * stride

    return lax.ppermute(array, "pairs", [(p, target(p)) for p in range(count)])


def tied(*arrays):
    return lax.optimization_barrier(arrays)


def gather_line(shard):
    others = [along(shard, "z", by) for by in (4, 3, -3, 2, -2, 1, -1)]
    return jnp.concatenate([shard, *others], axis=1)


def first_hop(block, axis):
    return along(block, axis, 1), along(block, axis, -1)


def second_hop(left, right, axis):
    half = left.shape[1] // 2
    return along(left[:, :half], axis, 1), along(right[:, half:], axis, -1)


def on_device(
    features,
    image_slot,
    slot_images,
    slot_count,
    gain_self,
    gain_query,
    gain_memory,
    gain_mlp,
    gain_head,
    w_qkv,
    w_self_out,
    w_query,
    w_memory,
    w_cross_out,
    w_fc1,
    w_fc2,
    w_head,
):
    place = jnp.stack([lax.axis_index("pairs"), lax.axis_index("side")]).astype(jnp.int32)
    shard = jnp.concatenate([w_fc1, w_fc2], axis=0)
    second_next = shifted(features, -2)
    blocks = [features, shifted(features, -1), second_next, shifted(second_next, -1)]
    mine = jnp.concatenate(blocks, axis=0)
    theirs = other_core(mine)
    line = gather_line(shard)
    half = line.shape[1] // 2
    part_x, part_y = line[:, :half], line[:, half:]
    scalars = [image_slot, slot_images.reshape(-1), place]
    near_x, near_y = first_hop(part_x, "x"), first_hop(part_y, "y")
    rows, triple = triple_call(scalars, mine, theirs, gain_self, w_qkv[0])
    near_x, near_y, rows, triple, mine, theirs = tied(near_x, near_y, rows, triple, mine, theirs)
    far_x, far_y = second_hop(*near_x, "x"), second_hop(*near_y, "y")
    key_value = memory_call(scalars, mine, theirs, gain_memory, w_memory[0])
    far_x, far_y, key_value, rows, triple = tied(far_x, far_y, key_value, rows, triple)
    plane_x = jnp.concatenate([part_x, *near_x, *far_x], axis=1)
    plane_y = jnp.concatenate([part_y, *near_y, *far_y], axis=1)
    near_x, near_y = first_hop(plane_x, "y"), first_hop(plane_y, "x")
    first, query = self_call(rows, triple, gain_query, w_self_out[0], w_query[0])
    second, mlp_in = cross_call(first, query, key_value, gain_mlp, w_cross_out[0])
    near_x, near_y, second, mlp_in = tied(near_x, near_y, second, mlp_in)
    far_x, far_y = second_hop(*near_x, "y"), second_hop(*near_y, "x")
    fc_early = jnp.concatenate([plane_x, *near_x, plane_y, *near_y], axis=1)
    early = early_call(second, mlp_in, fc_early)
    fc_late = jnp.concatenate([*far_x, *far_y], axis=1)
    keep, send = late_call(place, early, mlp_in, fc_late, gain_head, w_head[0])
    got = other_core(send)
    pieces = window_call([image_slot, slot_images.reshape(-1), slot_count, place], keep, got)
    third = shifted(pieces[3], 1)
    nearest = shifted(pieces[1], 1)
    further = shifted((pieces[2].astype(F32) + third.astype(F32)).astype(BF16), 2)
    return merge_call(pieces[0], nearest, further)


def solution(mesh):
    placed = (
        P("pairs", None, "side"),
        P(),
        P("pairs", None),
        P("pairs"),
        P("side", None),
        P("side", None),
        P("side", None),
        P("side", None),
        P("side", None),
        P("side", None, None),
        P("side", None, None),
        P("side", None, None),
        P("side", None, None),
        P("side", None, None),
        P("side", "pairs", None),
        P("side", "pairs", None),
        P("side", None, None),
    )
    return jax.shard_map(
        on_device, mesh=mesh, in_specs=placed, out_specs=P("pairs", None, "side"), check_vma=False
    )
```

```python
import jax
import jax.numpy as jnp
from jax import lax
from jax.experimental import pallas as pl
from jax.experimental.pallas import tpu as pltpu
from jax.sharding import PartitionSpec as P

D = 768
HEAD_DIM = 64
TOKI = 196
ROWS = 208
HALF = 384
TOP = 104
WINDOW = 4
SLOTS = 3
ALL = SLOTS * ROWS
CHUNK = 256
F32 = jnp.float32
BF16 = jnp.bfloat16


def shifted(array, by):
    count = lax.axis_size("pairs")
    return lax.ppermute(array, "pairs", [(i, (i + by) % count) for i in range(count)])


def other_core(array):
    return lax.ppermute(array, "side", [(0, 1), (1, 0)])


def layer_norm(values, gain):
    center = values - jnp.mean(values, axis=-1, keepdims=True)
    spread = jnp.mean(center * center, axis=-1, keepdims=True)
    return center * lax.rsqrt(spread + 1e-06) * gain


def window_place(image_slot, slot_images, place, slot, which):
    stored = image_slot[slot_images[2 * slot + which]]
    return lax.rem(stored - place[0] + 128, 128)


def padded_rows(image_slot, slot_images, place, mine, theirs, swap, target):
    which = place[1] if not swap else 1 - place[1]
    first = place[1] == 0
    for slot in range(SLOTS):
        index = window_place(image_slot, slot_images, place, slot, which)
        own, far = mine[index].astype(F32), theirs[index].astype(F32)
        base = slot * ROWS
        target[base + 192 : base + ROWS, :] = jnp.zeros((ROWS - 192, D), F32)
        for part, count in ((0, TOP), (1, TOKI - TOP)):
            rows = slice(base + part * TOP, base + part * TOP + count)
            cols = slice(part * HALF, (part + 1) * HALF)
            target[rows, :HALF] = jnp.where(first, own[:count, cols], far[:count, cols])
            target[rows, HALF:] = jnp.where(first, far[:count, cols], own[:count, cols])


def norm_into(source, gain, target):
    for slot in range(SLOTS):
        rows = slice(slot * ROWS, (slot + 1) * ROWS)
        target[rows, :] = layer_norm(source[rows, :], gain[...]).astype(BF16)


def attention(q_ref, q_base, k_ref, k_base, v_ref, v_base, out_ref):
    lane = lax.broadcasted_iota(jnp.int32, (ROWS, 128), 1)
    low_lanes = lane < HEAD_DIM
    key_ok = lax.broadcasted_iota(jnp.int32, (ROWS, ROWS), 1) < TOKI

    def step(t, carry):
        slot = t // 3
        group = t - 3 * slot
        rows = pl.ds(pl.multiple_of(slot * ROWS, ROWS), ROWS)
        for pair in range(2):
            col = group * 256 + pair * 128
            q = q_ref[rows, pl.ds(pl.multiple_of(q_base + col, 128), 128)]
            k = k_ref[rows, pl.ds(pl.multiple_of(k_base + col, 128), 128)]
            v = v_ref[rows, pl.ds(pl.multiple_of(v_base + col, 128), 128)]
            outs = []
            for head in range(2):
                own = low_lanes if head == 0 else jnp.logical_not(low_lanes)
                scores = lax.dot_general(
                    jnp.where(own, q, jnp.zeros_like(q)),
                    k,
                    (((1,), (1,)), ((), ())),
                    preferred_element_type=F32,
                )
                expon = jnp.where(key_ok, jnp.exp(scores), 0.0)
                total = jnp.sum(expon, axis=-1, keepdims=True)
                weights = (expon * (1.0 / total)).astype(BF16)
                outs.append(jnp.dot(weights, v, preferred_element_type=F32))
            out_ref[rows, pl.ds(pl.multiple_of(col, 128), 128)] = jnp.where(
                low_lanes, outs[0], outs[1]
            ).astype(BF16)
        return carry

    lax.fori_loop(0, 3 * SLOTS, step, 0)


def project(source, weight, width, write):
    def step(n, carry):
        cols = pl.ds(pl.multiple_of(n * 256, 256), 256)
        write(n, cols, jnp.dot(source[...], weight[:, cols], preferred_element_type=F32))
        return carry

    lax.fori_loop(0, width // 256, step, 0)


def triple_kernel(
    image_slot, slot_images, place, mine, theirs, g_self, w_qkv, rows_ref, triple_ref, hidden
):
    padded_rows(image_slot, slot_images, place, mine, theirs, False, rows_ref)
    norm_into(rows_ref, g_self, hidden)

    def write_triple(n, cols, value):
        triple_ref[:, cols] = (value * jnp.where(n < 3, 0.125, 1.0)).astype(BF16)

    project(hidden, w_qkv, 3 * D, write_triple)


def memory_kernel(
    image_slot, slot_images, place, mine, theirs, g_memory, w_memory, kv_ref, rows, hidden
):
    padded_rows(image_slot, slot_images, place, mine, theirs, True, rows)
    norm_into(rows, g_memory, hidden)

    def write_kv(n, cols, value):
        kv_ref[:, cols] = value.astype(BF16)

    project(hidden, w_memory, 2 * D, write_kv)


def self_kernel(rows, triple, g_query, w_out, w_query, first_ref, query_ref, hidden, mixed):
    attention(triple, 0, triple, D, triple, 2 * D, mixed)

    def add_first(n, cols, value):
        first_ref[:, cols] = rows[:, cols] + value

    project(mixed, w_out, D, add_first)
    norm_into(first_ref, g_query, hidden)

    def write_query(n, cols, value):
        query_ref[:, cols] = (value * 0.125).astype(BF16)

    project(hidden, w_query, D, write_query)


def cross_kernel(first, query, key_value, g_mlp, w_out, second_ref, mlp_ref, mixed):
    attention(query, 0, key_value, 0, key_value, D, mixed)

    def add_second(n, cols, value):
        second_ref[:, cols] = first[:, cols] + value

    project(mixed, w_out, D, add_second)
    norm_into(second_ref, g_mlp, mlp_ref)


def gelu(value):
    return value * (1.0 + lax.erf(value * 0.7071067811865476)) * 0.5


def hidden_units(mlp_in, fc, pre, total):
    steps = fc.shape[1] // CHUNK

    def before(c):
        rows = pl.ds(pl.multiple_of(c * CHUNK, CHUNK), CHUNK)
        return lax.dot_general(
            mlp_in[...], fc[0, rows, :], (((1,), (1,)), ((), ())), preferred_element_type=F32
        )

    def after(c, active):
        rows = pl.ds(pl.multiple_of(c * CHUNK, CHUNK), CHUNK)
        total[...] = total[...] + jnp.dot(active, fc[1, rows, :], preferred_element_type=F32)

    pre[0] = before(0)

    def step(c, carry):
        now = lax.rem(c, 2)
        active = gelu(pre[now]).astype(BF16)
        pre[1 - now] = before(c + 1)
        after(c, active)
        return carry

    lax.fori_loop(0, steps - 1, step, 0)
    after(steps - 1, gelu(pre[(steps - 1) % 2]).astype(BF16))


def early_kernel(second, mlp_in, fc, total, pre):
    total[...] = second[...]
    hidden_units(mlp_in, fc, pre, total)


def late_kernel(place, early, mlp_in, fc, g_head, w_head, keep_ref, send_ref, pre, total, hidden):
    total[...] = early[...]
    hidden_units(mlp_in, fc, pre, total)
    norm_into(total, g_head, hidden)
    first = place[1] == 0
    for slot in range(SLOTS):
        rows = slice(slot * ROWS, (slot + 1) * ROWS)
        terms = []
        for half in range(2):
            raw = jnp.dot(
                hidden[rows, :], w_head[:, half * 512 : (half + 1) * 512],
                preferred_element_type=F32,
            )
            conf = 1.0 + jnp.exp(raw[:, 384:])
            terms.append([conf * raw[:, c * 128 : (c + 1) * 128] for c in range(3)] + [conf])
        for c in range(4):
            cols = slice(c * 128, (c + 1) * 128)
            low, high = terms[0][c][:TOKI], terms[1][c][:TOKI]
            keep_ref[slot, :, cols] = jnp.where(first, low, high)
            send_ref[slot, :, cols] = jnp.where(first, high, low).astype(BF16)


def window_kernel(
    image_slot, slot_images, slot_count, place, keep, got, out0, out1, out2, out3
):
    outs = [out0, out1, out2, out3]
    chosen = []
    for slot in range(SLOTS):
        live = slot < slot_count[0]
        for which in range(2):
            index = window_place(image_slot, slot_images, place, slot, which)
            chosen.append((slot, which, jnp.where(live, index, -1)))
    for w in range(WINDOW):
        for c in range(4):
            cols = slice(c * 128, (c + 1) * 128)
            acc = jnp.zeros((TOKI, 128), F32)
            for slot in range(SLOTS):
                own = jnp.where(place[1] == 0, chosen[2 * slot][2], chosen[2 * slot + 1][2])
                far = jnp.where(place[1] == 0, chosen[2 * slot + 1][2], chosen[2 * slot][2])
                acc = acc + jnp.where(own == w, keep[slot, :, cols], 0.0)
                acc = acc + jnp.where(far == w, got[slot, :, cols].astype(F32), 0.0)
            outs[w][:, cols] = acc.astype(outs[w].dtype)


def merge_kernel(base, nearest, further, out):
    def total(cols):
        return base[:, cols] + nearest[:, cols].astype(F32) + further[:, cols].astype(F32)

    weight = jnp.maximum(total(slice(384, 512)), 1.0)
    for c in range(3):
        cols = slice(c * 128, (c + 1) * 128)
        out[0, :, cols] = (total(cols) / weight).astype(BF16)


SMEM = pl.BlockSpec(memory_space=pltpu.SMEM)
VMEM = pl.BlockSpec(memory_space=pltpu.VMEM)


def call(kernel, scalars, arrays, outs, scratch, flops, name):
    return pl.pallas_call(
        kernel,
        in_specs=[SMEM] * len(scalars) + [VMEM] * len(arrays),
        out_specs=[VMEM] * len(outs),
        out_shape=[jax.ShapeDtypeStruct(s, d) for s, d in outs],
        scratch_shapes=[pltpu.VMEM(s, d) for s, d in scratch],
        compiler_params=pltpu.CompilerParams(vmem_limit_bytes=20 << 20),
        cost_estimate=pl.CostEstimate(flops=flops, transcendentals=0, bytes_accessed=8 << 20),
        name=name,
    )(*scalars, *arrays)


def triple_call(scalars, mine, theirs, g_self, w_qkv):
    return call(
        triple_kernel, scalars, [mine, theirs, g_self, w_qkv],
        [((ALL, D), F32), ((ALL, 3 * D), BF16)], [((ALL, D), BF16)],
        4 * 10**9, "triple_part",
    )


def memory_call(scalars, mine, theirs, g_memory, w_memory):
    return call(
        memory_kernel, scalars, [mine, theirs, g_memory, w_memory],
        [((ALL, 2 * D), BF16)], [((ALL, D), F32), ((ALL, D), BF16)],
        3 * 10**9, "memory_part",
    )[0]


def self_call(rows, triple, g_query, w_out, w_query):
    return call(
        self_kernel, [], [rows, triple, g_query, w_out, w_query],
        [((ALL, D), F32), ((ALL, D), BF16)], [((ALL, D), BF16), ((ALL, D), BF16)],
        12 * 10**9, "self_part",
    )


def cross_call(first, query, key_value, g_mlp, w_out):
    return call(
        cross_kernel, [], [first, query, key_value, g_mlp, w_out],
        [((ALL, D), F32), ((ALL, D), BF16)], [((ALL, D), BF16)],
        12 * 10**9, "cross_part",
    )


def early_call(second, mlp_in, fc):
    return call(
        early_kernel, [], [second, mlp_in, fc],
        [((ALL, D), F32)], [((2, ALL, CHUNK), F32)], 10 * 10**9, "early_part",
    )[0]


def late_call(place, early, mlp_in, fc, g_head, w_head):
    return call(
        late_kernel, [place], [early, mlp_in, fc, g_head, w_head],
        [((SLOTS, TOKI, 512), F32), ((SLOTS, TOKI, 512), BF16)],
        [((2, ALL, CHUNK), F32), ((ALL, D), F32), ((ALL, D), BF16)],
        5 * 10**9, "late_part",
    )


def window_call(scalars, keep, got):
    return call(
        window_kernel, scalars, [keep, got],
        [((TOKI, 512), F32)] + [((TOKI, 512), BF16)] * 3, [], 10**8, "window_part",
    )


def merge_call(*arrays):
    return call(merge_kernel, [], arrays, [((1, TOKI, HALF), BF16)], [], 10**8, "merge_part")[0]


def along(array, axis, by):
    count = lax.axis_size("pairs")
    stride, size = {"y": (32, 4), "x": (8, 4), "z": (1, 8)}[axis]

    def target(p):
        here = p // stride % size
        return p + ((here + by) % size - here) * stride

    return lax.ppermute(array, "pairs", [(p, target(p)) for p in range(count)])


def tied(*arrays):
    return lax.optimization_barrier(arrays)


def packed_shard(features, w_in, w_out):
    low, high = features[0, :TOP], features[0, TOP:]
    high = jnp.pad(high, ((0, 2 * TOP - TOKI), (0, 0)))
    return jnp.concatenate([jnp.concatenate([low, high], axis=1), w_in[0], w_out[0]], axis=0)


def hidden_rows(shards):
    inner = [s[-48:-24] for s in shards]
    outer = [s[-24:] for s in shards]
    return jnp.stack([jnp.concatenate(inner, axis=0), jnp.concatenate(outer, axis=0)])


def three_hops(block, axis):
    return [along(block, axis, by) for by in (1, -1, 2)]


def first_hop(block, axis):
    return along(block, axis, 1), along(block, axis, -1)


def second_hop(left, right, axis):
    half = left.shape[1] // 2
    return along(left[:, :half], axis, 1), along(right[:, half:], axis, -1)


def on_device(
    features,
    image_slot,
    slot_images,
    slot_count,
    gain_self,
    gain_query,
    gain_memory,
    gain_mlp,
    gain_head,
    w_qkv,
    w_self_out,
    w_query,
    w_memory,
    w_cross_out,
    w_fc1,
    w_fc2,
    w_head,
):
    place = jnp.stack([lax.axis_index("pairs"), lax.axis_index("side")]).astype(jnp.int32)
    (own,) = tied(packed_shard(features, w_fc1, w_fc2))
    next2 = shifted(own, -2)
    next1 = shifted(own, -1)
    last1 = shifted(own[TOP:], 1)
    last2 = shifted(own[TOP:], 2)
    next2, next1, last1, last2 = tied(next2, next1, last1, last2)
    next3 = shifted(next2, -1)
    last34 = shifted(jnp.concatenate([last1, last2], axis=0), 2)
    mine = jnp.stack([own[:TOP], next1[:TOP], next2[:TOP], next3[:TOP]])
    theirs = other_core(mine)
    part_x = hidden_rows([own, next1, next2, last1])
    part_y = hidden_rows([last2, next3, last34[:48], last34[48:]])
    scalars = [image_slot, slot_images.reshape(-1), place]
    near_x, near_y = three_hops(part_x, "x"), three_hops(part_y, "y")
    rows, triple = triple_call(scalars, mine, theirs, gain_self, w_qkv[0])
    key_value = memory_call(scalars, mine, theirs, gain_memory, w_memory[0])
    near_x, near_y, rows, triple, key_value = tied(near_x, near_y, rows, triple, key_value)
    plane_x = jnp.concatenate([part_x, *near_x], axis=1)
    plane_y = jnp.concatenate([part_y, *near_y], axis=1)
    near_x, near_y = first_hop(plane_x, "y"), first_hop(plane_y, "x")
    first, query = self_call(rows, triple, gain_query, w_self_out[0], w_query[0])
    second, mlp_in = cross_call(first, query, key_value, gain_mlp, w_cross_out[0])
    near_x, near_y, second, mlp_in = tied(near_x, near_y, second, mlp_in)
    far_x, far_y = second_hop(*near_x, "y"), second_hop(*near_y, "x")
    fc_early = jnp.concatenate([plane_x, *near_x, plane_y, *near_y], axis=1)
    early = early_call(second, mlp_in, fc_early)
    fc_late = jnp.concatenate([*far_x, *far_y], axis=1)
    keep, send = late_call(place, early, mlp_in, fc_late, gain_head, w_head[0])
    got = other_core(send)
    pieces = window_call([image_slot, slot_images.reshape(-1), slot_count, place], keep, got)
    third, nearest = tied(shifted(pieces[3], 1), pieces[1])
    further = shifted((pieces[2].astype(F32) + third.astype(F32)).astype(BF16), 2)
    nearest = shifted(nearest, 1)
    return merge_call(pieces[0], nearest, further)


def solution(mesh):
    placed = (
        P("pairs", None, "side"),
        P(),
        P("pairs", None),
        P("pairs"),
        P("side", None),
        P("side", None),
        P("side", None),
        P("side", None),
        P("side", None),
        P("side", None, None),
        P("side", None, None),
        P("side", None, None),
        P("side", None, None),
        P("side", None, None),
        P("side", "pairs", None),
        P("side", "pairs", None),
        P("side", None, None),
    )
    return jax.shard_map(
        on_device, mesh=mesh, in_specs=placed, out_specs=P("pairs", None, "side"), check_vma=False
    )
```

```python
import jax
import jax.numpy as jnp
from jax import lax
from jax.experimental import pallas as pl
from jax.experimental.pallas import tpu as pltpu
from jax.sharding import PartitionSpec as P

D = 768
HEAD_DIM = 64
TOKI = 196
ROWS = 208
HALF = 384
TOP = 104
WINDOW = 4
SLOTS = 3
ALL = SLOTS * ROWS
CHUNK = 256
F32 = jnp.float32
BF16 = jnp.bfloat16


def shifted(array, by):
    count = lax.axis_size("pairs")
    return lax.ppermute(array, "pairs", [(i, (i + by) % count) for i in range(count)])


def other_core(array):
    return lax.ppermute(array, "side", [(0, 1), (1, 0)])


def layer_norm(values, gain):
    center = values - jnp.mean(values, axis=-1, keepdims=True)
    spread = jnp.mean(center * center, axis=-1, keepdims=True)
    return center * lax.rsqrt(spread + 1e-06) * gain


def window_place(image_slot, slot_images, place, slot, which):
    stored = image_slot[slot_images[2 * slot + which]]
    return lax.rem(stored - place[0] + 128, 128)


def padded_rows(image_slot, slot_images, place, mine, theirs, swap, target):
    which = place[1] if not swap else 1 - place[1]
    first = place[1] == 0
    for slot in range(SLOTS):
        index = window_place(image_slot, slot_images, place, slot, which)
        own, far = mine[index].astype(F32), theirs[index].astype(F32)
        base = slot * ROWS
        target[base + 192 : base + ROWS, :] = jnp.zeros((ROWS - 192, D), F32)
        for part, count in ((0, TOP), (1, TOKI - TOP)):
            rows = slice(base + part * TOP, base + part * TOP + count)
            cols = slice(part * HALF, (part + 1) * HALF)
            target[rows, :HALF] = jnp.where(first, own[:count, cols], far[:count, cols])
            target[rows, HALF:] = jnp.where(first, far[:count, cols], own[:count, cols])


def norm_into(source, gain, target):
    for slot in range(SLOTS):
        rows = slice(slot * ROWS, (slot + 1) * ROWS)
        target[rows, :] = layer_norm(source[rows, :], gain[...]).astype(BF16)


def attention(q_ref, q_base, k_ref, k_base, v_ref, v_base, out_ref):
    lane = lax.broadcasted_iota(jnp.int32, (ROWS, 128), 1)
    low_lanes = lane < HEAD_DIM
    key_ok = lax.broadcasted_iota(jnp.int32, (ROWS, ROWS), 1) < TOKI

    def step(t, carry):
        slot = t // 3
        group = t - 3 * slot
        rows = pl.ds(pl.multiple_of(slot * ROWS, ROWS), ROWS)
        for pair in range(2):
            col = group * 256 + pair * 128
            q = q_ref[rows, pl.ds(pl.multiple_of(q_base + col, 128), 128)]
            k = k_ref[rows, pl.ds(pl.multiple_of(k_base + col, 128), 128)]
            v = v_ref[rows, pl.ds(pl.multiple_of(v_base + col, 128), 128)]
            outs = []
            for head in range(2):
                own = low_lanes if head == 0 else jnp.logical_not(low_lanes)
                scores = lax.dot_general(
                    jnp.where(own, q, jnp.zeros_like(q)),
                    k,
                    (((1,), (1,)), ((), ())),
                    preferred_element_type=F32,
                )
                expon = jnp.where(key_ok, jnp.exp(scores), 0.0)
                total = jnp.sum(expon, axis=-1, keepdims=True)
                weights = (expon * (1.0 / total)).astype(BF16)
                outs.append(jnp.dot(weights, v, preferred_element_type=F32))
            out_ref[rows, pl.ds(pl.multiple_of(col, 128), 128)] = jnp.where(
                low_lanes, outs[0], outs[1]
            ).astype(BF16)
        return carry

    lax.fori_loop(0, 3 * SLOTS, step, 0)


def project(source, weight, width, write):
    def step(n, carry):
        cols = pl.ds(pl.multiple_of(n * 256, 256), 256)
        write(n, cols, jnp.dot(source[...], weight[:, cols], preferred_element_type=F32))
        return carry

    lax.fori_loop(0, width // 256, step, 0)


def triple_kernel(
    image_slot, slot_images, place, mine, theirs, g_self, w_qkv, rows_ref, triple_ref, hidden
):
    padded_rows(image_slot, slot_images, place, mine, theirs, False, rows_ref)
    norm_into(rows_ref, g_self, hidden)

    def write_triple(n, cols, value):
        triple_ref[:, cols] = (value * jnp.where(n < 3, 0.125, 1.0)).astype(BF16)

    project(hidden, w_qkv, 3 * D, write_triple)


def memory_kernel(
    image_slot, slot_images, place, mine, theirs, g_memory, w_memory, kv_ref, rows, hidden
):
    padded_rows(image_slot, slot_images, place, mine, theirs, True, rows)
    norm_into(rows, g_memory, hidden)

    def write_kv(n, cols, value):
        kv_ref[:, cols] = value.astype(BF16)

    project(hidden, w_memory, 2 * D, write_kv)


def self_kernel(rows, triple, g_query, w_out, w_query, first_ref, query_ref, hidden, mixed):
    attention(triple, 0, triple, D, triple, 2 * D, mixed)

    def add_first(n, cols, value):
        first_ref[:, cols] = rows[:, cols] + value

    project(mixed, w_out, D, add_first)
    norm_into(first_ref, g_query, hidden)

    def write_query(n, cols, value):
        query_ref[:, cols] = (value * 0.125).astype(BF16)

    project(hidden, w_query, D, write_query)


def cross_kernel(first, query, key_value, g_mlp, w_out, second_ref, mlp_ref, mixed):
    attention(query, 0, key_value, 0, key_value, D, mixed)

    def add_second(n, cols, value):
        second_ref[:, cols] = first[:, cols] + value

    project(mixed, w_out, D, add_second)
    norm_into(second_ref, g_mlp, mlp_ref)


def gelu(value):
    return value * (1.0 + lax.erf(value * 0.7071067811865476)) * 0.5


def hidden_units(mlp_in, fc, pre, total):
    steps = fc.shape[1] // CHUNK

    def before(c):
        rows = pl.ds(pl.multiple_of(c * CHUNK, CHUNK), CHUNK)
        return lax.dot_general(
            mlp_in[...], fc[0, rows, :], (((1,), (1,)), ((), ())), preferred_element_type=F32
        )

    def after(c, active):
        rows = pl.ds(pl.multiple_of(c * CHUNK, CHUNK), CHUNK)
        total[...] = total[...] + jnp.dot(active, fc[1, rows, :], preferred_element_type=F32)

    pre[0] = before(0)

    def step(c, carry):
        now = lax.rem(c, 2)
        active = gelu(pre[now]).astype(BF16)
        pre[1 - now] = before(c + 1)
        after(c, active)
        return carry

    lax.fori_loop(0, steps - 1, step, 0)
    after(steps - 1, gelu(pre[(steps - 1) % 2]).astype(BF16))


def early_kernel(second, mlp_in, fc, total, pre):
    total[...] = second[...]
    hidden_units(mlp_in, fc, pre, total)


def late_kernel(place, early, mlp_in, fc, g_head, w_head, keep_ref, send_ref, pre, total, hidden):
    total[...] = early[...]
    hidden_units(mlp_in, fc, pre, total)
    norm_into(total, g_head, hidden)
    first = place[1] == 0
    for slot in range(SLOTS):
        rows = slice(slot * ROWS, (slot + 1) * ROWS)
        terms = []
        for half in range(2):
            raw = jnp.dot(
                hidden[rows, :], w_head[:, half * 512 : (half + 1) * 512],
                preferred_element_type=F32,
            )
            conf = 1.0 + jnp.exp(raw[:, 384:])
            terms.append([conf * raw[:, c * 128 : (c + 1) * 128] for c in range(3)] + [conf])
        for c in range(4):
            cols = slice(c * 128, (c + 1) * 128)
            low, high = terms[0][c][:TOKI], terms[1][c][:TOKI]
            keep_ref[slot, :, cols] = jnp.where(first, low, high)
            send_ref[slot, :, cols] = jnp.where(first, high, low).astype(BF16)


def window_kernel(
    image_slot, slot_images, slot_count, place, keep, got, out0, out1, out2, out3
):
    outs = [out0, out1, out2, out3]
    chosen = []
    for slot in range(SLOTS):
        live = slot < slot_count[0]
        for which in range(2):
            index = window_place(image_slot, slot_images, place, slot, which)
            chosen.append((slot, which, jnp.where(live, index, -1)))
    for w in range(WINDOW):
        for c in range(4):
            cols = slice(c * 128, (c + 1) * 128)
            acc = jnp.zeros((TOKI, 128), F32)
            for slot in range(SLOTS):
                own = jnp.where(place[1] == 0, chosen[2 * slot][2], chosen[2 * slot + 1][2])
                far = jnp.where(place[1] == 0, chosen[2 * slot + 1][2], chosen[2 * slot][2])
                acc = acc + jnp.where(own == w, keep[slot, :, cols], 0.0)
                acc = acc + jnp.where(far == w, got[slot, :, cols].astype(F32), 0.0)
            outs[w][:, cols] = acc.astype(outs[w].dtype)


def merge_kernel(base, nearest, further, out):
    def total(cols):
        return base[:, cols] + nearest[:, cols].astype(F32) + further[:, cols].astype(F32)

    weight = jnp.maximum(total(slice(384, 512)), 1.0)
    for c in range(3):
        cols = slice(c * 128, (c + 1) * 128)
        out[0, :, cols] = (total(cols) / weight).astype(BF16)


def pack_kernel(
    features, w_in, w_out, packed, shard, features_here, w_in_here, w_out_here, sems
):
    copies = [
        pltpu.make_async_copy(src, dst, sems.at[i])
        for i, (src, dst) in enumerate(
            ((features, features_here), (w_in, w_in_here), (w_out, w_out_here))
        )
    ]
    for copy in copies:
        copy.start()
    for copy in copies:
        copy.wait()
    count = TOKI - TOP
    packed[88:TOP, HALF:] = jnp.zeros((TOP - 88, HALF), BF16)
    packed[:TOP, :HALF] = features_here[0, :TOP]
    packed[:count, HALF:] = features_here[0, TOP:]
    for target, base in ((packed, TOP), (shard, 0)):
        target[base : base + 24] = w_in_here[0]
        target[base + 24 : base + 48] = w_out_here[0]


SMEM = pl.BlockSpec(memory_space=pltpu.SMEM)
VMEM = pl.BlockSpec(memory_space=pltpu.VMEM)


def call(kernel, scalars, arrays, outs, scratch, flops, name):
    return pl.pallas_call(
        kernel,
        in_specs=[SMEM] * len(scalars) + [VMEM] * len(arrays),
        out_specs=[VMEM] * len(outs),
        out_shape=[jax.ShapeDtypeStruct(s, d) for s, d in outs],
        scratch_shapes=[pltpu.VMEM(s, d) for s, d in scratch],
        compiler_params=pltpu.CompilerParams(vmem_limit_bytes=20 << 20),
        cost_estimate=pl.CostEstimate(flops=flops, transcendentals=0, bytes_accessed=8 << 20),
        name=name,
    )(*scalars, *arrays)


def triple_call(scalars, mine, theirs, g_self, w_qkv):
    return call(
        triple_kernel, scalars, [mine, theirs, g_self, w_qkv],
        [((ALL, D), F32), ((ALL, 3 * D), BF16)], [((ALL, D), BF16)],
        4 * 10**9, "triple_part",
    )


def memory_call(scalars, mine, theirs, g_memory, w_memory):
    return call(
        memory_kernel, scalars, [mine, theirs, g_memory, w_memory],
        [((ALL, 2 * D), BF16)], [((ALL, D), F32), ((ALL, D), BF16)],
        3 * 10**9, "memory_part",
    )[0]


def self_call(rows, triple, g_query, w_out, w_query):
    return call(
        self_kernel, [], [rows, triple, g_query, w_out, w_query],
        [((ALL, D), F32), ((ALL, D), BF16)], [((ALL, D), BF16), ((ALL, D), BF16)],
        12 * 10**9, "self_part",
    )


def cross_call(first, query, key_value, g_mlp, w_out):
    return call(
        cross_kernel, [], [first, query, key_value, g_mlp, w_out],
        [((ALL, D), F32), ((ALL, D), BF16)], [((ALL, D), BF16)],
        12 * 10**9, "cross_part",
    )


def early_call(second, mlp_in, fc):
    return call(
        early_kernel, [], [second, mlp_in, fc],
        [((ALL, D), F32)], [((2, ALL, CHUNK), F32)], 10 * 10**9, "early_part",
    )[0]


def late_call(place, early, mlp_in, fc, g_head, w_head):
    return call(
        late_kernel, [place], [early, mlp_in, fc, g_head, w_head],
        [((SLOTS, TOKI, 512), F32), ((SLOTS, TOKI, 512), BF16)],
        [((2, ALL, CHUNK), F32), ((ALL, D), F32), ((ALL, D), BF16)],
        5 * 10**9, "late_part",
    )


def window_call(scalars, keep, got):
    return call(
        window_kernel, scalars, [keep, got],
        [((TOKI, 512), F32)] + [((TOKI, 512), BF16)] * 3, [], 10**8, "window_part",
    )


def pack_call(features, w_in, w_out):
    outs = [((TOP + 48, D), BF16), ((48, D), BF16)]
    return pl.pallas_call(
        pack_kernel,
        in_specs=[pl.BlockSpec(memory_space=pltpu.MemorySpace.HBM)] * 3,
        out_specs=[VMEM] * 2,
        out_shape=[jax.ShapeDtypeStruct(s, d) for s, d in outs],
        scratch_shapes=[
            pltpu.VMEM((1, TOKI, HALF), BF16),
            pltpu.VMEM((1, 24, D), BF16),
            pltpu.VMEM((1, 24, D), BF16),
            pltpu.SemaphoreType.DMA((3,)),
        ],
        name="pack_part",
    )(features, w_in, w_out)


def merge_call(*arrays):
    return call(merge_kernel, [], arrays, [((1, TOKI, HALF), BF16)], [], 10**8, "merge_part")[0]


def along(array, axis, by):
    count = lax.axis_size("pairs")
    stride, size = {"y": (32, 4), "x": (8, 4), "z": (1, 8)}[axis]

    def target(p):
        here = p // stride % size
        return p + ((here + by) % size - here) * stride

    return lax.ppermute(array, "pairs", [(p, target(p)) for p in range(count)])


def tied(*arrays):
    return lax.optimization_barrier(arrays)


def hidden_rows(shards):
    inner = [s[-48:-24] for s in shards]
    outer = [s[-24:] for s in shards]
    return jnp.stack([jnp.concatenate(inner, axis=0), jnp.concatenate(outer, axis=0)])


def three_hops(block, axis):
    return [along(block, axis, by) for by in (1, -1, 2)]


def first_hop(block, axis):
    return along(block, axis, 1), along(block, axis, -1)


def second_hop(left, right, axis):
    half = left.shape[1] // 2
    return along(left[:, :half], axis, 1), along(right[:, half:], axis, -1)


def on_device(
    features,
    image_slot,
    slot_images,
    slot_count,
    gain_self,
    gain_query,
    gain_memory,
    gain_mlp,
    gain_head,
    w_qkv,
    w_self_out,
    w_query,
    w_memory,
    w_cross_out,
    w_fc1,
    w_fc2,
    w_head,
):
    place = jnp.stack([lax.axis_index("pairs"), lax.axis_index("side")]).astype(jnp.int32)
    packed, shard = pack_call(features, w_fc1, w_fc2)
    next3, next2, next1 = [shifted(packed, -by) for by in (3, 2, 1)]
    last1, last2 = shifted(shard, 1), shifted(shard, 2)
    last34 = shifted(jnp.concatenate([last1, last2], axis=0), 2)
    next1, next2, next3, last34 = tied(next1, next2, next3, last34)
    part_x = hidden_rows([shard, next1, next2, last1])
    part_y = hidden_rows([last2, next3, last34[:48], last34[48:]])
    mine = jnp.stack([packed[:TOP], next1[:TOP], next2[:TOP], next3[:TOP]])
    theirs = other_core(mine)
    scalars = [image_slot, slot_images.reshape(-1), place]
    near_x, near_y = three_hops(part_x, "x"), list(first_hop(part_y, "y"))
    rows, triple = triple_call(scalars, mine, theirs, gain_self, w_qkv[0])
    triple, later = tied(triple, part_y)
    near_y.append(along(later, "y", 2))
    key_value = memory_call(scalars, mine, theirs, gain_memory, w_memory[0])
    near_x, near_y, rows, triple, key_value = tied(near_x, near_y, rows, triple, key_value)
    plane_x = jnp.concatenate([part_x, *near_x], axis=1)
    plane_y = jnp.concatenate([part_y, *near_y], axis=1)
    near_x, near_y = first_hop(plane_x, "y"), first_hop(plane_y, "x")
    first, query = self_call(rows, triple, gain_query, w_self_out[0], w_query[0])
    second, mlp_in = cross_call(first, query, key_value, gain_mlp, w_cross_out[0])
    near_x, near_y, second, mlp_in = tied(near_x, near_y, second, mlp_in)
    far_x, far_y = second_hop(*near_x, "y"), second_hop(*near_y, "x")
    fc_early = jnp.concatenate([plane_x, *near_x, plane_y, *near_y], axis=1)
    early = early_call(second, mlp_in, fc_early)
    fc_late = jnp.concatenate([*far_x, *far_y], axis=1)
    keep, send = late_call(place, early, mlp_in, fc_late, gain_head, w_head[0])
    got = other_core(send)
    pieces = window_call([image_slot, slot_images.reshape(-1), slot_count, place], keep, got)
    third, nearest = tied(shifted(pieces[3], 1), pieces[1])
    further = shifted((pieces[2].astype(F32) + third.astype(F32)).astype(BF16), 2)
    nearest = shifted(nearest, 1)
    return merge_call(pieces[0], nearest, further)


def solution(mesh):
    placed = (
        P("pairs", None, "side"),
        P(),
        P("pairs", None),
        P("pairs"),
        P("side", None),
        P("side", None),
        P("side", None),
        P("side", None),
        P("side", None),
        P("side", None, None),
        P("side", None, None),
        P("side", None, None),
        P("side", None, None),
        P("side", None, None),
        P("side", "pairs", None),
        P("side", "pairs", None),
        P("side", None, None),
    )
    return jax.shard_map(
        on_device, mesh=mesh, in_specs=placed, out_specs=P("pairs", None, "side"), check_vma=False
    )
```

```python
import jax
import jax.numpy as jnp
from jax import lax
from jax.experimental import pallas as pl
from jax.experimental.pallas import tpu as pltpu
from jax.sharding import PartitionSpec as P

D = 768
HEAD_DIM = 64
TOKI = 196
ROWS = 208
HALF = 384
TOP = 104
WINDOW = 4
SLOTS = 3
ALL = SLOTS * ROWS
CHUNK = 256
F32 = jnp.float32
BF16 = jnp.bfloat16


def shifted(array, by):
    count = lax.axis_size("pairs")
    return lax.ppermute(array, "pairs", [(i, (i + by) % count) for i in range(count)])


def other_core(array):
    return lax.ppermute(array, "side", [(0, 1), (1, 0)])


def layer_norm(values, gain):
    center = values - jnp.mean(values, axis=-1, keepdims=True)
    spread = jnp.mean(center * center, axis=-1, keepdims=True)
    return center * lax.rsqrt(spread + 1e-06) * gain


def window_place(image_slot, slot_images, place, slot, which):
    stored = image_slot[slot_images[2 * slot + which]]
    return lax.rem(stored - place[0] + 128, 128)


def padded_rows(image_slot, slot_images, place, mine, theirs, swap, target):
    which = place[1] if not swap else 1 - place[1]
    first = place[1] == 0
    for slot in range(SLOTS):
        index = window_place(image_slot, slot_images, place, slot, which)
        own, far = mine[index].astype(F32), theirs[index].astype(F32)
        base = slot * ROWS
        target[base + 192 : base + ROWS, :] = jnp.zeros((ROWS - 192, D), F32)
        for part, count in ((0, TOP), (1, TOKI - TOP)):
            rows = slice(base + part * TOP, base + part * TOP + count)
            cols = slice(part * HALF, (part + 1) * HALF)
            target[rows, :HALF] = jnp.where(first, own[:count, cols], far[:count, cols])
            target[rows, HALF:] = jnp.where(first, far[:count, cols], own[:count, cols])


def norm_into(source, gain, target):
    for slot in range(SLOTS):
        rows = slice(slot * ROWS, (slot + 1) * ROWS)
        target[rows, :] = layer_norm(source[rows, :], gain[...]).astype(BF16)


def attention(q_ref, q_base, k_ref, k_base, v_ref, v_base, out_ref):
    lane = lax.broadcasted_iota(jnp.int32, (ROWS, 128), 1)
    low_lanes = lane < HEAD_DIM
    key_ok = lax.broadcasted_iota(jnp.int32, (ROWS, ROWS), 1) < TOKI

    def step(t, carry):
        slot = t // 3
        group = t - 3 * slot
        rows = pl.ds(pl.multiple_of(slot * ROWS, ROWS), ROWS)
        for pair in range(2):
            col = group * 256 + pair * 128
            q = q_ref[rows, pl.ds(pl.multiple_of(q_base + col, 128), 128)]
            k = k_ref[rows, pl.ds(pl.multiple_of(k_base + col, 128), 128)]
            v = v_ref[rows, pl.ds(pl.multiple_of(v_base + col, 128), 128)]
            outs = []
            for head in range(2):
                own = low_lanes if head == 0 else jnp.logical_not(low_lanes)
                scores = lax.dot_general(
                    jnp.where(own, q, jnp.zeros_like(q)),
                    k,
                    (((1,), (1,)), ((), ())),
                    preferred_element_type=F32,
                )
                expon = jnp.where(key_ok, jnp.exp(scores), 0.0)
                total = jnp.sum(expon, axis=-1, keepdims=True)
                weights = (expon * (1.0 / total)).astype(BF16)
                outs.append(jnp.dot(weights, v, preferred_element_type=F32))
            out_ref[rows, pl.ds(pl.multiple_of(col, 128), 128)] = jnp.where(
                low_lanes, outs[0], outs[1]
            ).astype(BF16)
        return carry

    lax.fori_loop(0, 3 * SLOTS, step, 0)


def project(source, weight, width, write):
    def step(n, carry):
        cols = pl.ds(pl.multiple_of(n * 256, 256), 256)
        write(n, cols, jnp.dot(source[...], weight[:, cols], preferred_element_type=F32))
        return carry

    lax.fori_loop(0, width // 256, step, 0)


def triple_kernel(
    image_slot, slot_images, place, mine, theirs, g_self, w_qkv, rows_ref, triple_ref, hidden
):
    padded_rows(image_slot, slot_images, place, mine, theirs, False, rows_ref)
    norm_into(rows_ref, g_self, hidden)

    def write_triple(n, cols, value):
        triple_ref[:, cols] = (value * jnp.where(n < 3, 0.125, 1.0)).astype(BF16)

    project(hidden, w_qkv, 3 * D, write_triple)


def memory_kernel(
    image_slot, slot_images, place, mine, theirs, g_memory, w_memory, kv_ref, rows, hidden
):
    padded_rows(image_slot, slot_images, place, mine, theirs, True, rows)
    norm_into(rows, g_memory, hidden)

    def write_kv(n, cols, value):
        kv_ref[:, cols] = value.astype(BF16)

    project(hidden, w_memory, 2 * D, write_kv)


def self_kernel(rows, triple, g_query, w_out, w_query, first_ref, query_ref, hidden, mixed):
    attention(triple, 0, triple, D, triple, 2 * D, mixed)

    def add_first(n, cols, value):
        first_ref[:, cols] = rows[:, cols] + value

    project(mixed, w_out, D, add_first)
    norm_into(first_ref, g_query, hidden)

    def write_query(n, cols, value):
        query_ref[:, cols] = (value * 0.125).astype(BF16)

    project(hidden, w_query, D, write_query)


def cross_kernel(first, query, key_value, g_mlp, w_out, second_ref, mlp_ref, mixed):
    attention(query, 0, key_value, 0, key_value, D, mixed)

    def add_second(n, cols, value):
        second_ref[:, cols] = first[:, cols] + value

    project(mixed, w_out, D, add_second)
    norm_into(second_ref, g_mlp, mlp_ref)


def gelu(value):
    return value * (1.0 + lax.erf(value * 0.7071067811865476)) * 0.5


def hidden_units(mlp_in, fc, pre, total):
    steps = fc.shape[1] // CHUNK

    def before(c):
        rows = pl.ds(pl.multiple_of(c * CHUNK, CHUNK), CHUNK)
        return lax.dot_general(
            mlp_in[...], fc[0, rows, :], (((1,), (1,)), ((), ())), preferred_element_type=F32
        )

    def after(c, active):
        rows = pl.ds(pl.multiple_of(c * CHUNK, CHUNK), CHUNK)
        total[...] = total[...] + jnp.dot(active, fc[1, rows, :], preferred_element_type=F32)

    pre[0] = before(0)

    def step(c, carry):
        now = lax.rem(c, 2)
        active = gelu(pre[now]).astype(BF16)
        pre[1 - now] = before(c + 1)
        after(c, active)
        return carry

    lax.fori_loop(0, steps - 1, step, 0)
    after(steps - 1, gelu(pre[(steps - 1) % 2]).astype(BF16))


def early_kernel(second, mlp_in, fc, total, pre):
    total[...] = second[...]
    hidden_units(mlp_in, fc, pre, total)


def late_kernel(place, early, mlp_in, fc, g_head, w_head, keep_ref, send_ref, pre, total, hidden):
    total[...] = early[...]
    hidden_units(mlp_in, fc, pre, total)
    norm_into(total, g_head, hidden)
    first = place[1] == 0
    for slot in range(SLOTS):
        rows = slice(slot * ROWS, (slot + 1) * ROWS)
        terms = []
        for half in range(2):
            raw = jnp.dot(
                hidden[rows, :], w_head[:, half * 512 : (half + 1) * 512],
                preferred_element_type=F32,
            )
            conf = 1.0 + jnp.exp(raw[:, 384:])
            terms.append([conf * raw[:, c * 128 : (c + 1) * 128] for c in range(3)] + [conf])
        for c in range(4):
            cols = slice(c * 128, (c + 1) * 128)
            low, high = terms[0][c][:TOKI], terms[1][c][:TOKI]
            keep_ref[slot, :, cols] = jnp.where(first, low, high)
            send_ref[slot, :, cols] = jnp.where(first, high, low).astype(BF16)


def window_kernel(
    image_slot, slot_images, slot_count, place, keep, got, out0, out1, out2, out3
):
    outs = [out0, out1, out2, out3]
    chosen = []
    for slot in range(SLOTS):
        live = slot < slot_count[0]
        for which in range(2):
            index = window_place(image_slot, slot_images, place, slot, which)
            chosen.append((slot, which, jnp.where(live, index, -1)))
    for w in range(WINDOW):
        for c in range(4):
            cols = slice(c * 128, (c + 1) * 128)
            acc = jnp.zeros((TOKI, 128), F32)
            for slot in range(SLOTS):
                own = jnp.where(place[1] == 0, chosen[2 * slot][2], chosen[2 * slot + 1][2])
                far = jnp.where(place[1] == 0, chosen[2 * slot + 1][2], chosen[2 * slot][2])
                acc = acc + jnp.where(own == w, keep[slot, :, cols], 0.0)
                acc = acc + jnp.where(far == w, got[slot, :, cols].astype(F32), 0.0)
            outs[w][:, cols] = acc.astype(outs[w].dtype)


def merge_kernel(base, nearest, further, out):
    def total(cols):
        return base[:, cols] + nearest[:, cols].astype(F32) + further[:, cols].astype(F32)

    weight = jnp.maximum(total(slice(384, 512)), 1.0)
    for c in range(3):
        cols = slice(c * 128, (c + 1) * 128)
        out[0, :, cols] = (total(cols) / weight).astype(BF16)


def pack_kernel(
    features, w_in, w_out, tokens, shard, features_here, w_in_here, w_out_here, sems
):
    copies = [
        pltpu.make_async_copy(src, dst, sems.at[i])
        for i, (src, dst) in enumerate(
            ((features, features_here), (w_in, w_in_here), (w_out, w_out_here))
        )
    ]
    for copy in copies:
        copy.start()
    for copy in copies:
        copy.wait()
    count = TOKI - TOP
    tokens[88:TOP, HALF:] = jnp.zeros((TOP - 88, HALF), BF16)
    tokens[:TOP, :HALF] = features_here[0, :TOP]
    tokens[:count, HALF:] = features_here[0, TOP:]
    shard[:24] = w_in_here[0]
    shard[24:] = w_out_here[0]


SMEM = pl.BlockSpec(memory_space=pltpu.SMEM)
VMEM = pl.BlockSpec(memory_space=pltpu.VMEM)


def call(kernel, scalars, arrays, outs, scratch, flops, name):
    return pl.pallas_call(
        kernel,
        in_specs=[SMEM] * len(scalars) + [VMEM] * len(arrays),
        out_specs=[VMEM] * len(outs),
        out_shape=[jax.ShapeDtypeStruct(s, d) for s, d in outs],
        scratch_shapes=[pltpu.VMEM(s, d) for s, d in scratch],
        compiler_params=pltpu.CompilerParams(vmem_limit_bytes=20 << 20),
        cost_estimate=pl.CostEstimate(flops=flops, transcendentals=0, bytes_accessed=8 << 20),
        name=name,
    )(*scalars, *arrays)


def triple_call(scalars, mine, theirs, g_self, w_qkv):
    return call(
        triple_kernel, scalars, [mine, theirs, g_self, w_qkv],
        [((ALL, D), F32), ((ALL, 3 * D), BF16)], [((ALL, D), BF16)],
        4 * 10**9, "triple_part",
    )


def memory_call(scalars, mine, theirs, g_memory, w_memory):
    return call(
        memory_kernel, scalars, [mine, theirs, g_memory, w_memory],
        [((ALL, 2 * D), BF16)], [((ALL, D), F32), ((ALL, D), BF16)],
        3 * 10**9, "memory_part",
    )[0]


def self_call(rows, triple, g_query, w_out, w_query):
    return call(
        self_kernel, [], [rows, triple, g_query, w_out, w_query],
        [((ALL, D), F32), ((ALL, D), BF16)], [((ALL, D), BF16), ((ALL, D), BF16)],
        12 * 10**9, "self_part",
    )


def cross_call(first, query, key_value, g_mlp, w_out):
    return call(
        cross_kernel, [], [first, query, key_value, g_mlp, w_out],
        [((ALL, D), F32), ((ALL, D), BF16)], [((ALL, D), BF16)],
        12 * 10**9, "cross_part",
    )


def early_call(second, mlp_in, fc):
    return call(
        early_kernel, [], [second, mlp_in, fc],
        [((ALL, D), F32)], [((2, ALL, CHUNK), F32)], 10 * 10**9, "early_part",
    )[0]


def late_call(place, early, mlp_in, fc, g_head, w_head):
    return call(
        late_kernel, [place], [early, mlp_in, fc, g_head, w_head],
        [((SLOTS, TOKI, 512), F32), ((SLOTS, TOKI, 512), BF16)],
        [((2, ALL, CHUNK), F32), ((ALL, D), F32), ((ALL, D), BF16)],
        5 * 10**9, "late_part",
    )


def window_call(scalars, keep, got):
    return call(
        window_kernel, scalars, [keep, got],
        [((TOKI, 512), F32)] + [((TOKI, 512), BF16)] * 3, [], 10**8, "window_part",
    )


def pack_call(features, w_in, w_out):
    outs = [((TOP, D), BF16), ((48, D), BF16)]
    return pl.pallas_call(
        pack_kernel,
        in_specs=[pl.BlockSpec(memory_space=pltpu.MemorySpace.HBM)] * 3,
        out_specs=[VMEM] * 2,
        out_shape=[jax.ShapeDtypeStruct(s, d) for s, d in outs],
        scratch_shapes=[
            pltpu.VMEM((1, TOKI, HALF), BF16),
            pltpu.VMEM((1, 24, D), BF16),
            pltpu.VMEM((1, 24, D), BF16),
            pltpu.SemaphoreType.DMA((3,)),
        ],
        name="pack_part",
    )(features, w_in, w_out)


def merge_call(*arrays):
    return call(merge_kernel, [], arrays, [((1, TOKI, HALF), BF16)], [], 10**8, "merge_part")[0]


def along(array, axis, by):
    count = lax.axis_size("pairs")
    stride, size = {"y": (32, 4), "x": (8, 4), "z": (1, 8)}[axis]

    def target(p):
        here = p // stride % size
        return p + ((here + by) % size - here) * stride

    return lax.ppermute(array, "pairs", [(p, target(p)) for p in range(count)])


def tied(*arrays):
    return lax.optimization_barrier(arrays)


def hidden_rows(shards):
    inner = [s[-48:-24] for s in shards]
    outer = [s[-24:] for s in shards]
    return jnp.stack([jnp.concatenate(inner, axis=0), jnp.concatenate(outer, axis=0)])


def first_hop(block, axis):
    return along(block, axis, 1), along(block, axis, -1)


def second_hop(left, right, axis):
    half = left.shape[1] // 2
    return along(left[:, :half], axis, 1), along(right[:, half:], axis, -1)


def on_device(
    features,
    image_slot,
    slot_images,
    slot_count,
    gain_self,
    gain_query,
    gain_memory,
    gain_mlp,
    gain_head,
    w_qkv,
    w_self_out,
    w_query,
    w_memory,
    w_cross_out,
    w_fc1,
    w_fc2,
    w_head,
):
    place = jnp.stack([lax.axis_index("pairs"), lax.axis_index("side")]).astype(jnp.int32)
    tokens, shard = pack_call(features, w_fc1, w_fc2)
    last1, last2, below1, below2 = [shifted(shard, by) for by in (1, 2, -1, -2)]
    next2 = shifted(tokens, -2)
    last1, last2, below1, below2, tokens = tied(last1, last2, below1, below2, tokens)
    last34 = shifted(jnp.concatenate([last1, last2], axis=0), 2)
    below3 = shifted(below2, -1)
    next1 = shifted(tokens, -1)
    part_x = hidden_rows([shard, last1, below1, below2])
    last34, below3, next1, next2, part_x = tied(last34, below3, next1, next2, part_x)
    next3 = shifted(next2, -1)
    part_y = hidden_rows([last2, below3, last34[:48], last34[48:]])
    near_x, near_y = first_hop(part_x, "x"), first_hop(part_y, "y")
    next3, near_x, near_y, part_x, part_y = tied(next3, near_x, near_y, part_x, part_y)
    near_x = [*near_x, along(part_x, "x", 2)]
    near_y = [*near_y, along(part_y, "y", 2)]
    mine = jnp.stack([tokens, next1, next2, next3])
    theirs = other_core(mine)
    scalars = [image_slot, slot_images.reshape(-1), place]
    rows, triple = triple_call(scalars, mine, theirs, gain_self, w_qkv[0])
    key_value = memory_call(scalars, mine, theirs, gain_memory, w_memory[0])
    near_x, near_y, rows, triple, key_value = tied(near_x, near_y, rows, triple, key_value)
    plane_x = jnp.concatenate([part_x, *near_x], axis=1)
    plane_y = jnp.concatenate([part_y, *near_y], axis=1)
    near_x, near_y = first_hop(plane_x, "y"), first_hop(plane_y, "x")
    first, query = self_call(rows, triple, gain_query, w_self_out[0], w_query[0])
    second, mlp_in = cross_call(first, query, key_value, gain_mlp, w_cross_out[0])
    near_x, near_y, second, mlp_in = tied(near_x, near_y, second, mlp_in)
    far_x, far_y = second_hop(*near_x, "y"), second_hop(*near_y, "x")
    fc_early = jnp.concatenate([plane_x, *near_x, plane_y, *near_y], axis=1)
    early = early_call(second, mlp_in, fc_early)
    fc_late = jnp.concatenate([*far_x, *far_y], axis=1)
    keep, send = late_call(place, early, mlp_in, fc_late, gain_head, w_head[0])
    got = other_core(send)
    pieces = window_call([image_slot, slot_images.reshape(-1), slot_count, place], keep, got)
    third, nearest = tied(shifted(pieces[3], 1), pieces[1])
    further = shifted((pieces[2].astype(F32) + third.astype(F32)).astype(BF16), 2)
    nearest = shifted(nearest, 1)
    return merge_call(pieces[0], nearest, further)


def solution(mesh):
    placed = (
        P("pairs", None, "side"),
        P(),
        P("pairs", None),
        P("pairs"),
        P("side", None),
        P("side", None),
        P("side", None),
        P("side", None),
        P("side", None),
        P("side", None, None),
        P("side", None, None),
        P("side", None, None),
        P("side", None, None),
        P("side", None, None),
        P("side", "pairs", None),
        P("side", "pairs", None),
        P("side", None, None),
    )
    return jax.shard_map(
        on_device, mesh=mesh, in_specs=placed, out_specs=P("pairs", None, "side"), check_vma=False
    )
```

```python
import functools

import jax
import jax.numpy as jnp
from jax import lax
from jax.experimental import pallas as pl
from jax.experimental.pallas import tpu as pltpu
from jax.sharding import PartitionSpec as P

D = 768
HEAD_DIM = 64
TOKI = 196
ROWS = 208
HALF = 384
TOP = 104
WINDOW = 4
SLOTS = 3
ALL = SLOTS * ROWS
CHUNK = 256
F32 = jnp.float32
BF16 = jnp.bfloat16


def shifted(array, by):
    count = lax.axis_size("pairs")
    return lax.ppermute(array, "pairs", [(i, (i + by) % count) for i in range(count)])


def other_core(array):
    return lax.ppermute(array, "side", [(0, 1), (1, 0)])


def layer_norm(values, gain):
    center = values - jnp.mean(values, axis=-1, keepdims=True)
    spread = jnp.mean(center * center, axis=-1, keepdims=True)
    return center * lax.rsqrt(spread + 1e-06) * gain


def window_place(image_slot, slot_images, place, slot, which):
    stored = image_slot[slot_images[2 * slot + which]]
    return lax.rem(stored - place[0] + 128, 128)


def padded_rows(image_slot, slot_images, place, mine, theirs, swap, target):
    which = place[1] if not swap else 1 - place[1]
    first = place[1] == 0
    for slot in range(SLOTS):
        index = window_place(image_slot, slot_images, place, slot, which)
        own, far = mine[index].astype(F32), theirs[index].astype(F32)
        base = slot * ROWS
        target[base + 192 : base + ROWS, :] = jnp.zeros((ROWS - 192, D), F32)
        for part, count in ((0, TOP), (1, TOKI - TOP)):
            rows = slice(base + part * TOP, base + part * TOP + count)
            cols = slice(part * HALF, (part + 1) * HALF)
            target[rows, :HALF] = jnp.where(first, own[:count, cols], far[:count, cols])
            target[rows, HALF:] = jnp.where(first, far[:count, cols], own[:count, cols])


def norm_into(source, gain, target):
    for slot in range(SLOTS):
        rows = slice(slot * ROWS, (slot + 1) * ROWS)
        target[rows, :] = layer_norm(source[rows, :], gain[...]).astype(BF16)


def attention(q_ref, q_base, k_ref, k_base, v_ref, v_base, out_ref):
    lane = lax.broadcasted_iota(jnp.int32, (ROWS, 128), 1)
    low_lanes = lane < HEAD_DIM
    key_ok = lax.broadcasted_iota(jnp.int32, (ROWS, ROWS), 1) < TOKI

    def step(t, carry):
        slot = t // 3
        group = t - 3 * slot
        rows = pl.ds(pl.multiple_of(slot * ROWS, ROWS), ROWS)
        for pair in range(2):
            col = group * 256 + pair * 128
            q = q_ref[rows, pl.ds(pl.multiple_of(q_base + col, 128), 128)]
            k = k_ref[rows, pl.ds(pl.multiple_of(k_base + col, 128), 128)]
            v = v_ref[rows, pl.ds(pl.multiple_of(v_base + col, 128), 128)]
            outs = []
            for head in range(2):
                own = low_lanes if head == 0 else jnp.logical_not(low_lanes)
                scores = lax.dot_general(
                    jnp.where(own, q, jnp.zeros_like(q)),
                    k,
                    (((1,), (1,)), ((), ())),
                    preferred_element_type=F32,
                )
                expon = jnp.where(key_ok, jnp.exp(scores), 0.0)
                total = jnp.sum(expon, axis=-1, keepdims=True)
                weights = (expon * (1.0 / total)).astype(BF16)
                outs.append(jnp.dot(weights, v, preferred_element_type=F32))
            out_ref[rows, pl.ds(pl.multiple_of(col, 128), 128)] = jnp.where(
                low_lanes, outs[0], outs[1]
            ).astype(BF16)
        return carry

    lax.fori_loop(0, 3 * SLOTS, step, 0)


def project(source, weight, width, write):
    def step(n, carry):
        cols = pl.ds(pl.multiple_of(n * 256, 256), 256)
        write(n, cols, jnp.dot(source[...], weight[:, cols], preferred_element_type=F32))
        return carry

    lax.fori_loop(0, width // 256, step, 0)


def triple_kernel(
    image_slot, slot_images, place, mine, theirs, g_self, w_qkv, rows_ref, triple_ref, hidden
):
    padded_rows(image_slot, slot_images, place, mine, theirs, False, rows_ref)
    norm_into(rows_ref, g_self, hidden)

    def write_triple(n, cols, value):
        triple_ref[:, cols] = (value * jnp.where(n < 3, 0.125, 1.0)).astype(BF16)

    project(hidden, w_qkv, 3 * D, write_triple)


def memory_kernel(
    image_slot, slot_images, place, mine, theirs, g_memory, w_memory, kv_ref, rows, hidden
):
    padded_rows(image_slot, slot_images, place, mine, theirs, True, rows)
    norm_into(rows, g_memory, hidden)

    def write_kv(n, cols, value):
        kv_ref[:, cols] = value.astype(BF16)

    project(hidden, w_memory, 2 * D, write_kv)


def self_kernel(rows, triple, g_query, w_out, w_query, first_ref, query_ref, hidden, mixed):
    attention(triple, 0, triple, D, triple, 2 * D, mixed)

    def add_first(n, cols, value):
        first_ref[:, cols] = rows[:, cols] + value

    project(mixed, w_out, D, add_first)
    norm_into(first_ref, g_query, hidden)

    def write_query(n, cols, value):
        query_ref[:, cols] = (value * 0.125).astype(BF16)

    project(hidden, w_query, D, write_query)


def cross_kernel(first, query, key_value, g_mlp, w_out, second_ref, mlp_ref, mixed):
    attention(query, 0, key_value, 0, key_value, D, mixed)

    def add_second(n, cols, value):
        second_ref[:, cols] = first[:, cols] + value

    project(mixed, w_out, D, add_second)
    norm_into(second_ref, g_mlp, mlp_ref)


def gelu(value):
    return value * (1.0 + lax.erf(value * 0.7071067811865476)) * 0.5


def hidden_units(mlp_in, fc, pre, total):
    steps = fc.shape[1] // CHUNK

    def before(c):
        rows = pl.ds(pl.multiple_of(c * CHUNK, CHUNK), CHUNK)
        return lax.dot_general(
            mlp_in[...], fc[0, rows, :], (((1,), (1,)), ((), ())), preferred_element_type=F32
        )

    def after(c, active):
        rows = pl.ds(pl.multiple_of(c * CHUNK, CHUNK), CHUNK)
        total[...] = total[...] + jnp.dot(active, fc[1, rows, :], preferred_element_type=F32)

    pre[0] = before(0)

    def step(c, carry):
        now = lax.rem(c, 2)
        active = gelu(pre[now]).astype(BF16)
        pre[1 - now] = before(c + 1)
        after(c, active)
        return carry

    lax.fori_loop(0, steps - 1, step, 0)
    after(steps - 1, gelu(pre[(steps - 1) % 2]).astype(BF16))


def early_kernel(second, mlp_in, fc, total, pre):
    total[...] = second[...]
    hidden_units(mlp_in, fc, pre, total)


def late_kernel(place, early, mlp_in, fc, g_head, w_head, keep_ref, send_ref, pre, total, hidden):
    total[...] = early[...]
    hidden_units(mlp_in, fc, pre, total)
    norm_into(total, g_head, hidden)
    first = place[1] == 0
    for slot in range(SLOTS):
        rows = slice(slot * ROWS, (slot + 1) * ROWS)
        terms = []
        for half in range(2):
            raw = jnp.dot(
                hidden[rows, :], w_head[:, half * 512 : (half + 1) * 512],
                preferred_element_type=F32,
            )
            conf = 1.0 + jnp.exp(raw[:, 384:])
            terms.append([conf * raw[:, c * 128 : (c + 1) * 128] for c in range(3)] + [conf])
        for c in range(4):
            cols = slice(c * 128, (c + 1) * 128)
            low, high = terms[0][c][:TOKI], terms[1][c][:TOKI]
            keep_ref[slot, :, cols] = jnp.where(first, low, high)
            send_ref[slot, :, cols] = jnp.where(first, high, low).astype(BF16)


def window_kernel(windows, image_slot, slot_images, slot_count, place, keep, got, *outs):
    chosen = []
    for slot in range(SLOTS):
        live = slot < slot_count[0]
        for which in range(2):
            index = window_place(image_slot, slot_images, place, slot, which)
            chosen.append(jnp.where(live, index, -1))
    first = place[1] == 0
    for w, out in zip(windows, outs):
        for c in range(4):
            cols = slice(c * 128, (c + 1) * 128)
            acc = jnp.zeros((TOKI, 128), F32)
            for slot in range(SLOTS):
                own = jnp.where(first, chosen[2 * slot], chosen[2 * slot + 1])
                far = jnp.where(first, chosen[2 * slot + 1], chosen[2 * slot])
                acc = acc + jnp.where(own == w, keep[slot, :, cols], 0.0)
                acc = acc + jnp.where(far == w, got[slot, :, cols].astype(F32), 0.0)
            out[:, cols] = acc.astype(out.dtype)


def merge_kernel(base, nearest, further, out):
    def total(cols):
        return base[:, cols] + nearest[:, cols].astype(F32) + further[:, cols].astype(F32)

    weight = jnp.maximum(total(slice(384, 512)), 1.0)
    for c in range(3):
        cols = slice(c * 128, (c + 1) * 128)
        out[0, :, cols] = (total(cols) / weight).astype(BF16)


def pack_kernel(
    features, w_in, w_out, packed, shard, features_here, w_in_here, w_out_here, sems
):
    copies = [
        pltpu.make_async_copy(src, dst, sems.at[i])
        for i, (src, dst) in enumerate(
            ((features, features_here), (w_in, w_in_here), (w_out, w_out_here))
        )
    ]
    for copy in copies:
        copy.start()
    for copy in copies:
        copy.wait()
    count = TOKI - TOP
    packed[88:TOP, HALF:] = jnp.zeros((TOP - 88, HALF), BF16)
    packed[:TOP, :HALF] = features_here[0, :TOP]
    packed[:count, HALF:] = features_here[0, TOP:]
    for target, base in ((packed, TOP), (shard, 0)):
        target[base : base + 24] = w_in_here[0]
        target[base + 24 : base + 48] = w_out_here[0]


SMEM = pl.BlockSpec(memory_space=pltpu.SMEM)
VMEM = pl.BlockSpec(memory_space=pltpu.VMEM)


def call(kernel, scalars, arrays, outs, scratch, flops, name):
    return pl.pallas_call(
        kernel,
        in_specs=[SMEM] * len(scalars) + [VMEM] * len(arrays),
        out_specs=[VMEM] * len(outs),
        out_shape=[jax.ShapeDtypeStruct(s, d) for s, d in outs],
        scratch_shapes=[pltpu.VMEM(s, d) for s, d in scratch],
        compiler_params=pltpu.CompilerParams(vmem_limit_bytes=20 << 20),
        cost_estimate=pl.CostEstimate(flops=flops, transcendentals=0, bytes_accessed=8 << 20),
        name=name,
    )(*scalars, *arrays)


def triple_call(scalars, mine, theirs, g_self, w_qkv):
    return call(
        triple_kernel, scalars, [mine, theirs, g_self, w_qkv],
        [((ALL, D), F32), ((ALL, 3 * D), BF16)], [((ALL, D), BF16)],
        4 * 10**9, "triple_part",
    )


def memory_call(scalars, mine, theirs, g_memory, w_memory):
    return call(
        memory_kernel, scalars, [mine, theirs, g_memory, w_memory],
        [((ALL, 2 * D), BF16)], [((ALL, D), F32), ((ALL, D), BF16)],
        3 * 10**9, "memory_part",
    )[0]


def self_call(rows, triple, g_query, w_out, w_query):
    return call(
        self_kernel, [], [rows, triple, g_query, w_out, w_query],
        [((ALL, D), F32), ((ALL, D), BF16)], [((ALL, D), BF16), ((ALL, D), BF16)],
        12 * 10**9, "self_part",
    )


def cross_call(first, query, key_value, g_mlp, w_out):
    return call(
        cross_kernel, [], [first, query, key_value, g_mlp, w_out],
        [((ALL, D), F32), ((ALL, D), BF16)], [((ALL, D), BF16)],
        12 * 10**9, "cross_part",
    )


def early_call(second, mlp_in, fc):
    return call(
        early_kernel, [], [second, mlp_in, fc],
        [((ALL, D), F32)], [((2, ALL, CHUNK), F32)], 10 * 10**9, "early_part",
    )[0]


def late_call(place, early, mlp_in, fc, g_head, w_head):
    return call(
        late_kernel, [place], [early, mlp_in, fc, g_head, w_head],
        [((SLOTS, TOKI, 512), F32), ((SLOTS, TOKI, 512), BF16)],
        [((2, ALL, CHUNK), F32), ((ALL, D), F32), ((ALL, D), BF16)],
        5 * 10**9, "late_part",
    )


def window_call(windows, scalars, keep, got):
    return call(
        functools.partial(window_kernel, windows), scalars, [keep, got],
        [((TOKI, 512), BF16 if w else F32) for w in windows], [], 10**8,
        "furthest_part" if windows == (3,) else "window_part",
    )


def pack_call(features, w_in, w_out):
    outs = [((TOP + 48, D), BF16), ((48, D), BF16)]
    return pl.pallas_call(
        pack_kernel,
        in_specs=[pl.BlockSpec(memory_space=pltpu.MemorySpace.HBM)] * 3,
        out_specs=[VMEM] * 2,
        out_shape=[jax.ShapeDtypeStruct(s, d) for s, d in outs],
        scratch_shapes=[
            pltpu.VMEM((1, TOKI, HALF), BF16),
            pltpu.VMEM((1, 24, D), BF16),
            pltpu.VMEM((1, 24, D), BF16),
            pltpu.SemaphoreType.DMA((3,)),
        ],
        name="pack_part",
    )(features, w_in, w_out)


def merge_call(*arrays):
    return call(merge_kernel, [], arrays, [((1, TOKI, HALF), BF16)], [], 10**8, "merge_part")[0]


def along(array, axis, by):
    count = lax.axis_size("pairs")
    stride, size = {"y": (32, 4), "x": (8, 4), "z": (1, 8)}[axis]

    def target(p):
        here = p // stride % size
        return p + ((here + by) % size - here) * stride

    return lax.ppermute(array, "pairs", [(p, target(p)) for p in range(count)])


def tied(*arrays):
    return lax.optimization_barrier(arrays)


def hidden_rows(shards):
    inner = [s[-48:-24] for s in shards]
    outer = [s[-24:] for s in shards]
    return jnp.stack([jnp.concatenate(inner, axis=0), jnp.concatenate(outer, axis=0)])


def three_hops(block, axis):
    return [along(block, axis, by) for by in (1, -1, 2)]


def first_hop(block, axis):
    return along(block, axis, 1), along(block, axis, -1)


def second_hop(left, right, axis):
    half = left.shape[1] // 2
    return along(left[:, :half], axis, 1), along(right[:, half:], axis, -1)


def on_device(
    features,
    image_slot,
    slot_images,
    slot_count,
    gain_self,
    gain_query,
    gain_memory,
    gain_mlp,
    gain_head,
    w_qkv,
    w_self_out,
    w_query,
    w_memory,
    w_cross_out,
    w_fc1,
    w_fc2,
    w_head,
):
    place = jnp.stack([lax.axis_index("pairs"), lax.axis_index("side")]).astype(jnp.int32)
    packed, shard = pack_call(features, w_fc1, w_fc2)
    next2, next1 = shifted(packed, -2), shifted(packed, -1)
    last1, last2 = shifted(shard, 1), shifted(shard, 2)
    last34 = shifted(jnp.concatenate([last1, last2], axis=0), 2)
    next3, last34 = tied(shifted(next2, -1), last34)
    part_x = hidden_rows([shard, next1, next2, last1])
    part_y = hidden_rows([last2, next3, last34[:48], last34[48:]])
    mine = jnp.stack([packed[:TOP], next1[:TOP], next2[:TOP], next3[:TOP]])
    theirs = other_core(mine)
    scalars = [image_slot, slot_images.reshape(-1), place]
    near_x, near_y = three_hops(part_x, "x"), list(first_hop(part_y, "y"))
    rows, triple = triple_call(scalars, mine, theirs, gain_self, w_qkv[0])
    triple, later = tied(triple, part_y)
    near_y.append(along(later, "y", 2))
    key_value = memory_call(scalars, mine, theirs, gain_memory, w_memory[0])
    near_x, near_y, rows, triple, key_value = tied(near_x, near_y, rows, triple, key_value)
    plane_x = jnp.concatenate([part_x, *near_x], axis=1)
    plane_y = jnp.concatenate([part_y, *near_y], axis=1)
    near_x, near_y = first_hop(plane_x, "y"), first_hop(plane_y, "x")
    first, query = self_call(rows, triple, gain_query, w_self_out[0], w_query[0])
    second, mlp_in = cross_call(first, query, key_value, gain_mlp, w_cross_out[0])
    near_x, near_y, second, mlp_in = tied(near_x, near_y, second, mlp_in)
    far_x, far_y = second_hop(*near_x, "y"), second_hop(*near_y, "x")
    fc_early = jnp.concatenate([plane_x, *near_x, plane_y, *near_y], axis=1)
    early = early_call(second, mlp_in, fc_early)
    fc_late = jnp.concatenate([*far_x, *far_y], axis=1)
    keep, send = late_call(place, early, mlp_in, fc_late, gain_head, w_head[0])
    got = other_core(send)
    scalars = [image_slot, slot_images.reshape(-1), slot_count, place]
    (furthest,) = window_call((3,), scalars, keep, got)
    third = shifted(furthest, 1)
    base, piece1, piece2 = window_call((0, 1, 2), scalars, keep, got)
    nearest = shifted(piece1, 1)
    further = shifted((piece2.astype(F32) + third.astype(F32)).astype(BF16), 2)
    return merge_call(base, nearest, further)


def solution(mesh):
    placed = (
        P("pairs", None, "side"),
        P(),
        P("pairs", None),
        P("pairs"),
        P("side", None),
        P("side", None),
        P("side", None),
        P("side", None),
        P("side", None),
        P("side", None, None),
        P("side", None, None),
        P("side", None, None),
        P("side", None, None),
        P("side", None, None),
        P("side", "pairs", None),
        P("side", "pairs", None),
        P("side", None, None),
    )
    return jax.shard_map(
        on_device, mesh=mesh, in_specs=placed, out_specs=P("pairs", None, "side"), check_vma=False
    )
```

```python
import functools

import jax
import jax.numpy as jnp
from jax import lax
from jax.experimental import pallas as pl
from jax.experimental.pallas import tpu as pltpu
from jax.sharding import PartitionSpec as P

D = 768
HEAD_DIM = 64
TOKI = 196
ROWS = 208
HALF = 384
TOP = 104
WINDOW = 4
SLOTS = 3
ALL = SLOTS * ROWS
CHUNK = 256
F32 = jnp.float32
BF16 = jnp.bfloat16


def shifted(array, by):
    count = lax.axis_size("pairs")
    return lax.ppermute(array, "pairs", [(i, (i + by) % count) for i in range(count)])


def other_core(array):
    return lax.ppermute(array, "side", [(0, 1), (1, 0)])


def layer_norm(values, gain):
    center = values - jnp.mean(values, axis=-1, keepdims=True)
    spread = jnp.mean(center * center, axis=-1, keepdims=True)
    return center * lax.rsqrt(spread + 1e-06) * gain


def window_place(image_slot, slot_images, place, slot, which):
    stored = image_slot[slot_images[2 * slot + which]]
    return lax.rem(stored - place[0] + 128, 128)


def padded_rows(image_slot, slot_images, place, mine, theirs, swap, target):
    which = place[1] if not swap else 1 - place[1]
    first = place[1] == 0
    for slot in range(SLOTS):
        index = window_place(image_slot, slot_images, place, slot, which)
        own, far = mine[index].astype(F32), theirs[index].astype(F32)
        base = slot * ROWS
        target[base + 192 : base + ROWS, :] = jnp.zeros((ROWS - 192, D), F32)
        for part, count in ((0, TOP), (1, TOKI - TOP)):
            rows = slice(base + part * TOP, base + part * TOP + count)
            cols = slice(part * HALF, (part + 1) * HALF)
            target[rows, :HALF] = jnp.where(first, own[:count, cols], far[:count, cols])
            target[rows, HALF:] = jnp.where(first, far[:count, cols], own[:count, cols])


def norm_into(source, gain, target):
    for slot in range(SLOTS):
        rows = slice(slot * ROWS, (slot + 1) * ROWS)
        target[rows, :] = layer_norm(source[rows, :], gain[...]).astype(BF16)


def attention(q_ref, q_base, k_ref, k_base, v_ref, v_base, out_ref):
    lane = lax.broadcasted_iota(jnp.int32, (ROWS, 128), 1)
    low_lanes = lane < HEAD_DIM
    key_ok = lax.broadcasted_iota(jnp.int32, (ROWS, ROWS), 1) < TOKI

    def step(t, carry):
        slot = t // 3
        group = t - 3 * slot
        rows = pl.ds(pl.multiple_of(slot * ROWS, ROWS), ROWS)
        for pair in range(2):
            col = group * 256 + pair * 128
            q = q_ref[rows, pl.ds(pl.multiple_of(q_base + col, 128), 128)]
            k = k_ref[rows, pl.ds(pl.multiple_of(k_base + col, 128), 128)]
            v = v_ref[rows, pl.ds(pl.multiple_of(v_base + col, 128), 128)]
            outs = []
            for head in range(2):
                own = low_lanes if head == 0 else jnp.logical_not(low_lanes)
                scores = lax.dot_general(
                    jnp.where(own, q, jnp.zeros_like(q)),
                    k,
                    (((1,), (1,)), ((), ())),
                    preferred_element_type=F32,
                )
                expon = jnp.where(key_ok, jnp.exp(scores), 0.0)
                total = jnp.sum(expon, axis=-1, keepdims=True)
                weights = (expon * (1.0 / total)).astype(BF16)
                outs.append(jnp.dot(weights, v, preferred_element_type=F32))
            out_ref[rows, pl.ds(pl.multiple_of(col, 128), 128)] = jnp.where(
                low_lanes, outs[0], outs[1]
            ).astype(BF16)
        return carry

    lax.fori_loop(0, 3 * SLOTS, step, 0)


def project(source, weight, width, write):
    def step(n, carry):
        cols = pl.ds(pl.multiple_of(n * 256, 256), 256)
        write(n, cols, jnp.dot(source[...], weight[:, cols], preferred_element_type=F32))
        return carry

    lax.fori_loop(0, width // 256, step, 0)


def triple_kernel(
    image_slot, slot_images, place, mine, theirs, g_self, w_qkv, rows_ref, triple_ref, hidden
):
    padded_rows(image_slot, slot_images, place, mine, theirs, False, rows_ref)
    norm_into(rows_ref, g_self, hidden)

    def write_triple(n, cols, value):
        triple_ref[:, cols] = (value * jnp.where(n < 3, 0.125, 1.0)).astype(BF16)

    project(hidden, w_qkv, 3 * D, write_triple)


def memory_kernel(
    image_slot, slot_images, place, mine, theirs, g_memory, w_memory, kv_ref, rows, hidden
):
    padded_rows(image_slot, slot_images, place, mine, theirs, True, rows)
    norm_into(rows, g_memory, hidden)

    def write_kv(n, cols, value):
        kv_ref[:, cols] = value.astype(BF16)

    project(hidden, w_memory, 2 * D, write_kv)


def self_kernel(rows, triple, g_query, w_out, w_query, first_ref, query_ref, hidden, mixed):
    attention(triple, 0, triple, D, triple, 2 * D, mixed)

    def add_first(n, cols, value):
        first_ref[:, cols] = rows[:, cols] + value

    project(mixed, w_out, D, add_first)
    norm_into(first_ref, g_query, hidden)

    def write_query(n, cols, value):
        query_ref[:, cols] = (value * 0.125).astype(BF16)

    project(hidden, w_query, D, write_query)


def cross_kernel(first, query, key_value, g_mlp, w_out, second_ref, mlp_ref, mixed):
    attention(query, 0, key_value, 0, key_value, D, mixed)

    def add_second(n, cols, value):
        second_ref[:, cols] = first[:, cols] + value

    project(mixed, w_out, D, add_second)
    norm_into(second_ref, g_mlp, mlp_ref)


def gelu(value):
    return value * (1.0 + lax.erf(value * 0.7071067811865476)) * 0.5


def hidden_units(mlp_in, fc, pre, total):
    steps = fc.shape[1] // CHUNK

    def before(c):
        rows = pl.ds(pl.multiple_of(c * CHUNK, CHUNK), CHUNK)
        return lax.dot_general(
            mlp_in[...], fc[0, rows, :], (((1,), (1,)), ((), ())), preferred_element_type=F32
        )

    def after(c, active):
        rows = pl.ds(pl.multiple_of(c * CHUNK, CHUNK), CHUNK)
        total[...] = total[...] + jnp.dot(active, fc[1, rows, :], preferred_element_type=F32)

    pre[0] = before(0)

    def step(c, carry):
        now = lax.rem(c, 2)
        active = gelu(pre[now]).astype(BF16)
        pre[1 - now] = before(c + 1)
        after(c, active)
        return carry

    lax.fori_loop(0, steps - 1, step, 0)
    after(steps - 1, gelu(pre[(steps - 1) % 2]).astype(BF16))


def early_kernel(second, mlp_in, fc, total, pre):
    total[...] = second[...]
    hidden_units(mlp_in, fc, pre, total)


def late_kernel(place, early, mlp_in, fc, g_head, w_head, keep_ref, send_ref, pre, total, hidden):
    total[...] = early[...]
    hidden_units(mlp_in, fc, pre, total)
    norm_into(total, g_head, hidden)
    first = place[1] == 0
    for slot in range(SLOTS):
        rows = slice(slot * ROWS, (slot + 1) * ROWS)
        terms = []
        for half in range(2):
            raw = jnp.dot(
                hidden[rows, :], w_head[:, half * 512 : (half + 1) * 512],
                preferred_element_type=F32,
            )
            conf = 1.0 + jnp.exp(raw[:, 384:])
            terms.append([conf * raw[:, c * 128 : (c + 1) * 128] for c in range(3)] + [conf])
        for c in range(4):
            cols = slice(c * 128, (c + 1) * 128)
            low, high = terms[0][c][:TOKI], terms[1][c][:TOKI]
            keep_ref[slot, :, cols] = jnp.where(first, low, high)
            send_ref[slot, :, cols] = jnp.where(first, high, low).astype(BF16)


def window_kernel(windows, image_slot, slot_images, slot_count, place, keep, got, *outs):
    chosen = []
    for slot in range(SLOTS):
        live = slot < slot_count[0]
        for which in range(2):
            index = window_place(image_slot, slot_images, place, slot, which)
            chosen.append(jnp.where(live, index, -1))
    first = place[1] == 0
    for w, out in zip(windows, outs):
        for c in range(4):
            cols = slice(c * 128, (c + 1) * 128)
            acc = jnp.zeros((TOKI, 128), F32)
            for slot in range(SLOTS):
                own = jnp.where(first, chosen[2 * slot], chosen[2 * slot + 1])
                far = jnp.where(first, chosen[2 * slot + 1], chosen[2 * slot])
                acc = acc + jnp.where(own == w, keep[slot, :, cols], 0.0)
                acc = acc + jnp.where(far == w, got[slot, :, cols].astype(F32), 0.0)
            out[:, cols] = acc.astype(out.dtype)


def merge_kernel(base, nearest, further, out):
    def total(cols):
        return base[:, cols] + nearest[:, cols].astype(F32) + further[:, cols].astype(F32)

    weight = jnp.maximum(total(slice(384, 512)), 1.0)
    for c in range(3):
        cols = slice(c * 128, (c + 1) * 128)
        out[0, :, cols] = (total(cols) / weight).astype(BF16)


def pack_kernel(
    features, w_in, w_out, packed, shard, features_here, w_in_here, w_out_here, sems
):
    copies = [
        pltpu.make_async_copy(src, dst, sems.at[i])
        for i, (src, dst) in enumerate(
            ((features, features_here), (w_in, w_in_here), (w_out, w_out_here))
        )
    ]
    for copy in copies:
        copy.start()
    for copy in copies:
        copy.wait()
    count = TOKI - TOP
    packed[88:TOP, HALF:] = jnp.zeros((TOP - 88, HALF), BF16)
    packed[:TOP, :HALF] = features_here[0, :TOP]
    packed[:count, HALF:] = features_here[0, TOP:]
    for target, base in ((packed, TOP), (shard, 0)):
        target[base : base + 24] = w_in_here[0]
        target[base + 24 : base + 48] = w_out_here[0]


SMEM = pl.BlockSpec(memory_space=pltpu.SMEM)
VMEM = pl.BlockSpec(memory_space=pltpu.VMEM)


def call(kernel, scalars, arrays, outs, scratch, flops, name):
    return pl.pallas_call(
        kernel,
        in_specs=[SMEM] * len(scalars) + [VMEM] * len(arrays),
        out_specs=[VMEM] * len(outs),
        out_shape=[jax.ShapeDtypeStruct(s, d) for s, d in outs],
        scratch_shapes=[pltpu.VMEM(s, d) for s, d in scratch],
        compiler_params=pltpu.CompilerParams(vmem_limit_bytes=20 << 20),
        cost_estimate=pl.CostEstimate(flops=flops, transcendentals=0, bytes_accessed=8 << 20),
        name=name,
    )(*scalars, *arrays)


def triple_call(scalars, mine, theirs, g_self, w_qkv):
    return call(
        triple_kernel, scalars, [mine, theirs, g_self, w_qkv],
        [((ALL, D), F32), ((ALL, 3 * D), BF16)], [((ALL, D), BF16)],
        4 * 10**9, "triple_part",
    )


def memory_call(scalars, mine, theirs, g_memory, w_memory):
    return call(
        memory_kernel, scalars, [mine, theirs, g_memory, w_memory],
        [((ALL, 2 * D), BF16)], [((ALL, D), F32), ((ALL, D), BF16)],
        3 * 10**9, "memory_part",
    )[0]


def self_call(rows, triple, g_query, w_out, w_query):
    return call(
        self_kernel, [], [rows, triple, g_query, w_out, w_query],
        [((ALL, D), F32), ((ALL, D), BF16)], [((ALL, D), BF16), ((ALL, D), BF16)],
        12 * 10**9, "self_part",
    )


def cross_call(first, query, key_value, g_mlp, w_out):
    return call(
        cross_kernel, [], [first, query, key_value, g_mlp, w_out],
        [((ALL, D), F32), ((ALL, D), BF16)], [((ALL, D), BF16)],
        12 * 10**9, "cross_part",
    )


def early_call(second, mlp_in, fc):
    return call(
        early_kernel, [], [second, mlp_in, fc],
        [((ALL, D), F32)], [((2, ALL, CHUNK), F32)], 10 * 10**9, "early_part",
    )[0]


def late_call(place, early, mlp_in, fc, g_head, w_head):
    return call(
        late_kernel, [place], [early, mlp_in, fc, g_head, w_head],
        [((SLOTS, TOKI, 512), F32), ((SLOTS, TOKI, 512), BF16)],
        [((2, ALL, CHUNK), F32), ((ALL, D), F32), ((ALL, D), BF16)],
        5 * 10**9, "late_part",
    )


def window_call(windows, scalars, keep, got):
    return call(
        functools.partial(window_kernel, windows), scalars, [keep, got],
        [((TOKI, 512), BF16 if w else F32) for w in windows], [], 10**8,
        "furthest_part" if windows == (3,) else "window_part",
    )


def pack_call(features, w_in, w_out):
    outs = [((TOP + 48, D), BF16), ((48, D), BF16)]
    return pl.pallas_call(
        pack_kernel,
        in_specs=[pl.BlockSpec(memory_space=pltpu.MemorySpace.HBM)] * 3,
        out_specs=[VMEM] * 2,
        out_shape=[jax.ShapeDtypeStruct(s, d) for s, d in outs],
        scratch_shapes=[
            pltpu.VMEM((1, TOKI, HALF), BF16),
            pltpu.VMEM((1, 24, D), BF16),
            pltpu.VMEM((1, 24, D), BF16),
            pltpu.SemaphoreType.DMA((3,)),
        ],
        name="pack_part",
    )(features, w_in, w_out)


def merge_call(*arrays):
    return call(merge_kernel, [], arrays, [((1, TOKI, HALF), BF16)], [], 10**8, "merge_part")[0]


def along(array, axis, by):
    count = lax.axis_size("pairs")
    stride, size = {"y": (32, 4), "x": (8, 4), "z": (1, 8)}[axis]

    def target(p):
        here = p // stride % size
        return p + ((here + by) % size - here) * stride

    return lax.ppermute(array, "pairs", [(p, target(p)) for p in range(count)])


def tied(*arrays):
    return lax.optimization_barrier(arrays)


def hidden_rows(shards):
    inner = [s[-48:-24] for s in shards]
    outer = [s[-24:] for s in shards]
    return jnp.stack([jnp.concatenate(inner, axis=0), jnp.concatenate(outer, axis=0)])


def three_hops(block, axis):
    return [along(block, axis, by) for by in (1, -1, 2)]


def first_hop(block, axis):
    return along(block, axis, 1), along(block, axis, -1)


def second_hop(left, right, axis):
    half = left.shape[1] // 2
    return along(left[:, :half], axis, 1), along(right[:, half:], axis, -1)


def on_device(
    features,
    image_slot,
    slot_images,
    slot_count,
    gain_self,
    gain_query,
    gain_memory,
    gain_mlp,
    gain_head,
    w_qkv,
    w_self_out,
    w_query,
    w_memory,
    w_cross_out,
    w_fc1,
    w_fc2,
    w_head,
):
    place = jnp.stack([lax.axis_index("pairs"), lax.axis_index("side")]).astype(jnp.int32)
    packed, shard = pack_call(features, w_fc1, w_fc2)
    next2, next1 = shifted(packed, -2), shifted(packed, -1)
    last1, last2 = shifted(shard, 1), shifted(shard, 2)
    last34 = shifted(jnp.concatenate([last1, last2], axis=0), 2)
    next3, last34 = tied(shifted(next2, -1), last34)
    part_x = hidden_rows([shard, last1, last2, next1])
    part_y = hidden_rows([next2, next3, last34[:48], last34[48:]])
    mine = jnp.stack([packed[:TOP], next1[:TOP], next2[:TOP], next3[:TOP]])
    theirs = other_core(mine)
    scalars = [image_slot, slot_images.reshape(-1), place]
    near_x, near_y = three_hops(part_x, "x"), three_hops(part_y, "y")
    rows, triple = triple_call(scalars, mine, theirs, gain_self, w_qkv[0])
    key_value = memory_call(scalars, mine, theirs, gain_memory, w_memory[0])
    near_x, near_y, rows, triple, key_value = tied(near_x, near_y, rows, triple, key_value)
    plane_x = jnp.concatenate([part_x, *near_x], axis=1)
    plane_y = jnp.concatenate([part_y, *near_y], axis=1)
    near_x, near_y = first_hop(plane_x, "y"), first_hop(plane_y, "x")
    first, query = self_call(rows, triple, gain_query, w_self_out[0], w_query[0])
    second, mlp_in = cross_call(first, query, key_value, gain_mlp, w_cross_out[0])
    near_x, near_y, second, mlp_in = tied(near_x, near_y, second, mlp_in)
    far_x, far_y = second_hop(*near_x, "y"), second_hop(*near_y, "x")
    fc_early = jnp.concatenate([plane_x, *near_x, plane_y, *near_y], axis=1)
    early = early_call(second, mlp_in, fc_early)
    fc_late = jnp.concatenate([*far_x, *far_y], axis=1)
    keep, send = late_call(place, early, mlp_in, fc_late, gain_head, w_head[0])
    got = other_core(send)
    scalars = [image_slot, slot_images.reshape(-1), slot_count, place]
    (furthest,) = window_call((3,), scalars, keep, got)
    third = shifted(furthest, 1)
    base, piece1, piece2 = window_call((0, 1, 2), scalars, keep, got)
    nearest = shifted(piece1, 1)
    further = shifted((piece2.astype(F32) + third.astype(F32)).astype(BF16), 2)
    return merge_call(base, nearest, further)


def solution(mesh):
    placed = (
        P("pairs", None, "side"),
        P(),
        P("pairs", None),
        P("pairs"),
        P("side", None),
        P("side", None),
        P("side", None),
        P("side", None),
        P("side", None),
        P("side", None, None),
        P("side", None, None),
        P("side", None, None),
        P("side", None, None),
        P("side", None, None),
        P("side", "pairs", None),
        P("side", "pairs", None),
        P("side", None, None),
    )
    return jax.shard_map(
        on_device, mesh=mesh, in_specs=placed, out_specs=P("pairs", None, "side"), check_vma=False
    )
```

```python
import functools

import jax
import jax.numpy as jnp
from jax import lax
from jax.experimental import pallas as pl
from jax.experimental.pallas import tpu as pltpu
from jax.sharding import PartitionSpec as P

D = 768
HEAD_DIM = 64
TOKI = 196
ROWS = 208
HALF = 384
TOP = 104
WINDOW = 4
SLOTS = 3
ALL = SLOTS * ROWS
CHUNK = 256
F32 = jnp.float32
BF16 = jnp.bfloat16


def shifted(array, by):
    count = lax.axis_size("pairs")
    return lax.ppermute(array, "pairs", [(i, (i + by) % count) for i in range(count)])


def other_core(array):
    return lax.ppermute(array, "side", [(0, 1), (1, 0)])


def layer_norm(values, gain):
    center = values - jnp.mean(values, axis=-1, keepdims=True)
    spread = jnp.mean(center * center, axis=-1, keepdims=True)
    return center * lax.rsqrt(spread + 1e-06) * gain


def window_place(image_slot, slot_images, place, slot, which):
    stored = image_slot[slot_images[2 * slot + which]]
    return lax.rem(stored - place[0] + 128, 128)


def padded_rows(image_slot, slot_images, place, mine, theirs, swap, target):
    which = place[1] if not swap else 1 - place[1]
    first = place[1] == 0
    for slot in range(SLOTS):
        index = window_place(image_slot, slot_images, place, slot, which)
        own, far = mine[index].astype(F32), theirs[index].astype(F32)
        base = slot * ROWS
        target[base + 192 : base + ROWS, :] = jnp.zeros((ROWS - 192, D), F32)
        for part, count in ((0, TOP), (1, TOKI - TOP)):
            rows = slice(base + part * TOP, base + part * TOP + count)
            cols = slice(part * HALF, (part + 1) * HALF)
            target[rows, :HALF] = jnp.where(first, own[:count, cols], far[:count, cols])
            target[rows, HALF:] = jnp.where(first, far[:count, cols], own[:count, cols])


def norm_into(source, gain, target):
    for slot in range(SLOTS):
        rows = slice(slot * ROWS, (slot + 1) * ROWS)
        target[rows, :] = layer_norm(source[rows, :], gain[...]).astype(BF16)


def attention(q_ref, q_base, k_ref, k_base, v_ref, v_base, out_ref):
    lane = lax.broadcasted_iota(jnp.int32, (ROWS, 128), 1)
    low_lanes = lane < HEAD_DIM
    key_ok = lax.broadcasted_iota(jnp.int32, (ROWS, ROWS), 1) < TOKI

    def step(t, carry):
        slot = t // 3
        group = t - 3 * slot
        rows = pl.ds(pl.multiple_of(slot * ROWS, ROWS), ROWS)
        for pair in range(2):
            col = group * 256 + pair * 128
            q = q_ref[rows, pl.ds(pl.multiple_of(q_base + col, 128), 128)]
            k = k_ref[rows, pl.ds(pl.multiple_of(k_base + col, 128), 128)]
            v = v_ref[rows, pl.ds(pl.multiple_of(v_base + col, 128), 128)]
            outs = []
            for head in range(2):
                own = low_lanes if head == 0 else jnp.logical_not(low_lanes)
                scores = lax.dot_general(
                    jnp.where(own, q, jnp.zeros_like(q)),
                    k,
                    (((1,), (1,)), ((), ())),
                    preferred_element_type=F32,
                )
                expon = jnp.where(key_ok, jnp.exp(scores), 0.0)
                total = jnp.sum(expon, axis=-1, keepdims=True)
                weights = (expon * (1.0 / total)).astype(BF16)
                outs.append(jnp.dot(weights, v, preferred_element_type=F32))
            out_ref[rows, pl.ds(pl.multiple_of(col, 128), 128)] = jnp.where(
                low_lanes, outs[0], outs[1]
            ).astype(BF16)
        return carry

    lax.fori_loop(0, 3 * SLOTS, step, 0)


def project(source, weight, width, write):
    def step(n, carry):
        cols = pl.ds(pl.multiple_of(n * 256, 256), 256)
        write(n, cols, jnp.dot(source[...], weight[:, cols], preferred_element_type=F32))
        return carry

    lax.fori_loop(0, width // 256, step, 0)


def triple_kernel(
    image_slot, slot_images, place, mine, theirs, g_self, w_qkv, rows_ref, triple_ref, hidden
):
    padded_rows(image_slot, slot_images, place, mine, theirs, False, rows_ref)
    norm_into(rows_ref, g_self, hidden)

    def write_triple(n, cols, value):
        triple_ref[:, cols] = (value * jnp.where(n < 3, 0.125, 1.0)).astype(BF16)

    project(hidden, w_qkv, 3 * D, write_triple)


def memory_kernel(
    image_slot, slot_images, place, mine, theirs, g_memory, w_memory, kv_ref, rows, hidden
):
    padded_rows(image_slot, slot_images, place, mine, theirs, True, rows)
    norm_into(rows, g_memory, hidden)

    def write_kv(n, cols, value):
        kv_ref[:, cols] = value.astype(BF16)

    project(hidden, w_memory, 2 * D, write_kv)


def self_kernel(rows, triple, g_query, w_out, w_query, first_ref, query_ref, hidden, mixed):
    attention(triple, 0, triple, D, triple, 2 * D, mixed)

    def add_first(n, cols, value):
        first_ref[:, cols] = rows[:, cols] + value

    project(mixed, w_out, D, add_first)
    norm_into(first_ref, g_query, hidden)

    def write_query(n, cols, value):
        query_ref[:, cols] = (value * 0.125).astype(BF16)

    project(hidden, w_query, D, write_query)


def cross_kernel(first, query, key_value, g_mlp, w_out, second_ref, mlp_ref, mixed):
    attention(query, 0, key_value, 0, key_value, D, mixed)

    def add_second(n, cols, value):
        second_ref[:, cols] = first[:, cols] + value

    project(mixed, w_out, D, add_second)
    norm_into(second_ref, g_mlp, mlp_ref)


def gelu(value):
    return value * (1.0 + lax.erf(value * 0.7071067811865476)) * 0.5


def hidden_units(mlp_in, fc, pre, total):
    steps = fc.shape[1] // CHUNK

    def before(c):
        rows = pl.ds(pl.multiple_of(c * CHUNK, CHUNK), CHUNK)
        return lax.dot_general(
            mlp_in[...], fc[0, rows, :], (((1,), (1,)), ((), ())), preferred_element_type=F32
        )

    def after(c, active):
        rows = pl.ds(pl.multiple_of(c * CHUNK, CHUNK), CHUNK)
        total[...] = total[...] + jnp.dot(active, fc[1, rows, :], preferred_element_type=F32)

    pre[0] = before(0)

    def step(c, carry):
        now = lax.rem(c, 2)
        active = gelu(pre[now]).astype(BF16)
        pre[1 - now] = before(c + 1)
        after(c, active)
        return carry

    lax.fori_loop(0, steps - 1, step, 0)
    after(steps - 1, gelu(pre[(steps - 1) % 2]).astype(BF16))


def early_kernel(second, mlp_in, fc, total, pre):
    total[...] = second[...]
    hidden_units(mlp_in, fc, pre, total)


def late_kernel(place, early, mlp_in, fc, g_head, w_head, keep_ref, send_ref, pre, total, hidden):
    total[...] = early[...]
    hidden_units(mlp_in, fc, pre, total)
    norm_into(total, g_head, hidden)
    first = place[1] == 0
    for slot in range(SLOTS):
        rows = slice(slot * ROWS, (slot + 1) * ROWS)
        terms = []
        for half in range(2):
            raw = jnp.dot(
                hidden[rows, :], w_head[:, half * 512 : (half + 1) * 512],
                preferred_element_type=F32,
            )
            conf = 1.0 + jnp.exp(raw[:, 384:])
            terms.append([conf * raw[:, c * 128 : (c + 1) * 128] for c in range(3)] + [conf])
        for c in range(4):
            cols = slice(c * 128, (c + 1) * 128)
            low, high = terms[0][c][:TOKI], terms[1][c][:TOKI]
            keep_ref[slot, :, cols] = jnp.where(first, low, high)
            send_ref[slot, :, cols] = jnp.where(first, high, low).astype(BF16)


def window_kernel(windows, image_slot, slot_images, slot_count, place, keep, got, *outs):
    chosen = []
    for slot in range(SLOTS):
        live = slot < slot_count[0]
        for which in range(2):
            index = window_place(image_slot, slot_images, place, slot, which)
            chosen.append(jnp.where(live, index, -1))
    first = place[1] == 0
    for w, out in zip(windows, outs):
        for c in range(4):
            cols = slice(c * 128, (c + 1) * 128)
            acc = jnp.zeros((TOKI, 128), F32)
            for slot in range(SLOTS):
                own = jnp.where(first, chosen[2 * slot], chosen[2 * slot + 1])
                far = jnp.where(first, chosen[2 * slot + 1], chosen[2 * slot])
                acc = acc + jnp.where(own == w, keep[slot, :, cols], 0.0)
                acc = acc + jnp.where(far == w, got[slot, :, cols].astype(F32), 0.0)
            out[:, cols] = acc.astype(out.dtype)


def merge_kernel(base, nearest, further, out):
    def total(cols):
        return base[:, cols] + nearest[:, cols].astype(F32) + further[:, cols].astype(F32)

    weight = jnp.maximum(total(slice(384, 512)), 1.0)
    for c in range(3):
        cols = slice(c * 128, (c + 1) * 128)
        out[0, :, cols] = (total(cols) / weight).astype(BF16)


def pack_kernel(
    features, w_in, w_out, packed, shard, features_here, w_in_here, w_out_here, sems
):
    copies = [
        pltpu.make_async_copy(src, dst, sems.at[i])
        for i, (src, dst) in enumerate(
            ((features, features_here), (w_in, w_in_here), (w_out, w_out_here))
        )
    ]
    for copy in copies:
        copy.start()
    for copy in copies:
        copy.wait()
    count = TOKI - TOP
    packed[88:TOP, HALF:] = jnp.zeros((TOP - 88, HALF), BF16)
    packed[:TOP, :HALF] = features_here[0, :TOP]
    packed[:count, HALF:] = features_here[0, TOP:]
    for target, base in ((packed, TOP), (shard, 0)):
        target[base : base + 24] = w_in_here[0]
        target[base + 24 : base + 48] = w_out_here[0]


SMEM = pl.BlockSpec(memory_space=pltpu.SMEM)
VMEM = pl.BlockSpec(memory_space=pltpu.VMEM)


def call(kernel, scalars, arrays, outs, scratch, flops, name):
    return pl.pallas_call(
        kernel,
        in_specs=[SMEM] * len(scalars) + [VMEM] * len(arrays),
        out_specs=[VMEM] * len(outs),
        out_shape=[jax.ShapeDtypeStruct(s, d) for s, d in outs],
        scratch_shapes=[pltpu.VMEM(s, d) for s, d in scratch],
        compiler_params=pltpu.CompilerParams(vmem_limit_bytes=20 << 20),
        cost_estimate=pl.CostEstimate(flops=flops, transcendentals=0, bytes_accessed=8 << 20),
        name=name,
    )(*scalars, *arrays)


def triple_call(scalars, mine, theirs, g_self, w_qkv):
    return call(
        triple_kernel, scalars, [mine, theirs, g_self, w_qkv],
        [((ALL, D), F32), ((ALL, 3 * D), BF16)], [((ALL, D), BF16)],
        4 * 10**9, "triple_part",
    )


def memory_call(scalars, mine, theirs, g_memory, w_memory):
    return call(
        memory_kernel, scalars, [mine, theirs, g_memory, w_memory],
        [((ALL, 2 * D), BF16)], [((ALL, D), F32), ((ALL, D), BF16)],
        3 * 10**9, "memory_part",
    )[0]


def self_call(rows, triple, g_query, w_out, w_query):
    return call(
        self_kernel, [], [rows, triple, g_query, w_out, w_query],
        [((ALL, D), F32), ((ALL, D), BF16)], [((ALL, D), BF16), ((ALL, D), BF16)],
        12 * 10**9, "self_part",
    )


def cross_call(first, query, key_value, g_mlp, w_out):
    return call(
        cross_kernel, [], [first, query, key_value, g_mlp, w_out],
        [((ALL, D), F32), ((ALL, D), BF16)], [((ALL, D), BF16)],
        12 * 10**9, "cross_part",
    )


def early_call(second, mlp_in, fc):
    return call(
        early_kernel, [], [second, mlp_in, fc],
        [((ALL, D), F32)], [((2, ALL, CHUNK), F32)], 10 * 10**9, "early_part",
    )[0]


def late_call(place, early, mlp_in, fc, g_head, w_head):
    return call(
        late_kernel, [place], [early, mlp_in, fc, g_head, w_head],
        [((SLOTS, TOKI, 512), F32), ((SLOTS, TOKI, 512), BF16)],
        [((2, ALL, CHUNK), F32), ((ALL, D), F32), ((ALL, D), BF16)],
        5 * 10**9, "late_part",
    )


def window_call(windows, scalars, keep, got):
    return call(
        functools.partial(window_kernel, windows), scalars, [keep, got],
        [((TOKI, 512), BF16 if w else F32) for w in windows], [], 10**8,
        "furthest_part" if windows == (3,) else "window_part",
    )


def pack_call(features, w_in, w_out):
    outs = [((TOP + 48, D), BF16), ((48, D), BF16)]
    return pl.pallas_call(
        pack_kernel,
        in_specs=[pl.BlockSpec(memory_space=pltpu.MemorySpace.HBM)] * 3,
        out_specs=[VMEM] * 2,
        out_shape=[jax.ShapeDtypeStruct(s, d) for s, d in outs],
        scratch_shapes=[
            pltpu.VMEM((1, TOKI, HALF), BF16),
            pltpu.VMEM((1, 24, D), BF16),
            pltpu.VMEM((1, 24, D), BF16),
            pltpu.SemaphoreType.DMA((3,)),
        ],
        name="pack_part",
    )(features, w_in, w_out)


def merge_call(*arrays):
    return call(merge_kernel, [], arrays, [((1, TOKI, HALF), BF16)], [], 10**8, "merge_part")[0]


def along(array, axis, by):
    count = lax.axis_size("pairs")
    stride, size = {"y": (32, 4), "x": (8, 4), "z": (1, 8)}[axis]

    def target(p):
        here = p // stride % size
        return p + ((here + by) % size - here) * stride

    return lax.ppermute(array, "pairs", [(p, target(p)) for p in range(count)])


def tied(*arrays):
    return lax.optimization_barrier(arrays)


def hidden_rows(shards):
    inner = [s[-48:-24] for s in shards]
    outer = [s[-24:] for s in shards]
    return jnp.stack([jnp.concatenate(inner, axis=0), jnp.concatenate(outer, axis=0)])


def three_hops(block, axis):
    return [along(block, axis, by) for by in (1, -1, 2)]


def first_hop(block, axis):
    return along(block, axis, 1), along(block, axis, -1)


def second_hop(left, right, axis):
    half = left.shape[1] // 2
    return along(left[:, :half], axis, 1), along(right[:, half:], axis, -1)


def on_device(
    features,
    image_slot,
    slot_images,
    slot_count,
    gain_self,
    gain_query,
    gain_memory,
    gain_mlp,
    gain_head,
    w_qkv,
    w_self_out,
    w_query,
    w_memory,
    w_cross_out,
    w_fc1,
    w_fc2,
    w_head,
):
    place = jnp.stack([lax.axis_index("pairs"), lax.axis_index("side")]).astype(jnp.int32)
    packed, shard = pack_call(features, w_fc1, w_fc2)
    next2 = shifted(packed, -2)
    last1, last2, later = tied(shifted(shard, 1), shifted(shard, 2), packed)
    next1 = shifted(later, -1)
    last34 = shifted(jnp.concatenate([last1, last2], axis=0), 2)
    next3, last34, next1 = tied(shifted(next2, -1), last34, next1)
    part_x = hidden_rows([shard, last1, last2, next2])
    part_y = hidden_rows([next1, next3, last34[:48], last34[48:]])
    mine = jnp.stack([packed[:TOP], next1[:TOP], next2[:TOP], next3[:TOP]])
    theirs = other_core(mine)
    scalars = [image_slot, slot_images.reshape(-1), place]
    near_x, near_y = three_hops(part_x, "x"), three_hops(part_y, "y")
    rows, triple = triple_call(scalars, mine, theirs, gain_self, w_qkv[0])
    key_value = memory_call(scalars, mine, theirs, gain_memory, w_memory[0])
    near_x, near_y, rows, triple, key_value = tied(near_x, near_y, rows, triple, key_value)
    plane_x = jnp.concatenate([part_x, *near_x], axis=1)
    plane_y = jnp.concatenate([part_y, *near_y], axis=1)
    near_x, near_y = first_hop(plane_x, "y"), first_hop(plane_y, "x")
    first, query = self_call(rows, triple, gain_query, w_self_out[0], w_query[0])
    second, mlp_in = cross_call(first, query, key_value, gain_mlp, w_cross_out[0])
    near_x, near_y, second, mlp_in = tied(near_x, near_y, second, mlp_in)
    far_x, far_y = second_hop(*near_x, "y"), second_hop(*near_y, "x")
    fc_early = jnp.concatenate([plane_x, *near_x, plane_y, *near_y], axis=1)
    early = early_call(second, mlp_in, fc_early)
    fc_late = jnp.concatenate([*far_x, *far_y], axis=1)
    keep, send = late_call(place, early, mlp_in, fc_late, gain_head, w_head[0])
    got = other_core(send)
    scalars = [image_slot, slot_images.reshape(-1), slot_count, place]
    (furthest,) = window_call((3,), scalars, keep, got)
    third = shifted(furthest, 1)
    base, piece1, piece2 = window_call((0, 1, 2), scalars, keep, got)
    nearest = shifted(piece1, 1)
    further = shifted((piece2.astype(F32) + third.astype(F32)).astype(BF16), 2)
    return merge_call(base, nearest, further)


def solution(mesh):
    placed = (
        P("pairs", None, "side"),
        P(),
        P("pairs", None),
        P("pairs"),
        P("side", None),
        P("side", None),
        P("side", None),
        P("side", None),
        P("side", None),
        P("side", None, None),
        P("side", None, None),
        P("side", None, None),
        P("side", None, None),
        P("side", None, None),
        P("side", "pairs", None),
        P("side", "pairs", None),
        P("side", None, None),
    )
    return jax.shard_map(
        on_device, mesh=mesh, in_specs=placed, out_specs=P("pairs", None, "side"), check_vma=False
    )
```

```python
import functools

import jax
import jax.numpy as jnp
from jax import lax
from jax.experimental import pallas as pl
from jax.experimental.pallas import tpu as pltpu
from jax.sharding import PartitionSpec as P

D = 768
HEAD_DIM = 64
TOKI = 196
ROWS = 208
HALF = 384
TOP = 104
WINDOW = 4
SLOTS = 3
ALL = SLOTS * ROWS
CHUNK = 256
F32 = jnp.float32
BF16 = jnp.bfloat16


def shifted(array, by):
    count = lax.axis_size("pairs")
    return lax.ppermute(array, "pairs", [(i, (i + by) % count) for i in range(count)])


def other_core(array):
    return lax.ppermute(array, "side", [(0, 1), (1, 0)])


def layer_norm(values, gain):
    center = values - jnp.mean(values, axis=-1, keepdims=True)
    spread = jnp.mean(center * center, axis=-1, keepdims=True)
    return center * lax.rsqrt(spread + 1e-06) * gain


def window_place(image_slot, slot_images, place, slot, which):
    stored = image_slot[slot_images[2 * slot + which]]
    return lax.rem(stored - place[0] + 128, 128)


def padded_rows(image_slot, slot_images, place, mine, theirs, swap, target):
    which = place[1] if not swap else 1 - place[1]
    first = place[1] == 0
    for slot in range(SLOTS):
        index = window_place(image_slot, slot_images, place, slot, which)
        own, far = mine[index].astype(F32), theirs[index].astype(F32)
        base = slot * ROWS
        target[base + 192 : base + ROWS, :] = jnp.zeros((ROWS - 192, D), F32)
        for part, count in ((0, TOP), (1, TOKI - TOP)):
            rows = slice(base + part * TOP, base + part * TOP + count)
            cols = slice(part * HALF, (part + 1) * HALF)
            target[rows, :HALF] = jnp.where(first, own[:count, cols], far[:count, cols])
            target[rows, HALF:] = jnp.where(first, far[:count, cols], own[:count, cols])


def norm_into(source, gain, target):
    for slot in range(SLOTS):
        rows = slice(slot * ROWS, (slot + 1) * ROWS)
        target[rows, :] = layer_norm(source[rows, :], gain[...]).astype(BF16)


def attention(q_ref, q_base, k_ref, k_base, v_ref, v_base, out_ref):
    lane = lax.broadcasted_iota(jnp.int32, (ROWS, 128), 1)
    low_lanes = lane < HEAD_DIM
    key_ok = lax.broadcasted_iota(jnp.int32, (ROWS, ROWS), 1) < TOKI

    def step(t, carry):
        slot = t // 3
        group = t - 3 * slot
        rows = pl.ds(pl.multiple_of(slot * ROWS, ROWS), ROWS)
        for pair in range(2):
            col = group * 256 + pair * 128
            q = q_ref[rows, pl.ds(pl.multiple_of(q_base + col, 128), 128)]
            k = k_ref[rows, pl.ds(pl.multiple_of(k_base + col, 128), 128)]
            v = v_ref[rows, pl.ds(pl.multiple_of(v_base + col, 128), 128)]
            outs = []
            for head in range(2):
                own = low_lanes if head == 0 else jnp.logical_not(low_lanes)
                scores = lax.dot_general(
                    jnp.where(own, q, jnp.zeros_like(q)),
                    k,
                    (((1,), (1,)), ((), ())),
                    preferred_element_type=F32,
                )
                expon = jnp.where(key_ok, jnp.exp(scores), 0.0)
                total = jnp.sum(expon, axis=-1, keepdims=True)
                weights = (expon * (1.0 / total)).astype(BF16)
                outs.append(jnp.dot(weights, v, preferred_element_type=F32))
            out_ref[rows, pl.ds(pl.multiple_of(col, 128), 128)] = jnp.where(
                low_lanes, outs[0], outs[1]
            ).astype(BF16)
        return carry

    lax.fori_loop(0, 3 * SLOTS, step, 0)


def project(source, weight, width, write):
    def step(n, carry):
        cols = pl.ds(pl.multiple_of(n * 256, 256), 256)
        write(n, cols, jnp.dot(source[...], weight[:, cols], preferred_element_type=F32))
        return carry

    lax.fori_loop(0, width // 256, step, 0)


def triple_kernel(
    image_slot, slot_images, place, mine, theirs, g_self, w_qkv, rows_ref, triple_ref, hidden
):
    padded_rows(image_slot, slot_images, place, mine, theirs, False, rows_ref)
    norm_into(rows_ref, g_self, hidden)

    def write_triple(n, cols, value):
        triple_ref[:, cols] = (value * jnp.where(n < 3, 0.125, 1.0)).astype(BF16)

    project(hidden, w_qkv, 3 * D, write_triple)


def memory_kernel(
    image_slot, slot_images, place, mine, theirs, g_memory, w_memory, kv_ref, rows, hidden
):
    padded_rows(image_slot, slot_images, place, mine, theirs, True, rows)
    norm_into(rows, g_memory, hidden)

    def write_kv(n, cols, value):
        kv_ref[:, cols] = value.astype(BF16)

    project(hidden, w_memory, 2 * D, write_kv)


def self_kernel(rows, triple, g_query, w_out, w_query, first_ref, query_ref, hidden, mixed):
    attention(triple, 0, triple, D, triple, 2 * D, mixed)

    def add_first(n, cols, value):
        first_ref[:, cols] = rows[:, cols] + value

    project(mixed, w_out, D, add_first)
    norm_into(first_ref, g_query, hidden)

    def write_query(n, cols, value):
        query_ref[:, cols] = (value * 0.125).astype(BF16)

    project(hidden, w_query, D, write_query)


def cross_kernel(first, query, key_value, g_mlp, w_out, second_ref, mlp_ref, mixed):
    attention(query, 0, key_value, 0, key_value, D, mixed)

    def add_second(n, cols, value):
        second_ref[:, cols] = first[:, cols] + value

    project(mixed, w_out, D, add_second)
    norm_into(second_ref, g_mlp, mlp_ref)


def gelu(value):
    return value * (1.0 + lax.erf(value * 0.7071067811865476)) * 0.5


def hidden_units(mlp_in, fc, pre, total):
    steps = fc.shape[1] // CHUNK

    def before(c):
        rows = pl.ds(pl.multiple_of(c * CHUNK, CHUNK), CHUNK)
        return lax.dot_general(
            mlp_in[...], fc[0, rows, :], (((1,), (1,)), ((), ())), preferred_element_type=F32
        )

    def after(c, active):
        rows = pl.ds(pl.multiple_of(c * CHUNK, CHUNK), CHUNK)
        total[...] = total[...] + jnp.dot(active, fc[1, rows, :], preferred_element_type=F32)

    pre[0] = before(0)

    def step(c, carry):
        now = lax.rem(c, 2)
        active = gelu(pre[now]).astype(BF16)
        pre[1 - now] = before(c + 1)
        after(c, active)
        return carry

    lax.fori_loop(0, steps - 1, step, 0)
    after(steps - 1, gelu(pre[(steps - 1) % 2]).astype(BF16))


def early_kernel(second, mlp_in, fc, total, pre):
    total[...] = second[...]
    hidden_units(mlp_in, fc, pre, total)


def late_kernel(place, early, mlp_in, fc, g_head, w_head, keep_ref, send_ref, pre, total, hidden):
    total[...] = early[...]
    hidden_units(mlp_in, fc, pre, total)
    norm_into(total, g_head, hidden)
    first = place[1] == 0
    for slot in range(SLOTS):
        rows = slice(slot * ROWS, (slot + 1) * ROWS)
        terms = []
        for half in range(2):
            raw = jnp.dot(
                hidden[rows, :], w_head[:, half * 512 : (half + 1) * 512],
                preferred_element_type=F32,
            )
            conf = 1.0 + jnp.exp(raw[:, 384:])
            terms.append([conf * raw[:, c * 128 : (c + 1) * 128] for c in range(3)] + [conf])
        for c in range(4):
            cols = slice(c * 128, (c + 1) * 128)
            low, high = terms[0][c][:TOKI], terms[1][c][:TOKI]
            keep_ref[slot, :, cols] = jnp.where(first, low, high)
            send_ref[slot, :, cols] = jnp.where(first, high, low).astype(BF16)


def window_kernel(windows, image_slot, slot_images, slot_count, place, keep, got, *outs):
    chosen = []
    for slot in range(SLOTS):
        live = slot < slot_count[0]
        for which in range(2):
            index = window_place(image_slot, slot_images, place, slot, which)
            chosen.append(jnp.where(live, index, -1))
    first = place[1] == 0
    for w, out in zip(windows, outs):
        for c in range(4):
            cols = slice(c * 128, (c + 1) * 128)
            acc = jnp.zeros((TOKI, 128), F32)
            for slot in range(SLOTS):
                own = jnp.where(first, chosen[2 * slot], chosen[2 * slot + 1])
                far = jnp.where(first, chosen[2 * slot + 1], chosen[2 * slot])
                acc = acc + jnp.where(own == w, keep[slot, :, cols], 0.0)
                acc = acc + jnp.where(far == w, got[slot, :, cols].astype(F32), 0.0)
            out[:, cols] = acc.astype(out.dtype)


def merge_kernel(base, nearest, further, out):
    def total(cols):
        return base[:, cols] + nearest[:, cols].astype(F32) + further[:, cols].astype(F32)

    weight = jnp.maximum(total(slice(384, 512)), 1.0)
    for c in range(3):
        cols = slice(c * 128, (c + 1) * 128)
        out[0, :, cols] = (total(cols) / weight).astype(BF16)


def pack_kernel(
    features, w_in, w_out, packed, shard, features_here, w_in_here, w_out_here, sems
):
    copies = [
        pltpu.make_async_copy(src, dst, sems.at[i])
        for i, (src, dst) in enumerate(
            ((features, features_here), (w_in, w_in_here), (w_out, w_out_here))
        )
    ]
    for copy in copies:
        copy.start()
    for copy in copies:
        copy.wait()
    count = TOKI - TOP
    packed[88:TOP, HALF:] = jnp.zeros((TOP - 88, HALF), BF16)
    packed[:TOP, :HALF] = features_here[0, :TOP]
    packed[:count, HALF:] = features_here[0, TOP:]
    for target, base in ((packed, TOP), (shard, 0)):
        target[base : base + 24] = w_in_here[0]
        target[base + 24 : base + 48] = w_out_here[0]


SMEM = pl.BlockSpec(memory_space=pltpu.SMEM)
VMEM = pl.BlockSpec(memory_space=pltpu.VMEM)


def call(kernel, scalars, arrays, outs, scratch, flops, name):
    return pl.pallas_call(
        kernel,
        in_specs=[SMEM] * len(scalars) + [VMEM] * len(arrays),
        out_specs=[VMEM] * len(outs),
        out_shape=[jax.ShapeDtypeStruct(s, d) for s, d in outs],
        scratch_shapes=[pltpu.VMEM(s, d) for s, d in scratch],
        compiler_params=pltpu.CompilerParams(vmem_limit_bytes=20 << 20),
        cost_estimate=pl.CostEstimate(flops=flops, transcendentals=0, bytes_accessed=8 << 20),
        name=name,
    )(*scalars, *arrays)


def triple_call(scalars, mine, theirs, g_self, w_qkv):
    return call(
        triple_kernel, scalars, [mine, theirs, g_self, w_qkv],
        [((ALL, D), F32), ((ALL, 3 * D), BF16)], [((ALL, D), BF16)],
        4 * 10**9, "triple_part",
    )


def memory_call(scalars, mine, theirs, g_memory, w_memory):
    return call(
        memory_kernel, scalars, [mine, theirs, g_memory, w_memory],
        [((ALL, 2 * D), BF16)], [((ALL, D), F32), ((ALL, D), BF16)],
        3 * 10**9, "memory_part",
    )[0]


def self_call(rows, triple, g_query, w_out, w_query):
    return call(
        self_kernel, [], [rows, triple, g_query, w_out, w_query],
        [((ALL, D), F32), ((ALL, D), BF16)], [((ALL, D), BF16), ((ALL, D), BF16)],
        12 * 10**9, "self_part",
    )


def cross_call(first, query, key_value, g_mlp, w_out):
    return call(
        cross_kernel, [], [first, query, key_value, g_mlp, w_out],
        [((ALL, D), F32), ((ALL, D), BF16)], [((ALL, D), BF16)],
        12 * 10**9, "cross_part",
    )


def early_call(second, mlp_in, fc):
    return call(
        early_kernel, [], [second, mlp_in, fc],
        [((ALL, D), F32)], [((2, ALL, CHUNK), F32)], 10 * 10**9, "early_part",
    )[0]


def late_call(place, early, mlp_in, fc, g_head, w_head):
    return call(
        late_kernel, [place], [early, mlp_in, fc, g_head, w_head],
        [((SLOTS, TOKI, 512), F32), ((SLOTS, TOKI, 512), BF16)],
        [((2, ALL, CHUNK), F32), ((ALL, D), F32), ((ALL, D), BF16)],
        5 * 10**9, "late_part",
    )


def window_call(windows, scalars, keep, got):
    return call(
        functools.partial(window_kernel, windows), scalars, [keep, got],
        [((TOKI, 512), BF16 if w else F32) for w in windows], [], 10**8,
        "furthest_part" if windows == (3,) else "window_part",
    )


def pack_call(features, w_in, w_out):
    outs = [((TOP + 48, D), BF16), ((48, D), BF16)]
    return pl.pallas_call(
        pack_kernel,
        in_specs=[pl.BlockSpec(memory_space=pltpu.MemorySpace.HBM)] * 3,
        out_specs=[VMEM] * 2,
        out_shape=[jax.ShapeDtypeStruct(s, d) for s, d in outs],
        scratch_shapes=[
            pltpu.VMEM((1, TOKI, HALF), BF16),
            pltpu.VMEM((1, 24, D), BF16),
            pltpu.VMEM((1, 24, D), BF16),
            pltpu.SemaphoreType.DMA((3,)),
        ],
        name="pack_part",
    )(features, w_in, w_out)


def merge_call(*arrays):
    return call(merge_kernel, [], arrays, [((1, TOKI, HALF), BF16)], [], 10**8, "merge_part")[0]


def along(array, axis, by):
    count = lax.axis_size("pairs")
    stride, size = {"y": (32, 4), "x": (8, 4), "z": (1, 8)}[axis]

    def target(p):
        here = p // stride % size
        return p + ((here + by) % size - here) * stride

    return lax.ppermute(array, "pairs", [(p, target(p)) for p in range(count)])


def tied(*arrays):
    return lax.optimization_barrier(arrays)


def hidden_rows(shards):
    inner = [s[-48:-24] for s in shards]
    outer = [s[-24:] for s in shards]
    return jnp.stack([jnp.concatenate(inner, axis=0), jnp.concatenate(outer, axis=0)])


def three_hops(block, axis):
    return [along(block, axis, by) for by in (1, -1, 2)]


def first_hop(block, axis):
    return along(block, axis, 1), along(block, axis, -1)


def second_hop(left, right, axis):
    half = left.shape[1] // 2
    return along(left[:, :half], axis, 1), along(right[:, half:], axis, -1)


def on_device(
    features,
    image_slot,
    slot_images,
    slot_count,
    gain_self,
    gain_query,
    gain_memory,
    gain_mlp,
    gain_head,
    w_qkv,
    w_self_out,
    w_query,
    w_memory,
    w_cross_out,
    w_fc1,
    w_fc2,
    w_head,
):
    place = jnp.stack([lax.axis_index("pairs"), lax.axis_index("side")]).astype(jnp.int32)
    packed, shard = pack_call(features, w_fc1, w_fc2)
    next2 = shifted(packed, -2)
    last1, later = tied(shifted(shard, 1), packed)
    last2 = shifted(shard, 2)
    next1 = shifted(later, -1)
    last34 = shifted(jnp.concatenate([last1, last2], axis=0), 2)
    next3, last34, next1 = tied(shifted(next2, -1), last34, next1)
    part_x = hidden_rows([shard, last1, last2, next2])
    part_y = hidden_rows([next1, next3, last34[:48], last34[48:]])
    mine = jnp.stack([packed[:TOP], next1[:TOP], next2[:TOP], next3[:TOP]])
    theirs = other_core(mine)
    scalars = [image_slot, slot_images.reshape(-1), place]
    near_x, near_y = three_hops(part_x, "x"), three_hops(part_y, "y")
    rows, triple = triple_call(scalars, mine, theirs, gain_self, w_qkv[0])
    key_value = memory_call(scalars, mine, theirs, gain_memory, w_memory[0])
    near_x, near_y, rows, triple, key_value = tied(near_x, near_y, rows, triple, key_value)
    plane_x = jnp.concatenate([part_x, *near_x], axis=1)
    plane_y = jnp.concatenate([part_y, *near_y], axis=1)
    near_x, near_y = first_hop(plane_x, "y"), first_hop(plane_y, "x")
    first, query = self_call(rows, triple, gain_query, w_self_out[0], w_query[0])
    second, mlp_in = cross_call(first, query, key_value, gain_mlp, w_cross_out[0])
    near_y, second, mlp_in = tied(near_y, second, mlp_in)
    far_y = second_hop(*near_y, "x")
    near_x, second, mlp_in = tied(near_x, second, mlp_in)
    far_x = second_hop(*near_x, "y")
    fc_early = jnp.concatenate([plane_x, *near_x, plane_y, *near_y], axis=1)
    early = early_call(second, mlp_in, fc_early)
    fc_late = jnp.concatenate([*far_x, *far_y], axis=1)
    keep, send = late_call(place, early, mlp_in, fc_late, gain_head, w_head[0])
    got = other_core(send)
    scalars = [image_slot, slot_images.reshape(-1), slot_count, place]
    (furthest,) = window_call((3,), scalars, keep, got)
    third = shifted(furthest, 1)
    base, piece1, piece2 = window_call((0, 1, 2), scalars, keep, got)
    nearest = shifted(piece1, 1)
    further = shifted((piece2.astype(F32) + third.astype(F32)).astype(BF16), 2)
    return merge_call(base, nearest, further)


def solution(mesh):
    placed = (
        P("pairs", None, "side"),
        P(),
        P("pairs", None),
        P("pairs"),
        P("side", None),
        P("side", None),
        P("side", None),
        P("side", None),
        P("side", None),
        P("side", None, None),
        P("side", None, None),
        P("side", None, None),
        P("side", None, None),
        P("side", None, None),
        P("side", "pairs", None),
        P("side", "pairs", None),
        P("side", None, None),
    )
    return jax.shard_map(
        on_device, mesh=mesh, in_specs=placed, out_specs=P("pairs", None, "side"), check_vma=False
    )
```

```python
import functools

import jax
import jax.numpy as jnp
from jax import lax
from jax.experimental import pallas as pl
from jax.experimental.pallas import tpu as pltpu
from jax.sharding import PartitionSpec as P

D = 768
HEAD_DIM = 64
TOKI = 196
ROWS = 208
HALF = 384
TOP = 104
WINDOW = 4
SLOTS = 3
ALL = SLOTS * ROWS
CHUNK = 256
F32 = jnp.float32
BF16 = jnp.bfloat16


def shifted(array, by):
    count = lax.axis_size("pairs")
    return lax.ppermute(array, "pairs", [(i, (i + by) % count) for i in range(count)])


def other_core(array):
    return lax.ppermute(array, "side", [(0, 1), (1, 0)])


def layer_norm(values, gain):
    center = values - jnp.mean(values, axis=-1, keepdims=True)
    spread = jnp.mean(center * center, axis=-1, keepdims=True)
    return center * lax.rsqrt(spread + 1e-06) * gain


def window_place(image_slot, slot_images, place, slot, which):
    stored = image_slot[slot_images[SLOTS * which + slot]]
    return lax.rem(stored - place[0] + 128, 128)


def padded_rows(image_slot, slot_images, place, mine, theirs, swap, target):
    which = place[1] if not swap else 1 - place[1]
    first = place[1] == 0
    for slot in range(SLOTS):
        index = window_place(image_slot, slot_images, place, slot, which)
        own, far = mine[index].astype(F32), theirs[index].astype(F32)
        base = slot * ROWS
        target[base + 192 : base + ROWS, :] = jnp.zeros((ROWS - 192, D), F32)
        for part, count in ((0, TOP), (1, TOKI - TOP)):
            rows = slice(base + part * TOP, base + part * TOP + count)
            cols = slice(part * HALF, (part + 1) * HALF)
            target[rows, :HALF] = jnp.where(first, own[:count, cols], far[:count, cols])
            target[rows, HALF:] = jnp.where(first, far[:count, cols], own[:count, cols])


def norm_into(source, gain, target):
    for slot in range(SLOTS):
        rows = slice(slot * ROWS, (slot + 1) * ROWS)
        target[rows, :] = layer_norm(source[rows, :], gain[...]).astype(BF16)


def attention(q_ref, q_base, k_ref, k_base, v_ref, v_base, out_ref):
    lane = lax.broadcasted_iota(jnp.int32, (ROWS, 128), 1)
    low_lanes = lane < HEAD_DIM
    key_ok = lax.broadcasted_iota(jnp.int32, (ROWS, ROWS), 1) < TOKI

    def step(t, carry):
        slot = t // 3
        group = t - 3 * slot
        rows = pl.ds(pl.multiple_of(slot * ROWS, ROWS), ROWS)
        for pair in range(2):
            col = group * 256 + pair * 128
            q = q_ref[rows, pl.ds(pl.multiple_of(q_base + col, 128), 128)]
            k = k_ref[rows, pl.ds(pl.multiple_of(k_base + col, 128), 128)]
            v = v_ref[rows, pl.ds(pl.multiple_of(v_base + col, 128), 128)]
            outs = []
            for head in range(2):
                own = low_lanes if head == 0 else jnp.logical_not(low_lanes)
                scores = lax.dot_general(
                    jnp.where(own, q, jnp.zeros_like(q)),
                    k,
                    (((1,), (1,)), ((), ())),
                    preferred_element_type=F32,
                )
                expon = jnp.where(key_ok, jnp.exp(scores), 0.0)
                total = jnp.sum(expon, axis=-1, keepdims=True)
                weights = (expon * (1.0 / total)).astype(BF16)
                outs.append(jnp.dot(weights, v, preferred_element_type=F32))
            out_ref[rows, pl.ds(pl.multiple_of(col, 128), 128)] = jnp.where(
                low_lanes, outs[0], outs[1]
            ).astype(BF16)
        return carry

    lax.fori_loop(0, 3 * SLOTS, step, 0)


def project(source, weight, width, write):
    def step(n, carry):
        cols = pl.ds(pl.multiple_of(n * 256, 256), 256)
        write(n, cols, jnp.dot(source[...], weight[:, cols], preferred_element_type=F32))
        return carry

    lax.fori_loop(0, width // 256, step, 0)


def triple_kernel(
    image_slot, slot_images, place, mine, theirs, g_self, w_qkv, rows_ref, triple_ref, hidden
):
    padded_rows(image_slot, slot_images, place, mine, theirs, False, rows_ref)
    norm_into(rows_ref, g_self, hidden)

    def write_triple(n, cols, value):
        triple_ref[:, cols] = (value * jnp.where(n < 3, 0.125, 1.0)).astype(BF16)

    project(hidden, w_qkv, 3 * D, write_triple)


def memory_kernel(
    image_slot, slot_images, place, mine, theirs, g_memory, w_memory, kv_ref, rows, hidden
):
    padded_rows(image_slot, slot_images, place, mine, theirs, True, rows)
    norm_into(rows, g_memory, hidden)

    def write_kv(n, cols, value):
        kv_ref[:, cols] = value.astype(BF16)

    project(hidden, w_memory, 2 * D, write_kv)


def self_kernel(rows, triple, g_query, w_out, w_query, first_ref, query_ref, hidden, mixed):
    attention(triple, 0, triple, D, triple, 2 * D, mixed)

    def add_first(n, cols, value):
        first_ref[:, cols] = rows[:, cols] + value

    project(mixed, w_out, D, add_first)
    norm_into(first_ref, g_query, hidden)

    def write_query(n, cols, value):
        query_ref[:, cols] = (value * 0.125).astype(BF16)

    project(hidden, w_query, D, write_query)


def cross_kernel(first, query, key_value, g_mlp, w_out, second_ref, mlp_ref, mixed):
    attention(query, 0, key_value, 0, key_value, D, mixed)

    def add_second(n, cols, value):
        second_ref[:, cols] = first[:, cols] + value

    project(mixed, w_out, D, add_second)
    norm_into(second_ref, g_mlp, mlp_ref)


def gelu(value):
    return value * (1.0 + lax.erf(value * 0.7071067811865476)) * 0.5


def hidden_units(mlp_in, fc, pre, total):
    steps = fc.shape[1] // CHUNK

    def before(c):
        rows = pl.ds(pl.multiple_of(c * CHUNK, CHUNK), CHUNK)
        return lax.dot_general(
            mlp_in[...], fc[0, rows, :], (((1,), (1,)), ((), ())), preferred_element_type=F32
        )

    def after(c, active):
        rows = pl.ds(pl.multiple_of(c * CHUNK, CHUNK), CHUNK)
        total[...] = total[...] + jnp.dot(active, fc[1, rows, :], preferred_element_type=F32)

    pre[0] = before(0)

    def step(c, carry):
        now = lax.rem(c, 2)
        active = gelu(pre[now]).astype(BF16)
        pre[1 - now] = before(c + 1)
        after(c, active)
        return carry

    lax.fori_loop(0, steps - 1, step, 0)
    after(steps - 1, gelu(pre[(steps - 1) % 2]).astype(BF16))


def early_kernel(second, mlp_in, fc, total, pre):
    total[...] = second[...]
    hidden_units(mlp_in, fc, pre, total)


def late_kernel(place, early, mlp_in, fc, g_head, w_head, keep_ref, send_ref, pre, total, hidden):
    total[...] = early[...]
    hidden_units(mlp_in, fc, pre, total)
    norm_into(total, g_head, hidden)
    first = place[1] == 0
    for slot in range(SLOTS):
        rows = slice(slot * ROWS, (slot + 1) * ROWS)
        terms = []
        for half in range(2):
            raw = jnp.dot(
                hidden[rows, :], w_head[:, half * 512 : (half + 1) * 512],
                preferred_element_type=F32,
            )
            conf = 1.0 + jnp.exp(raw[:, 384:])
            terms.append([conf * raw[:, c * 128 : (c + 1) * 128] for c in range(3)] + [conf])
        for c in range(4):
            cols = slice(c * 128, (c + 1) * 128)
            low, high = terms[0][c][:TOKI], terms[1][c][:TOKI]
            keep_ref[slot, :, cols] = jnp.where(first, low, high)
            send_ref[slot, :, cols] = jnp.where(first, high, low).astype(BF16)


def window_kernel(windows, image_slot, slot_images, slot_count, place, keep, got, *outs):
    chosen = []
    for slot in range(SLOTS):
        live = slot < slot_count[0]
        for which in range(2):
            index = window_place(image_slot, slot_images, place, slot, which)
            chosen.append(jnp.where(live, index, -1))
    first = place[1] == 0
    for w, out in zip(windows, outs):
        for c in range(4):
            cols = slice(c * 128, (c + 1) * 128)
            acc = jnp.zeros((TOKI, 128), F32)
            for slot in range(SLOTS):
                own = jnp.where(first, chosen[2 * slot], chosen[2 * slot + 1])
                far = jnp.where(first, chosen[2 * slot + 1], chosen[2 * slot])
                acc = acc + jnp.where(own == w, keep[slot, :, cols], 0.0)
                acc = acc + jnp.where(far == w, got[slot, :, cols].astype(F32), 0.0)
            out[:, cols] = acc.astype(out.dtype)


def merge_kernel(base, nearest, further, out):
    def total(cols):
        return base[:, cols] + nearest[:, cols].astype(F32) + further[:, cols].astype(F32)

    weight = jnp.maximum(total(slice(384, 512)), 1.0)
    for c in range(3):
        cols = slice(c * 128, (c + 1) * 128)
        out[0, :, cols] = (total(cols) / weight).astype(BF16)


def pack_kernel(
    features, w_in, w_out, packed, shard, features_here, w_in_here, w_out_here, sems
):
    copies = [
        pltpu.make_async_copy(src, dst, sems.at[i])
        for i, (src, dst) in enumerate(
            ((features, features_here), (w_in, w_in_here), (w_out, w_out_here))
        )
    ]
    for copy in copies:
        copy.start()
    for copy in copies:
        copy.wait()
    count = TOKI - TOP
    packed[88:TOP, HALF:] = jnp.zeros((TOP - 88, HALF), BF16)
    packed[:TOP, :HALF] = features_here[0, :TOP]
    packed[:count, HALF:] = features_here[0, TOP:]
    for target, base in ((packed, TOP), (shard, 0)):
        target[base : base + 24] = w_in_here[0]
        target[base + 24 : base + 48] = w_out_here[0]


SMEM = pl.BlockSpec(memory_space=pltpu.SMEM)
VMEM = pl.BlockSpec(memory_space=pltpu.VMEM)


def call(kernel, scalars, arrays, outs, scratch, flops, name):
    return pl.pallas_call(
        kernel,
        in_specs=[SMEM] * len(scalars) + [VMEM] * len(arrays),
        out_specs=[VMEM] * len(outs),
        out_shape=[jax.ShapeDtypeStruct(s, d) for s, d in outs],
        scratch_shapes=[pltpu.VMEM(s, d) for s, d in scratch],
        compiler_params=pltpu.CompilerParams(vmem_limit_bytes=20 << 20),
        cost_estimate=pl.CostEstimate(flops=flops, transcendentals=0, bytes_accessed=8 << 20),
        name=name,
    )(*scalars, *arrays)


def triple_call(scalars, mine, theirs, g_self, w_qkv):
    return call(
        triple_kernel, scalars, [mine, theirs, g_self, w_qkv],
        [((ALL, D), F32), ((ALL, 3 * D), BF16)], [((ALL, D), BF16)],
        4 * 10**9, "triple_part",
    )


def memory_call(scalars, mine, theirs, g_memory, w_memory):
    return call(
        memory_kernel, scalars, [mine, theirs, g_memory, w_memory],
        [((ALL, 2 * D), BF16)], [((ALL, D), F32), ((ALL, D), BF16)],
        3 * 10**9, "memory_part",
    )[0]


def self_call(rows, triple, g_query, w_out, w_query):
    return call(
        self_kernel, [], [rows, triple, g_query, w_out, w_query],
        [((ALL, D), F32), ((ALL, D), BF16)], [((ALL, D), BF16), ((ALL, D), BF16)],
        12 * 10**9, "self_part",
    )


def cross_call(first, query, key_value, g_mlp, w_out):
    return call(
        cross_kernel, [], [first, query, key_value, g_mlp, w_out],
        [((ALL, D), F32), ((ALL, D), BF16)], [((ALL, D), BF16)],
        12 * 10**9, "cross_part",
    )


def early_call(second, mlp_in, fc):
    return call(
        early_kernel, [], [second, mlp_in, fc],
        [((ALL, D), F32)], [((2, ALL, CHUNK), F32)], 10 * 10**9, "early_part",
    )[0]


def late_call(place, early, mlp_in, fc, g_head, w_head):
    return call(
        late_kernel, [place], [early, mlp_in, fc, g_head, w_head],
        [((SLOTS, TOKI, 512), F32), ((SLOTS, TOKI, 512), BF16)],
        [((2, ALL, CHUNK), F32), ((ALL, D), F32), ((ALL, D), BF16)],
        5 * 10**9, "late_part",
    )


def window_call(windows, scalars, keep, got):
    return call(
        functools.partial(window_kernel, windows), scalars, [keep, got],
        [((TOKI, 512), BF16 if w else F32) for w in windows], [], 10**8,
        "furthest_part" if windows == (3,) else "window_part",
    )


def pack_call(features, w_in, w_out):
    outs = [((TOP + 48, D), BF16), ((48, D), BF16)]
    return pl.pallas_call(
        pack_kernel,
        in_specs=[pl.BlockSpec(memory_space=pltpu.MemorySpace.HBM)] * 3,
        out_specs=[VMEM] * 2,
        out_shape=[jax.ShapeDtypeStruct(s, d) for s, d in outs],
        scratch_shapes=[
            pltpu.VMEM((1, TOKI, HALF), BF16),
            pltpu.VMEM((1, 24, D), BF16),
            pltpu.VMEM((1, 24, D), BF16),
            pltpu.SemaphoreType.DMA((3,)),
        ],
        name="pack_part",
    )(features, w_in, w_out)


def merge_call(*arrays):
    return call(merge_kernel, [], arrays, [((1, TOKI, HALF), BF16)], [], 10**8, "merge_part")[0]


def along(array, axis, by):
    count = lax.axis_size("pairs")
    stride, size = {"y": (32, 4), "x": (8, 4), "z": (1, 8)}[axis]

    def target(p):
        here = p // stride % size
        return p + ((here + by) % size - here) * stride

    return lax.ppermute(array, "pairs", [(p, target(p)) for p in range(count)])


def tied(*arrays):
    return lax.optimization_barrier(arrays)


def hidden_rows(shards):
    inner = [s[-48:-24] for s in shards]
    outer = [s[-24:] for s in shards]
    return jnp.stack([jnp.concatenate(inner, axis=0), jnp.concatenate(outer, axis=0)])


def three_hops(block, axis):
    return [along(block, axis, by) for by in (1, -1, 2)]


def first_hop(block, axis):
    return along(block, axis, 1), along(block, axis, -1)


def second_hop(left, right, axis):
    half = left.shape[1] // 2
    return along(left[:, :half], axis, 1), along(right[:, half:], axis, -1)


def on_device(
    features,
    image_slot,
    slot_images,
    slot_count,
    gain_self,
    gain_query,
    gain_memory,
    gain_mlp,
    gain_head,
    w_qkv,
    w_self_out,
    w_query,
    w_memory,
    w_cross_out,
    w_fc1,
    w_fc2,
    w_head,
):
    place = jnp.stack([lax.axis_index("pairs"), lax.axis_index("side")]).astype(jnp.int32)
    packed, shard = pack_call(features, w_fc1, w_fc2)
    next2 = shifted(packed, -2)
    last1, later = tied(shifted(shard, 1), packed)
    last2 = shifted(shard, 2)
    next1 = shifted(later, -1)
    last34 = shifted(jnp.concatenate([last1, last2], axis=0), 2)
    next3, last34, next1 = tied(shifted(next2, -1), last34, next1)
    part_x = hidden_rows([shard, last1, last2, next2])
    part_y = hidden_rows([next1, next3, last34[:48], last34[48:]])
    mine = jnp.stack([packed[:TOP], next1[:TOP], next2[:TOP], next3[:TOP]])
    theirs = other_core(mine)
    scalars = [image_slot, slot_images.T.reshape(-1), place]
    near_x, near_y = three_hops(part_x, "x"), three_hops(part_y, "y")
    rows, triple = triple_call(scalars, mine, theirs, gain_self, w_qkv[0])
    key_value = memory_call(scalars, mine, theirs, gain_memory, w_memory[0])
    near_x, near_y, rows, triple, key_value = tied(near_x, near_y, rows, triple, key_value)
    plane_x = jnp.concatenate([part_x, *near_x], axis=1)
    plane_y = jnp.concatenate([part_y, *near_y], axis=1)
    near_x, near_y = first_hop(plane_x, "y"), first_hop(plane_y, "x")
    first, query = self_call(rows, triple, gain_query, w_self_out[0], w_query[0])
    second, mlp_in = cross_call(first, query, key_value, gain_mlp, w_cross_out[0])
    near_y, second, mlp_in = tied(near_y, second, mlp_in)
    far_y = second_hop(*near_y, "x")
    near_x, second, mlp_in = tied(near_x, second, mlp_in)
    far_x = second_hop(*near_x, "y")
    fc_early = jnp.concatenate([plane_x, *near_x, plane_y, *near_y], axis=1)
    early = early_call(second, mlp_in, fc_early)
    fc_late = jnp.concatenate([*far_x, *far_y], axis=1)
    keep, send = late_call(place, early, mlp_in, fc_late, gain_head, w_head[0])
    got = other_core(send)
    scalars = [image_slot, slot_images.T.reshape(-1), slot_count, place]
    (furthest,) = window_call((3,), scalars, keep, got)
    third = shifted(furthest, 1)
    base, piece1, piece2 = window_call((0, 1, 2), scalars, keep, got)
    third, piece1 = tied(third, piece1)
    further = shifted((piece2.astype(F32) + third.astype(F32)).astype(BF16), 2)
    nearest = shifted(piece1, 1)
    return merge_call(base, nearest, further)


def solution(mesh):
    placed = (
        P("pairs", None, "side"),
        P(),
        P("pairs", None),
        P("pairs"),
        P("side", None),
        P("side", None),
        P("side", None),
        P("side", None),
        P("side", None),
        P("side", None, None),
        P("side", None, None),
        P("side", None, None),
        P("side", None, None),
        P("side", None, None),
        P("side", "pairs", None),
        P("side", "pairs", None),
        P("side", None, None),
    )
    return jax.shard_map(
        on_device, mesh=mesh, in_specs=placed, out_specs=P("pairs", None, "side"), check_vma=False
    )
```

```python
import functools

import jax
import jax.numpy as jnp
from jax import lax
from jax.experimental import pallas as pl
from jax.experimental.pallas import tpu as pltpu
from jax.sharding import PartitionSpec as P

D = 768
HEAD_DIM = 64
TOKI = 196
ROWS = 208
HALF = 384
TOP = 104
WINDOW = 4
SLOTS = 3
ALL = SLOTS * ROWS
CHUNK = 256
F32 = jnp.float32
BF16 = jnp.bfloat16


def shifted(array, by):
    count = lax.axis_size("pairs")
    return lax.ppermute(array, "pairs", [(i, (i + by) % count) for i in range(count)])


def other_core(array):
    return lax.ppermute(array, "side", [(0, 1), (1, 0)])


def layer_norm(values, gain):
    center = values - jnp.mean(values, axis=-1, keepdims=True)
    spread = jnp.mean(center * center, axis=-1, keepdims=True)
    return center * lax.rsqrt(spread + 1e-06) * gain


def window_place(image_slot, slot_images, place, slot, which):
    stored = image_slot[slot_images[SLOTS * which + slot]]
    return lax.rem(stored - place[0] + 128, 128)


def padded_rows(image_slot, slot_images, place, mine, theirs, swap, target):
    which = place[1] if not swap else 1 - place[1]
    first = place[1] == 0
    for slot in range(SLOTS):
        index = window_place(image_slot, slot_images, place, slot, which)
        own, far = mine[index].astype(F32), theirs[index].astype(F32)
        base = slot * ROWS
        target[base + 192 : base + ROWS, :] = jnp.zeros((ROWS - 192, D), F32)
        for part, count in ((0, TOP), (1, TOKI - TOP)):
            rows = slice(base + part * TOP, base + part * TOP + count)
            cols = slice(part * HALF, (part + 1) * HALF)
            target[rows, :HALF] = jnp.where(first, own[:count, cols], far[:count, cols])
            target[rows, HALF:] = jnp.where(first, far[:count, cols], own[:count, cols])


def norm_into(source, gain, target):
    for slot in range(SLOTS):
        rows = slice(slot * ROWS, (slot + 1) * ROWS)
        target[rows, :] = layer_norm(source[rows, :], gain[...]).astype(BF16)


def attention(q_ref, q_base, k_ref, k_base, v_ref, v_base, out_ref):
    lane = lax.broadcasted_iota(jnp.int32, (ROWS, 128), 1)
    low_lanes = lane < HEAD_DIM
    key_ok = lax.broadcasted_iota(jnp.int32, (ROWS, ROWS), 1) < TOKI

    def step(t, carry):
        slot = t // 3
        group = t - 3 * slot
        rows = pl.ds(pl.multiple_of(slot * ROWS, ROWS), ROWS)
        for pair in range(2):
            col = group * 256 + pair * 128
            q = q_ref[rows, pl.ds(pl.multiple_of(q_base + col, 128), 128)]
            k = k_ref[rows, pl.ds(pl.multiple_of(k_base + col, 128), 128)]
            v = v_ref[rows, pl.ds(pl.multiple_of(v_base + col, 128), 128)]
            outs = []
            for head in range(2):
                own = low_lanes if head == 0 else jnp.logical_not(low_lanes)
                scores = lax.dot_general(
                    jnp.where(own, q, jnp.zeros_like(q)),
                    k,
                    (((1,), (1,)), ((), ())),
                    preferred_element_type=F32,
                )
                expon = jnp.where(key_ok, jnp.exp(scores), 0.0)
                total = jnp.sum(expon, axis=-1, keepdims=True)
                weights = (expon * (1.0 / total)).astype(BF16)
                outs.append(jnp.dot(weights, v, preferred_element_type=F32))
            out_ref[rows, pl.ds(pl.multiple_of(col, 128), 128)] = jnp.where(
                low_lanes, outs[0], outs[1]
            ).astype(BF16)
        return carry

    lax.fori_loop(0, 3 * SLOTS, step, 0)


def project(source, weight, width, write):
    def step(n, carry):
        cols = pl.ds(pl.multiple_of(n * 256, 256), 256)
        write(n, cols, jnp.dot(source[...], weight[:, cols], preferred_element_type=F32))
        return carry

    lax.fori_loop(0, width // 256, step, 0)


def triple_kernel(
    image_slot, slot_images, place, mine, theirs, g_self, w_qkv, rows_ref, triple_ref, hidden
):
    padded_rows(image_slot, slot_images, place, mine, theirs, False, rows_ref)
    norm_into(rows_ref, g_self, hidden)

    def write_triple(n, cols, value):
        triple_ref[:, cols] = (value * jnp.where(n < 3, 0.125, 1.0)).astype(BF16)

    project(hidden, w_qkv, 3 * D, write_triple)


def memory_kernel(
    image_slot, slot_images, place, mine, theirs, g_memory, w_memory, kv_ref, rows, hidden
):
    padded_rows(image_slot, slot_images, place, mine, theirs, True, rows)
    norm_into(rows, g_memory, hidden)

    def write_kv(n, cols, value):
        kv_ref[:, cols] = value.astype(BF16)

    project(hidden, w_memory, 2 * D, write_kv)


def self_kernel(rows, triple, g_query, w_out, w_query, first_ref, query_ref, hidden, mixed):
    attention(triple, 0, triple, D, triple, 2 * D, mixed)

    def add_first(n, cols, value):
        first_ref[:, cols] = rows[:, cols] + value

    project(mixed, w_out, D, add_first)
    norm_into(first_ref, g_query, hidden)

    def write_query(n, cols, value):
        query_ref[:, cols] = (value * 0.125).astype(BF16)

    project(hidden, w_query, D, write_query)


def cross_kernel(first, query, key_value, g_mlp, w_out, second_ref, mlp_ref, mixed):
    attention(query, 0, key_value, 0, key_value, D, mixed)

    def add_second(n, cols, value):
        second_ref[:, cols] = first[:, cols] + value

    project(mixed, w_out, D, add_second)
    norm_into(second_ref, g_mlp, mlp_ref)


def gelu(value):
    return value * (1.0 + lax.erf(value * 0.7071067811865476)) * 0.5


def hidden_units(mlp_in, fc, pre, total):
    steps = fc.shape[1] // CHUNK

    def before(c):
        rows = pl.ds(pl.multiple_of(c * CHUNK, CHUNK), CHUNK)
        return lax.dot_general(
            mlp_in[...], fc[0, rows, :], (((1,), (1,)), ((), ())), preferred_element_type=F32
        )

    def after(c, active):
        rows = pl.ds(pl.multiple_of(c * CHUNK, CHUNK), CHUNK)
        total[...] = total[...] + jnp.dot(active, fc[1, rows, :], preferred_element_type=F32)

    pre[0] = before(0)

    def step(c, carry):
        now = lax.rem(c, 2)
        active = gelu(pre[now]).astype(BF16)
        pre[1 - now] = before(c + 1)
        after(c, active)
        return carry

    lax.fori_loop(0, steps - 1, step, 0)
    after(steps - 1, gelu(pre[(steps - 1) % 2]).astype(BF16))


def early_kernel(second, mlp_in, fc, total, pre):
    total[...] = second[...]
    hidden_units(mlp_in, fc, pre, total)


def late_kernel(place, early, mlp_in, fc, g_head, w_head, keep_ref, send_ref, pre, total, hidden):
    total[...] = early[...]
    hidden_units(mlp_in, fc, pre, total)
    norm_into(total, g_head, hidden)
    first = place[1] == 0
    for slot in range(SLOTS):
        rows = slice(slot * ROWS, (slot + 1) * ROWS)
        terms = []
        for half in range(2):
            raw = jnp.dot(
                hidden[rows, :], w_head[:, half * 512 : (half + 1) * 512],
                preferred_element_type=F32,
            )
            conf = 1.0 + jnp.exp(raw[:, 384:])
            terms.append([conf * raw[:, c * 128 : (c + 1) * 128] for c in range(3)] + [conf])
        for c in range(4):
            cols = slice(c * 128, (c + 1) * 128)
            low, high = terms[0][c][:TOKI], terms[1][c][:TOKI]
            keep_ref[slot, :, cols] = jnp.where(first, low, high)
            send_ref[slot, :, cols] = jnp.where(first, high, low).astype(BF16)


def window_kernel(windows, image_slot, slot_images, slot_count, place, keep, got, *outs):
    chosen = []
    for slot in range(SLOTS):
        live = slot < slot_count[0]
        for which in range(2):
            index = window_place(image_slot, slot_images, place, slot, which)
            chosen.append(jnp.where(live, index, -1))
    first = place[1] == 0
    for w, out in zip(windows, outs):
        for c in range(4):
            cols = slice(c * 128, (c + 1) * 128)
            acc = jnp.zeros((TOKI, 128), F32)
            for slot in range(SLOTS):
                own = jnp.where(first, chosen[2 * slot], chosen[2 * slot + 1])
                far = jnp.where(first, chosen[2 * slot + 1], chosen[2 * slot])
                acc = acc + jnp.where(own == w, keep[slot, :, cols], 0.0)
                acc = acc + jnp.where(far == w, got[slot, :, cols].astype(F32), 0.0)
            out[:, cols] = acc.astype(out.dtype)


def merge_kernel(base, nearest, further, out):
    def total(cols):
        return base[:, cols] + nearest[:, cols].astype(F32) + further[:, cols].astype(F32)

    weight = jnp.maximum(total(slice(384, 512)), 1.0)
    for c in range(3):
        cols = slice(c * 128, (c + 1) * 128)
        out[0, :, cols] = (total(cols) / weight).astype(BF16)


def pack_kernel(
    features, w_in, w_out, packed, shard, features_here, w_in_here, w_out_here, sems
):
    copies = [
        pltpu.make_async_copy(src, dst, sems.at[i])
        for i, (src, dst) in enumerate(
            ((features, features_here), (w_in, w_in_here), (w_out, w_out_here))
        )
    ]
    for copy in copies:
        copy.start()
    for copy in copies:
        copy.wait()
    count = TOKI - TOP
    packed[88:TOP, HALF:] = jnp.zeros((TOP - 88, HALF), BF16)
    packed[:TOP, :HALF] = features_here[0, :TOP]
    packed[:count, HALF:] = features_here[0, TOP:]
    for target, base in ((packed, TOP), (shard, 0)):
        target[base : base + 24] = w_in_here[0]
        target[base + 24 : base + 48] = w_out_here[0]


SMEM = pl.BlockSpec(memory_space=pltpu.SMEM)
VMEM = pl.BlockSpec(memory_space=pltpu.VMEM)


def call(kernel, scalars, arrays, outs, scratch, flops, name):
    return pl.pallas_call(
        kernel,
        in_specs=[SMEM] * len(scalars) + [VMEM] * len(arrays),
        out_specs=[VMEM] * len(outs),
        out_shape=[jax.ShapeDtypeStruct(s, d) for s, d in outs],
        scratch_shapes=[pltpu.VMEM(s, d) for s, d in scratch],
        compiler_params=pltpu.CompilerParams(vmem_limit_bytes=20 << 20),
        cost_estimate=pl.CostEstimate(flops=flops, transcendentals=0, bytes_accessed=8 << 20),
        name=name,
    )(*scalars, *arrays)


def triple_call(scalars, mine, theirs, g_self, w_qkv):
    return call(
        triple_kernel, scalars, [mine, theirs, g_self, w_qkv],
        [((ALL, D), F32), ((ALL, 3 * D), BF16)], [((ALL, D), BF16)],
        4 * 10**9, "triple_part",
    )


def memory_call(scalars, mine, theirs, g_memory, w_memory):
    return call(
        memory_kernel, scalars, [mine, theirs, g_memory, w_memory],
        [((ALL, 2 * D), BF16)], [((ALL, D), F32), ((ALL, D), BF16)],
        3 * 10**9, "memory_part",
    )[0]


def self_call(rows, triple, g_query, w_out, w_query):
    return call(
        self_kernel, [], [rows, triple, g_query, w_out, w_query],
        [((ALL, D), F32), ((ALL, D), BF16)], [((ALL, D), BF16), ((ALL, D), BF16)],
        12 * 10**9, "self_part",
    )


def cross_call(first, query, key_value, g_mlp, w_out):
    return call(
        cross_kernel, [], [first, query, key_value, g_mlp, w_out],
        [((ALL, D), F32), ((ALL, D), BF16)], [((ALL, D), BF16)],
        12 * 10**9, "cross_part",
    )


def early_call(second, mlp_in, fc):
    return call(
        early_kernel, [], [second, mlp_in, fc],
        [((ALL, D), F32)], [((2, ALL, CHUNK), F32)], 10 * 10**9, "early_part",
    )[0]


def late_call(place, early, mlp_in, fc, g_head, w_head):
    return call(
        late_kernel, [place], [early, mlp_in, fc, g_head, w_head],
        [((SLOTS, TOKI, 512), F32), ((SLOTS, TOKI, 512), BF16)],
        [((2, ALL, CHUNK), F32), ((ALL, D), F32), ((ALL, D), BF16)],
        5 * 10**9, "late_part",
    )


def window_call(windows, scalars, keep, got):
    return call(
        functools.partial(window_kernel, windows), scalars, [keep, got],
        [((TOKI, 512), BF16 if w else F32) for w in windows], [], 10**8,
        "furthest_part" if windows == (3,) else "window_part",
    )


def pack_call(features, w_in, w_out):
    outs = [((TOP + 48, D), BF16), ((48, D), BF16)]
    return pl.pallas_call(
        pack_kernel,
        in_specs=[pl.BlockSpec(memory_space=pltpu.MemorySpace.HBM)] * 3,
        out_specs=[VMEM] * 2,
        out_shape=[jax.ShapeDtypeStruct(s, d) for s, d in outs],
        scratch_shapes=[
            pltpu.VMEM((1, TOKI, HALF), BF16),
            pltpu.VMEM((1, 24, D), BF16),
            pltpu.VMEM((1, 24, D), BF16),
            pltpu.SemaphoreType.DMA((3,)),
        ],
        name="pack_part",
    )(features, w_in, w_out)


def merge_call(*arrays):
    return call(merge_kernel, [], arrays, [((1, TOKI, HALF), BF16)], [], 10**8, "merge_part")[0]


def along(array, axis, by):
    count = lax.axis_size("pairs")
    stride, size = {"y": (32, 4), "x": (8, 4), "z": (1, 8)}[axis]

    def target(p):
        here = p // stride % size
        return p + ((here + by) % size - here) * stride

    return lax.ppermute(array, "pairs", [(p, target(p)) for p in range(count)])


def tied(*arrays):
    return lax.optimization_barrier(arrays)


def hidden_rows(shards):
    inner = [s[-48:-24] for s in shards]
    outer = [s[-24:] for s in shards]
    return jnp.stack([jnp.concatenate(inner, axis=0), jnp.concatenate(outer, axis=0)])


def three_hops(block, axis):
    return [along(block, axis, by) for by in (1, -1, 2)]


def first_hop(block, axis):
    return along(block, axis, 1), along(block, axis, -1)


def second_hop(left, right, axis):
    half = left.shape[1] // 2
    return along(left[:, :half], axis, 1), along(right[:, half:], axis, -1)


def on_device(
    features,
    image_slot,
    slot_images,
    slot_count,
    gain_self,
    gain_query,
    gain_memory,
    gain_mlp,
    gain_head,
    w_qkv,
    w_self_out,
    w_query,
    w_memory,
    w_cross_out,
    w_fc1,
    w_fc2,
    w_head,
):
    place = jnp.stack([lax.axis_index("pairs"), lax.axis_index("side")]).astype(jnp.int32)
    packed, shard = pack_call(features, w_fc1, w_fc2)
    next2 = shifted(packed, -2)
    last1, later = tied(shifted(shard, 1), packed)
    last2 = shifted(shard, 2)
    next1 = shifted(later, -1)
    last34 = shifted(jnp.concatenate([last1, last2], axis=0), 2)
    next3, last34, next1 = tied(shifted(next2, -1), last34, next1)
    part_x = hidden_rows([shard, last1, last2, next2])
    part_y = hidden_rows([next1, next3, last34[:48], last34[48:]])
    mine = jnp.stack([packed[:TOP], next1[:TOP], next2[:TOP], next3[:TOP]])
    theirs = other_core(mine)
    scalars = [image_slot, slot_images.T.reshape(-1), place]
    near_x, near_y = three_hops(part_x, "x"), three_hops(part_y, "y")
    rows, triple = triple_call(scalars, mine, theirs, gain_self, w_qkv[0])
    key_value = memory_call(scalars, mine, theirs, gain_memory, w_memory[0])
    near_x, near_y, rows, triple, key_value = tied(near_x, near_y, rows, triple, key_value)
    plane_x = jnp.concatenate([part_x, *near_x], axis=1)
    plane_y = jnp.concatenate([part_y, *near_y], axis=1)
    near_x, near_y = first_hop(plane_x, "y"), first_hop(plane_y, "x")
    first, query = self_call(rows, triple, gain_query, w_self_out[0], w_query[0])
    second, mlp_in = cross_call(first, query, key_value, gain_mlp, w_cross_out[0])
    near_y, second, mlp_in = tied(near_y, second, mlp_in)
    far_y = second_hop(*near_y, "x")
    near_x, second, mlp_in = tied(near_x, second, mlp_in)
    far_x = second_hop(*near_x, "y")
    fc_early = jnp.concatenate([plane_x, *near_x, plane_y, *near_y], axis=1)
    early = early_call(second, mlp_in, fc_early)
    fc_late = jnp.concatenate([*far_x, *far_y], axis=1)
    keep, send = late_call(place, early, mlp_in, fc_late, gain_head, w_head[0])
    got = other_core(send)
    scalars = [image_slot, slot_images.T.reshape(-1), slot_count, place]
    (furthest,) = window_call((3,), scalars, keep, got)
    third = shifted(furthest, 1)
    base, piece1, piece2 = window_call((0, 1, 2), scalars, keep, got)
    nearest = shifted(piece1, 1)
    further = shifted((piece2.astype(F32) + third.astype(F32)).astype(BF16), 2)
    return merge_call(base, nearest, further)


def solution(mesh):
    placed = (
        P("pairs", None, "side"),
        P(),
        P("pairs", None),
        P("pairs"),
        P("side", None),
        P("side", None),
        P("side", None),
        P("side", None),
        P("side", None),
        P("side", None, None),
        P("side", None, None),
        P("side", None, None),
        P("side", None, None),
        P("side", None, None),
        P("side", "pairs", None),
        P("side", "pairs", None),
        P("side", None, None),
    )
    return jax.shard_map(
        on_device, mesh=mesh, in_specs=placed, out_specs=P("pairs", None, "side"), check_vma=False
    )
```
